256 devices in a mesh: dp: 8 (over y, core), seq: 32 (over z, x).
Axes of the slice: x: 4, y: 4, z: 8, core: 2. Of those that a mesh axis runs over, the one named last changes fastest.
Arguments:
- features: bfloat16 [8, 24576, 512], P('dp', 'seq'), may hold values from -12 to 12, as said below
- slot_kind: int32 [8, 96], P('dp', 'seq'), may hold values from 0 to 2, as said below
- block_gain: float32 [512], replicated, may hold values from 0.1 to 1.9
- block_shift: float32 [512], replicated, may hold values from -2 to 2
- block_weight: bfloat16 [4608, 512], replicated, may hold values from -0.09375 to 0.09375
- block_bias: float32 [512], replicated, may hold values from -2 to 2
- final_gain: float32 [512], replicated, may hold values from 0.1 to 1.9
- final_shift: float32 [512], replicated, may hold values from -2 to 2
- latent_weight: bfloat16 [512, 144], replicated, may hold values from -0.09375 to 0.09375
- latent_bias: float32 [16], replicated, may hold values from -2 to 2
- embed_weight: bfloat16 [64, 1152], P(None, 'dp'), may hold values from -0.75 to 0.75
- embed_bias: bfloat16 [1152], P('dp'), may hold values from -2 to 2
Outputs:
- sequence: bfloat16 [8, 4096, 1152], P('dp', 'seq')
The draws below stay inside these ranges and needn't reach their ends.
Inputs may be any that keep to these rules, and one draw needn't show every extreme that they name: `slot_kind`: the live slots of a device (kind 1 or 2) come before its empty ones. In every dp group, the live slots of the devices with seq index below d number between 2 d and 2 d + 2, and 2 * 32 over the whole group; in every group some device has 3 live slots. `features`: finite values.
All inputs are finite; a program needn't handle non-finite values.
Results may differ from the reference program's by a relative error of at most 0.014.
Values may be sent and summed in bfloat16 or wider, within the bound.
A program may use at most 64 MiB of HBM per device.

```python
import jax
import jax.numpy as jnp
from jax import lax

C = 512
GROUPS = 32
LAT = 16
HID = 1152
SLOT_ROWS = 32
SLOT_COLS = 8
SLOTS = 3
CELLS = 256
TOK_SLOT = 64
TOK_SEQ = 128
FEAT = 64
N_DP = 8
N_SEQ = 32


def draw_features(key, part):
    first_key, second_key, third_key = jax.random.split(key, 3)
    base_values = jax.random.normal(first_key, (N_DP, N_SEQ * SLOTS * CELLS, C), jnp.float32)
    channel_scale = jnp.exp(jax.random.uniform(second_key, (C,), jnp.float32, -1.15, 1.15))
    cell_scale = jnp.exp(jax.random.uniform(third_key, (N_DP, N_SEQ * SLOTS * CELLS, 1), jnp.float32, -0.7, 0.7))
    values = base_values * channel_scale * cell_scale
    return jnp.clip(values, -12.0, 12.0).astype(jnp.bfloat16)


def draw_slot_kind(key, part):
    first_key, second_key, third_key = jax.random.split(key, 3)
    raw_excess = jax.random.randint(first_key, (N_DP, N_SEQ), 0, 3).astype(jnp.int32)
    busiest = jax.random.randint(second_key, (N_DP, 1), 0, N_SEQ - 1).astype(jnp.int32)
    seat = jnp.arange(N_SEQ, dtype=jnp.int32)[None, :]
    raw_excess = jnp.where(seat == busiest, 1, raw_excess)
    raw_excess = jnp.where(seat == busiest - 1, 0, raw_excess)
    raw_excess = jnp.where(seat == N_SEQ - 1, 0, raw_excess)
    lowest = lax.cummin(raw_excess - seat, axis=1)
    excess = jnp.minimum(lowest + seat, seat + 1).astype(jnp.int32)
    before = jnp.concatenate([jnp.zeros((N_DP, 1), jnp.int32), excess[:, :-1]], axis=1)
    counts = 2 + excess - before
    buckets = jax.random.randint(third_key, (N_DP, N_SEQ, SLOTS), 1, 3).astype(jnp.int32)
    live_slots = jnp.arange(SLOTS, dtype=jnp.int32)[None, None, :] < counts[:, :, None]
    return jnp.where(live_slots, buckets, 0).reshape(N_DP, N_SEQ * SLOTS).astype(jnp.int32)


def shard_levels(key, shape, shards, smallest, largest):
    factor_of, own = 1.0, jax.random.fold_in(key, 6)
    for axis_at, parts in shards:
        heights = jnp.exp(jax.random.uniform(jax.random.fold_in(own, axis_at), (parts,), jnp.float32, smallest / len(shards), largest / len(shards)))
        factor_of = factor_of * jnp.repeat(heights, shape[axis_at] // parts).reshape([-1 if axis == axis_at else 1 for axis in range(len(shape))])
    return factor_of


def noise(rng, extent, scale, limit, cuts=(), kind=jnp.bfloat16):
    result = scale * jax.random.normal(rng, extent, jnp.float32)
    if cuts:
        result = result * shard_levels(rng, extent, cuts, -0.22, 0.18)
    return jnp.clip(result, -limit, limit).astype(kind)


def setup_inputs(seed: int = 0) -> dict:
    keys = jax.random.split(jax.random.key(seed), 13)
    features = draw_features(jax.random.fold_in(keys[12], 71), 0)
    slot_kind = draw_slot_kind(jax.random.fold_in(keys[12], 71), 0)
    block_gain = jnp.clip(1.0 + 0.18 * jax.random.normal(keys[2], (C,), jnp.float32), 0.1, 1.9)
    block_shift = noise(keys[3], (C,), 0.3, 2.0, (), jnp.float32)
    block_weight = noise(keys[4], (9 * C, C), (9 * C) ** -0.5, 0.09375)
    block_bias = noise(keys[5], (C,), 0.3, 2.0, (), jnp.float32)
    final_gain = jnp.clip(1.0 + 0.18 * jax.random.normal(keys[6], (C,), jnp.float32), 0.1, 1.9)
    final_shift = noise(keys[7], (C,), 0.3, 2.0, (), jnp.float32)
    latent_weight = noise(keys[8], (C, 9 * LAT), (9 * C) ** -0.5, 0.09375)
    latent_bias = noise(keys[9], (LAT,), 0.3, 2.0, (), jnp.float32)
    embed_weight = noise(keys[10], (FEAT, HID), FEAT ** -0.5, 0.75, ((1, 8),))
    embed_bias = noise(keys[11], (HID,), 0.3, 2.0, ((0, 8),))
    return dict(features=features, slot_kind=slot_kind, block_gain=block_gain, block_shift=block_shift, block_weight=block_weight, block_bias=block_bias, final_gain=final_gain, final_shift=final_shift, latent_weight=latent_weight, latent_bias=latent_bias, embed_weight=embed_weight, embed_bias=embed_bias)


LATENT_SHIFT = 0.0609
LATENT_SCALE = 1.5305
NORM_EPSILON = 1e-06
OFFSETS = [(-1, -1), (-1, 0), (-1, 1), (0, -1), (0, 0), (0, 1), (1, -1), (1, 0), (1, 1)]

def group_norm(values, slot_types, norm_gain, norm_shift):
    slot_count, height, across, channels = values.shape
    grouped = values.reshape(slot_count, 2, height // 2, across, GROUPS, channels // GROUPS)
    joined = (slot_types == 2)[:, None, None, None, None, None]
    half_centre = lax.optimization_barrier(jnp.mean(grouped, axis=(2, 3, 5), keepdims=True))
    centre = jnp.where(joined, lax.optimization_barrier(jnp.mean(half_centre, axis=1, keepdims=True)), half_centre)
    centred = grouped - centre
    half_spread = lax.optimization_barrier(jnp.mean(centred * centred, axis=(2, 3, 5), keepdims=True))
    spread = jnp.where(joined, lax.optimization_barrier(jnp.mean(half_spread, axis=1, keepdims=True)), half_spread)
    normed = (centred * lax.rsqrt(spread + NORM_EPSILON)).reshape(values.shape)
    return normed * norm_gain.astype(jnp.float32) + norm_shift.astype(jnp.float32)

def boundary_mask(slot_types, height, row_step, out_type):
    row_index = jnp.arange(height)
    edge_row = height // 2 if row_step < 0 else height // 2 - 1
    crossing = (slot_types == 1)[:, None] & (row_index == edge_row)[None, :]
    return jnp.where(crossing, 0.0, 1.0).astype(out_type)[:, :, None, None]

def neighbour(padded, slot_types, row_step, col_step):
    height = padded.shape[1] - 2
    across = padded.shape[2] - 2
    window = padded[:, 1 + row_step:1 + row_step + height, 1 + col_step:1 + col_step + across, :]
    if row_step != 0:
        window = window * boundary_mask(slot_types, height, row_step, window.dtype)
    return window

def encode(slots, slot_types, block_gain, block_shift, block_weight, block_bias, final_gain, final_shift, latent_weight, latent_bias):
    slot_count, height, across, channels = slots.shape
    lat_width = latent_weight.shape[1] // 9
    first_act = jax.nn.silu(group_norm(slots.astype(jnp.float32), slot_types, block_gain, block_shift)).astype(jnp.bfloat16)
    padded = jnp.pad(first_act, ((0, 0), (1, 1), (1, 1), (0, 0)))
    columns = jnp.concatenate([neighbour(padded, slot_types, row_step, col_step) for row_step, col_step in OFFSETS], axis=-1)
    conv_out = jnp.dot(columns.reshape(-1, 9 * channels), block_weight, preferred_element_type=jnp.float32) + block_bias.astype(jnp.float32)
    inner = (slots.reshape(-1, channels).astype(jnp.float32) + conv_out).astype(jnp.bfloat16).reshape(slots.shape)
    second_act = jax.nn.silu(group_norm(inner.astype(jnp.float32), slot_types, final_gain, final_shift)).astype(jnp.bfloat16)
    tap_terms = jnp.dot(second_act.reshape(-1, channels), latent_weight, preferred_element_type=jnp.float32)
    tap_terms = tap_terms.reshape(slot_count, height, across, 9 * lat_width)
    padded_terms = jnp.pad(tap_terms, ((0, 0), (1, 1), (1, 1), (0, 0)))
    latent = jnp.zeros((slot_count, height, across, lat_width), jnp.float32) + latent_bias.astype(jnp.float32)
    for tap_number, (row_step, col_step) in enumerate(OFFSETS):
        piece_terms = padded_terms[..., tap_number * lat_width:(tap_number + 1) * lat_width]
        latent = latent + neighbour(piece_terms, slot_types, row_step, col_step)
    scaled = (latent - LATENT_SHIFT) * LATENT_SCALE
    patches = scaled.reshape(slot_count, height // 2, 2, across // 2, 2, lat_width).transpose(0, 1, 3, 2, 4, 5)
    return patches.reshape(slot_count * (height // 2) * (across // 2), 4 * lat_width).astype(jnp.bfloat16)

def reference(features, slot_kind, block_gain, block_shift, block_weight, block_bias, final_gain, final_shift, latent_weight, latent_bias, embed_weight, embed_bias):
    block_size = min(8, 2 * N_SEQ)

    def one_group(group_args):
        group_features, group_types = group_args
        live_slots = (group_types.reshape(N_SEQ, SLOTS) > 0).astype(jnp.int32)
        counts = lax.optimization_barrier(jnp.sum(live_slots, axis=1)).astype(jnp.int32)
        starts = (jnp.cumsum(counts) - counts).astype(jnp.int32)
        global_slot = jnp.arange(2 * N_SEQ, dtype=jnp.int32)
        owner = (lax.optimization_barrier(jnp.sum((starts[None, :] <= global_slot[:, None]).astype(jnp.int32), axis=1)) - 1).astype(jnp.int32)
        flat_index = (owner * SLOTS + global_slot - starts[owner]).astype(jnp.int32)
        chosen_types = group_types[flat_index]
        chosen = group_features.reshape(N_SEQ * SLOTS, SLOT_ROWS, SLOT_COLS, C)[flat_index]

        def encode_block(block_args):
            return encode(block_args[0], block_args[1], block_gain, block_shift, block_weight, block_bias, final_gain, final_shift, latent_weight, latent_bias)
        patches = lax.map(encode_block, (chosen.reshape(-1, block_size, SLOT_ROWS, SLOT_COLS, C), chosen_types.reshape(-1, block_size)))
        patches = patches.reshape(2 * N_SEQ * TOK_SLOT, FEAT)
        tokens = (jnp.dot(patches, embed_weight, preferred_element_type=jnp.float32) + embed_bias.astype(jnp.float32)).astype(jnp.bfloat16)
        return tokens.reshape(N_SEQ * TOK_SEQ, HID)
    return lax.map(one_group, (features, slot_kind))
```

```python
import functools
import jax
import jax.numpy as jnp
from jax import lax
from jax.experimental import pallas as pl
from jax.experimental.pallas import tpu as pltpu
from jax.sharding import PartitionSpec as P

F32, BF16, I32 = jnp.float32, jnp.bfloat16, jnp.int32
MESH = pl.DeviceIdType.MESH
LATENT_SHIFT = 0.0609
LATENT_SCALE = 1.5305
EPS = 1e-06
C = 512
TAPS = [(a, b) for a in (-1, 0, 1) for b in (-1, 0, 1)]


def iota(shape, dim):
    return lax.broadcasted_iota(I32, shape, dim)


def lane_tiles(v):
    return [v[:, 128 * i : 128 * i + 128] for i in range(v.shape[1] // 128)]


def group_sums(parts, block):
    rows = jnp.concatenate([t for p in parts for t in lane_tiles(p)], axis=0)
    hi = rows.astype(BF16)
    rest = rows - hi.astype(F32)
    mid = rest.astype(BF16)
    low = (rest - mid.astype(F32)).astype(BF16)
    sums = jnp.dot(jnp.concatenate([hi, mid, low], axis=0), block, preferred_element_type=F32)
    count = rows.shape[0]
    total = sums[:count] + sums[count : 2 * count] + sums[2 * count :]
    out = []
    for i in range(len(parts)):
        tiles = []
        for j in range(4):
            tile = total[32 * i + 8 * j : 32 * i + 8 * j + 8]
            tiles.append(jnp.broadcast_to(jnp.sum(tile, axis=0, keepdims=True), (8, 128)))
        out.append(jnp.concatenate(tiles, axis=1))
    return out


def norm_scales(load, block, joined, gain, shift):
    zero = jnp.zeros((8, C), F32)
    low, high = zero, zero
    for r in range(16):
        x0, x1 = load(r)
        low, high = low + x0, high + x1
    m0, m1 = group_sums([low, high], block)
    m0, m1 = m0 * (1.0 / 2048), m1 * (1.0 / 2048)
    both = (m0 + m1) * 0.5
    c0, c1 = jnp.where(joined, both, m0), jnp.where(joined, both, m1)
    low, high = zero, zero
    for r in range(16):
        x0, x1 = load(r)
        x0, x1 = x0 - c0, x1 - c1
        low, high = low + x0 * x0, high + x1 * x1
    v0, v1 = group_sums([low, high], block)
    v0, v1 = v0 * (1.0 / 2048), v1 * (1.0 / 2048)
    both = (v0 + v1) * 0.5
    v0, v1 = jnp.where(joined, both, v0), jnp.where(joined, both, v1)
    s0 = lax.rsqrt(v0 + EPS) * gain * 0.5
    s1 = lax.rsqrt(v1 + EPS) * gain * 0.5
    return c0, c1, s0, s1, jnp.broadcast_to(shift * 0.5, (8, C))


def silu_half(half):
    return half + half * jnp.tanh(half)


def side_shifts(y):
    col = iota((8, C), 0)
    left = jnp.where(col >= 1, pltpu.roll(y, 1, 0), 0.0)
    right = jnp.where(col <= 6, pltpu.roll(y, 7, 0), 0.0)
    return left, y, right


def pair(top, bottom):
    return jnp.concatenate([top, bottom], axis=0).astype(BF16)


def norm_first(load, block, joined, gain, shift, pad):
    c0, c1, s0, s1, t = norm_scales(load, block, joined, gain, shift)
    zero = jnp.zeros((8, C), F32)
    for r in range(16):
        x0, x1 = load(r)
        y0, y1 = silu_half((x0 - c0) * s0 + t), silu_half((x1 - c1) * s1 + t)
        sides0, sides1 = side_shifts(y0), side_shifts(y1)
        for b in range(3):
            pad[b, 16 * (r + 1) : 16 * (r + 2), :] = pair(sides0[b], sides1[b])
            if r == 0:
                pad[b, 16 * 17 : 16 * 18, :] = pair(jnp.where(joined, sides1[b], 0.0), zero)
            if r == 15:
                pad[b, 0:16, :] = pair(zero, jnp.where(joined, sides0[b], 0.0))


def conv(pad, w_ref):
    lhs = jnp.concatenate(
        [pad[b + 1, 16 * (a + 1) : 16 * (a + 1) + 256, :] for a, b in TAPS], axis=1
    )
    return jnp.dot(lhs, w_ref[...], preferred_element_type=F32)


def norm_second(load, block, joined, gain, shift, act):
    c0, c1, s0, s1, t = norm_scales(load, block, joined, gain, shift)
    for r in range(16):
        x0, x1 = load(r)
        act[16 * r : 16 * r + 16, :] = pair(
            silu_half((x0 - c0) * s0 + t), silu_half((x1 - c1) * s1 + t)
        )


def latent_patches(act, lw3, lat_bias, joined, select):
    terms = jnp.dot(act[...], lw3, preferred_element_type=F32)
    joined = joined[:, :128]
    zero = jnp.zeros((8, 128), F32)

    def part(a, r, h):
        return terms[16 * r + 8 * h : 16 * r + 8 * h + 8, 128 * (a + 1) : 128 * (a + 2)]

    col = iota((8, 128), 0)
    lane = iota((8, 128), 1)
    rows = []
    for p in range(8):
        for h in range(2):
            total = None
            for i in range(2):
                r = 2 * p + i
                above = part(-1, r - 1, h) if r > 0 else (jnp.where(joined, part(-1, 15, 0), 0.0) if h == 1 else zero)
                below = part(1, r + 1, h) if r < 15 else (jnp.where(joined, part(1, 0, 1), 0.0) if h == 0 else zero)
                z = above + part(0, r, h) + below
                left = jnp.where(col >= 1, pltpu.roll(z, 1, 0), 0.0)
                right = jnp.where(col <= 6, pltpu.roll(z, 7, 0), 0.0)
                if i == 0:
                    lat = left + pltpu.roll(z, 96, 1) + pltpu.roll(right, 64, 1)
                else:
                    lat = pltpu.roll(left, 32, 1) + z + pltpu.roll(right, 96, 1)
                lat = (lat + lat_bias - LATENT_SHIFT) * LATENT_SCALE
                own = (lane // 16) == (2 * i + col % 2)
                lat = jnp.where(own, lat, 0.0)
                total = lat if total is None else total + lat
            rows.append(total)
    cells = jnp.concatenate(rows, axis=0).astype(BF16)
    return jnp.dot(select, cells, preferred_element_type=F32).astype(BF16)


def constants(lw, lat_bias):
    block = jnp.where(iota((128, 128), 0) // 16 == iota((128, 128), 1) // 16, 1.0, 0.0).astype(BF16)
    k, n = iota((144, 384), 0), iota((144, 384), 1)
    group = (n % 128) // 16
    source = ((n // 128) * 3 + group // 2) * 16 + n % 16
    place = jnp.where((k == source) & (group < 6), 1.0, 0.0).astype(BF16)
    lw3 = jnp.dot(lw, place, preferred_element_type=F32).astype(BF16)
    t, m = iota((64, 128), 0), iota((64, 128), 1)
    same = (m // 16 == (t // 4) % 8) & ((m // 8) % 2 == t // 32) & ((m % 8) // 2 == t % 4)
    select = jnp.where(same, 1.0, 0.0).astype(BF16)
    return block, lw3, select


N_SEQ = 32
N_DP = 8


def kernel(
    kind, feat_hbm, bg, bs, w_hbm, bb, fg, fs, lw, lb, ew, eb, out,
    feat, slots, w, pad, inner, act, lanes, mine, counts, shard, shards, full, sent, got,
    feat_sem, w_sem, count_send, count_recv, shard_send, shard_recv, patch_send, patch_recv,
):
    seat, row = lax.axis_index("seq"), lax.axis_index("dp")
    ahead = lax.rem(seat + 1, N_SEQ)
    feat_copy = pltpu.make_async_copy(feat_hbm.at[0], feat, feat_sem)
    feat_copy.start()
    w_copy = pltpu.make_async_copy(w_hbm, w, w_sem)
    w_copy.start()

    barrier = pltpu.get_barrier_semaphore()

    def greet_seq(i, carry):
        pl.semaphore_signal(barrier, inc=1, device_id={"seq": lax.rem(seat + i, N_SEQ)}, device_id_type=MESH)
        return carry

    def greet_dp(i, carry):
        pl.semaphore_signal(barrier, inc=1, device_id={"dp": lax.rem(row + i, N_DP)}, device_id_type=MESH)
        return carry

    lax.fori_loop(1, N_SEQ, greet_seq, 0)
    lax.fori_loop(1, N_DP, greet_dp, 0)

    live = [(kind[0, i] > 0).astype(I32) for i in range(3)]
    n = live[0] + live[1] + live[2]
    kinds = [
        jnp.where(n == 3, kind[0, 2], jnp.where(n == 2, kind[0, 1], kind[0, 0])),
        jnp.where(n == 2, kind[0, 0], kind[0, 1]),
        jnp.where(n == 3, kind[0, 0], kind[0, 2]),
    ]
    mine[...] = jnp.full((1, 128), n, I32)
    counts[pl.ds(seat, 1)] = jnp.full((1, 1, 128), n, I32)
    shard[0:64, :] = ew[...]
    shard[64:80, :] = jnp.broadcast_to(eb[...], (16, 144))
    shards[pl.ds(row, 1)] = shard[...].reshape(1, 80, 144)
    lanes[...] = jnp.zeros((8, 128), F32)
    lanes[0:1, 0:16] = lb[...]
    lat_bias = lanes[...]
    for step in (16, 32, 64):
        lat_bias = lat_bias + pltpu.roll(lat_bias, step, 1)
    lat_bias = lat_bias[0:1]
    block, lw3, select = constants(lw[...], lat_bias)

    def count_copy(i):
        return pltpu.make_async_remote_copy(
            src_ref=mine,
            dst_ref=counts.at[seat],
            send_sem=count_send.at[i],
            recv_sem=count_recv.at[i],
            device_id={"seq": lax.rem(seat + i, N_SEQ)},
            device_id_type=MESH,
        )

    def shard_copy(i):
        return pltpu.make_async_remote_copy(
            src_ref=shard,
            dst_ref=shards.at[row],
            send_sem=shard_send.at[i],
            recv_sem=shard_recv.at[i],
            device_id={"dp": lax.rem(row + i, N_DP)},
            device_id_type=MESH,
        )

    def patch_copy(t):
        return pltpu.make_async_remote_copy(
            src_ref=sent.at[t],
            dst_ref=got.at[t],
            send_sem=patch_send.at[t],
            recv_sem=patch_recv.at[t],
            device_id={"seq": ahead},
            device_id_type=MESH,
        )

    number = jnp.full((16, C), n, I32)
    feat_copy.wait()
    for i in range(16):
        first, middle, last = [feat[256 * k + 16 * i : 256 * k + 16 * i + 16, :] for k in range(3)]
        part = slice(16 * i, 16 * i + 16)
        slots[0, part, :] = jnp.where(number == 3, last, jnp.where(number == 2, middle, first))
        slots[1, part, :] = jnp.where(number == 2, first, middle)
        slots[2, part, :] = jnp.where(number == 3, first, last)
    for t in range(3):
        joined = jnp.full((8, C), kinds[t], I32) == 2

        def load(r):
            return slots[t, 8 * r : 8 * r + 8, :].astype(F32), slots[t, 128 + 8 * r : 136 + 8 * r, :].astype(F32)

        norm_first(load, block, joined, bg[...], bs[...], pad)
        if t == 0:
            w_copy.wait()
        res = conv(pad, w)
        bias = jnp.broadcast_to(bb[...], (8, C))
        for r in range(16):
            x0, x1 = load(r)
            top, bottom = res[16 * r : 16 * r + 8], res[16 * r + 8 : 16 * r + 16]
            inner[16 * r : 16 * r + 16, :] = pair(top + x0 + bias, bottom + x1 + bias)

        if t == 0:
            pl.semaphore_wait(barrier, N_SEQ + N_DP - 2)

            def send_count(i, carry):
                count_copy(i).start()
                return carry

            def send_shard(i, carry):
                shard_copy(i).start()
                return carry

            lax.fori_loop(1, N_SEQ, send_count, 0)
            lax.fori_loop(1, N_DP, send_shard, 0)

        def load_inner(r):
            v = inner[16 * r : 16 * r + 16, :].astype(F32)
            return v[:8], v[8:]

        norm_second(load_inner, block, joined, fg[...], fs[...], act)
        sent[t] = latent_patches(act, lw3, lat_bias, joined, select)
        if t < 2:
            patch_copy(t).start()

    def wait_count(i, carry):
        count_copy(i).wait()
        return carry

    def wait_shard(i, carry):
        shard_copy(i).wait()
        return carry

    lax.fori_loop(1, N_SEQ, wait_count, 0)
    lax.fori_loop(1, N_DP, wait_shard, 0)
    for i in range(N_DP):
        full[:, 144 * i : 144 * i + 144] = shards[i]
    before = iota((N_SEQ, 1, 128), 0) < seat
    carry_in = jnp.sum(jnp.where(before, counts[...], 0), axis=0) - 2 * seat
    for t in range(2):
        patch_copy(t).wait()

    def wide(v):
        return jnp.broadcast_to(v, (64, 128))

    carry_in = wide(carry_in)
    number = wide(jnp.full((1, 128), n, I32))
    own = [sent[t].astype(F32) for t in range(3)]
    came = [got[t].astype(F32) for t in range(2)]
    newest = jnp.where(number == 3, own[2], jnp.where(number == 2, own[1], own[0]))
    second = jnp.where(number == 3, own[1], own[0])
    out0 = jnp.where(carry_in == 0, newest, jnp.where(carry_in == 1, came[0], came[1]))
    out1 = jnp.where(carry_in == 0, second, jnp.where(carry_in == 1, newest, came[0]))
    patches = jnp.concatenate([out0, out1], axis=0).astype(BF16)[:, :64]
    tokens = jnp.dot(patches, full[0:64, :], preferred_element_type=F32)
    out[0] = (tokens + full[64:65, :].astype(F32)).astype(BF16)


def local(feat, kind, bg, bs, w, bb, fg, fs, lw, lb, ew, eb):
    in_vmem = pl.BlockSpec(memory_space=pltpu.VMEM)
    in_hbm = pl.BlockSpec(memory_space=pl.ANY)
    in_smem = pl.BlockSpec(memory_space=pltpu.SMEM)
    dma = pltpu.SemaphoreType.DMA
    return pl.pallas_call(
        kernel,
        out_shape=jax.ShapeDtypeStruct((1, 128, 1152), BF16),
        in_specs=[in_smem, in_hbm, in_vmem, in_vmem, in_hbm] + [in_vmem] * 7,
        out_specs=in_vmem,
        scratch_shapes=[
            pltpu.VMEM((768, C), BF16),
            pltpu.VMEM((3, 256, C), BF16),
            pltpu.VMEM((9 * C, C), BF16),
            pltpu.VMEM((3, 288, C), BF16),
            pltpu.VMEM((256, C), BF16),
            pltpu.VMEM((256, C), BF16),
            pltpu.VMEM((8, 128), F32),
            pltpu.VMEM((1, 128), I32),
            pltpu.VMEM((N_SEQ, 1, 128), I32),
            pltpu.VMEM((80, 144), BF16),
            pltpu.VMEM((N_DP, 80, 144), BF16),
            pltpu.VMEM((80, 1152), BF16),
            pltpu.VMEM((3, 64, 128), BF16),
            pltpu.VMEM((2, 64, 128), BF16),
            dma,
            dma,
            dma((N_SEQ,)),
            dma((N_SEQ,)),
            dma((N_DP,)),
            dma((N_DP,)),
            dma((2,)),
            dma((2,)),
        ],
        compiler_params=pltpu.CompilerParams(
            collective_id=0, has_side_effects=True, vmem_limit_bytes=60 << 20
        ),
    )(
        kind, feat, bg.reshape(1, C), bs.reshape(1, C), w, bb.reshape(1, C), fg.reshape(1, C),
        fs.reshape(1, C), lw, lb.reshape(1, 16), ew, eb.reshape(1, 144),
    )


def solution(mesh):
    shared = P()
    return jax.shard_map(
        local,
        mesh=mesh,
        in_specs=(P("dp", "seq", None), P("dp", "seq")) + (shared,) * 8 + (P(None, "dp"), P("dp")),
        out_specs=P("dp", "seq", None),
        check_vma=False,
    )
```

```python
import functools
import jax
import jax.numpy as jnp
from jax import lax
from jax.experimental import pallas as pl
from jax.experimental.pallas import tpu as pltpu
from jax.sharding import PartitionSpec as P

F32, BF16, I32 = jnp.float32, jnp.bfloat16, jnp.int32
MESH = pl.DeviceIdType.MESH
LATENT_SHIFT = 0.0609
LATENT_SCALE = 1.5305
EPS = 1e-06
C = 512
HID = 1152
TAPS = [(a, b) for a in (-1, 0, 1) for b in (-1, 0, 1)]
N_DP, N_Z, N_X = 8, 8, 4


def iota(shape, dim):
    return lax.broadcasted_iota(I32, shape, dim)


def lane_tiles(v):
    return [v[:, 128 * i : 128 * i + 128] for i in range(v.shape[1] // 128)]


def group_sums(parts, block):
    rows = jnp.concatenate([t for p in parts for t in lane_tiles(p)], axis=0)
    hi = rows.astype(BF16)
    rest = rows - hi.astype(F32)
    mid = rest.astype(BF16)
    low = (rest - mid.astype(F32)).astype(BF16)
    sums = jnp.dot(jnp.concatenate([hi, mid, low], axis=0), block, preferred_element_type=F32)
    count = rows.shape[0]
    total = sums[:count] + sums[count : 2 * count] + sums[2 * count :]
    out = []
    for i in range(len(parts)):
        tiles = []
        for j in range(4):
            tile = total[32 * i + 8 * j : 32 * i + 8 * j + 8]
            tiles.append(jnp.broadcast_to(jnp.sum(tile, axis=0, keepdims=True), (8, 128)))
        out.append(jnp.concatenate(tiles, axis=1))
    return out


def norm_scales(load, block, joined, gain, shift):
    zero = jnp.zeros((8, C), F32)
    low, high = zero, zero
    for r in range(16):
        x0, x1 = load(r)
        low, high = low + x0, high + x1
    m0, m1 = group_sums([low, high], block)
    m0, m1 = m0 * (1.0 / 2048), m1 * (1.0 / 2048)
    both = (m0 + m1) * 0.5
    c0, c1 = jnp.where(joined, both, m0), jnp.where(joined, both, m1)
    low, high = zero, zero
    for r in range(16):
        x0, x1 = load(r)
        x0, x1 = x0 - c0, x1 - c1
        low, high = low + x0 * x0, high + x1 * x1
    v0, v1 = group_sums([low, high], block)
    v0, v1 = v0 * (1.0 / 2048), v1 * (1.0 / 2048)
    both = (v0 + v1) * 0.5
    v0, v1 = jnp.where(joined, both, v0), jnp.where(joined, both, v1)
    s0 = lax.rsqrt(v0 + EPS) * gain * 0.5
    s1 = lax.rsqrt(v1 + EPS) * gain * 0.5
    return c0, c1, s0, s1, jnp.broadcast_to(shift * 0.5, (8, C))


def silu_half(half):
    return half + half * jnp.tanh(half)


def side_shifts(y):
    col = iota((8, C), 0)
    left = jnp.where(col >= 1, pltpu.roll(y, 1, 0), 0.0)
    right = jnp.where(col <= 6, pltpu.roll(y, 7, 0), 0.0)
    return left, y, right


def pair(top, bottom):
    return jnp.concatenate([top, bottom], axis=0).astype(BF16)


def norm_first(load, block, joined, gain, shift, pad):
    c0, c1, s0, s1, t = norm_scales(load, block, joined, gain, shift)
    zero = jnp.zeros((8, C), F32)
    for r in range(16):
        x0, x1 = load(r)
        y0, y1 = silu_half((x0 - c0) * s0 + t), silu_half((x1 - c1) * s1 + t)
        sides0, sides1 = side_shifts(y0), side_shifts(y1)
        for b in range(3):
            pad[b, 16 * (r + 1) : 16 * (r + 2), :] = pair(sides0[b], sides1[b])
            if r == 0:
                pad[b, 16 * 17 : 16 * 18, :] = pair(jnp.where(joined, sides1[b], 0.0), zero)
            if r == 15:
                pad[b, 0:16, :] = pair(zero, jnp.where(joined, sides0[b], 0.0))


def conv(pad, w, res):
    lhs = jnp.concatenate(
        [pad[b + 1, 16 * (a + 1) : 16 * (a + 1) + 256, :] for a, b in TAPS], axis=1
    )
    res[...] = jnp.dot(lhs, w[...], preferred_element_type=F32)


def residual(load, res, bias, inner):
    for r in range(16):
        x0, x1 = load(r)
        top, bottom = res[16 * r : 16 * r + 8, :], res[16 * r + 8 : 16 * r + 16, :]
        inner[16 * r : 16 * r + 16, :] = pair(top + x0 + bias, bottom + x1 + bias)


def norm_second(load, block, joined, gain, shift, act):
    c0, c1, s0, s1, t = norm_scales(load, block, joined, gain, shift)
    for r in range(16):
        x0, x1 = load(r)
        act[16 * r : 16 * r + 16, :] = pair(
            silu_half((x0 - c0) * s0 + t), silu_half((x1 - c1) * s1 + t)
        )


def latent_patches(act, lw3, lat_bias, joined, select):
    terms = jnp.dot(act[...], lw3, preferred_element_type=F32)
    joined = joined[:, :128]
    zero = jnp.zeros((8, 128), F32)

    def part(a, r, h):
        return terms[16 * r + 8 * h : 16 * r + 8 * h + 8, 128 * (a + 1) : 128 * (a + 2)]

    col = iota((8, 128), 0)
    lane = iota((8, 128), 1)
    rows = []
    for p in range(8):
        for h in range(2):
            total = None
            for i in range(2):
                r = 2 * p + i
                above = part(-1, r - 1, h) if r > 0 else (jnp.where(joined, part(-1, 15, 0), 0.0) if h == 1 else zero)
                below = part(1, r + 1, h) if r < 15 else (jnp.where(joined, part(1, 0, 1), 0.0) if h == 0 else zero)
                z = above + part(0, r, h) + below
                left = jnp.where(col >= 1, pltpu.roll(z, 1, 0), 0.0)
                right = jnp.where(col <= 6, pltpu.roll(z, 7, 0), 0.0)
                if i == 0:
                    lat = left + pltpu.roll(z, 96, 1) + pltpu.roll(right, 64, 1)
                else:
                    lat = pltpu.roll(left, 32, 1) + z + pltpu.roll(right, 96, 1)
                lat = (lat + lat_bias - LATENT_SHIFT) * LATENT_SCALE
                own = (lane // 16) == (2 * i + col % 2)
                lat = jnp.where(own, lat, 0.0)
                total = lat if total is None else total + lat
            rows.append(total)
    cells = jnp.concatenate(rows, axis=0).astype(BF16)
    return jnp.dot(select, cells, preferred_element_type=F32).astype(BF16)


def tap_columns(lwt, lw3):
    zero = jnp.zeros((16, C), BF16)
    for a in range(3):
        taps = [lwt[16 * (3 * a + b) : 16 * (3 * a + b) + 16, :] for b in range(3)]
        rows = jnp.concatenate([taps[0], taps[0], taps[1], taps[1], taps[2], taps[2], zero, zero], axis=0)
        lw3[:, 128 * a : 128 * a + 128] = rows.T


def masks():
    block = jnp.where(iota((128, 128), 0) // 16 == iota((128, 128), 1) // 16, 1.0, 0.0).astype(BF16)
    t, m = iota((64, 128), 0), iota((64, 128), 1)
    same = (m // 16 == (t // 4) % 8) & ((m // 8) % 2 == t // 32) & ((m % 8) // 2 == t % 4)
    return block, jnp.where(same, 1.0, 0.0).astype(BF16)


DP_ORDER = (6, 4, 2, 7, 5, 3, 1, 0)


def exchange(pairs, start_now):
    for condition, copy, ready in pairs:

        @pl.when(condition)
        def _(copy=copy, ready=ready):
            if not start_now:
                pl.semaphore_wait(ready, 1)
            copy.start()


def kernel(
    kind_hbm, feat_hbm, bg_hbm, bs_hbm, w_hbm, bb_hbm, fg_hbm, fs_hbm, lw_hbm, lb_hbm, ew_hbm, eb_hbm,
    patch_out, embed_out,
    kind, feat, bg, bs, w, bb, fg, fs, lw, lb, ew, eb,
    slots, pad, res, inner, act, lw3, lanes, mine, rowsum, xcounts, zsums, shard, shards, sent, got,
    in_sem, x_send, x_recv, z_send, z_recv, d_send, d_recv, p_send, p_recv, x_ready, z_ready, d_ready,
):
    seat, row = lax.axis_index("seq"), lax.axis_index("dp")
    z, x = seat // N_X, lax.rem(seat, N_X)
    rank = jnp.where(row == 0, 7, jnp.where(lax.rem(row, 2) == 0, 3 - row // 2, 6 - row // 2))

    def at_x(i):
        return {"seq": z * N_X + i}

    def at_z(i):
        return {"seq": i * N_X + x}

    fetches = [
        pltpu.make_async_copy(source, target, in_sem.at[i])
        for i, (source, target) in enumerate(
            [
                (kind_hbm, kind), (feat_hbm.at[0], feat), (w_hbm, w), (lw_hbm, lw), (bg_hbm, bg), (bs_hbm, bs),
                (bb_hbm, bb), (fg_hbm, fg), (fs_hbm, fs), (lb_hbm, lb), (ew_hbm, ew), (eb_hbm, eb),
            ]
        )
    ]
    for fetch in fetches:
        fetch.start()
    zsums[...] = jnp.zeros((N_Z, 1, 128), I32)
    got[...] = jnp.zeros((2, 64, 128), BF16)
    lanes[...] = jnp.zeros((8, 128), F32)

    barrier = pltpu.get_barrier_semaphore()

    def greet(target):
        pl.semaphore_signal(barrier, inc=1, device_id=target, device_id_type=MESH)

    for i in range(1, N_X):
        pl.when(i > x)(functools.partial(greet, at_x(i)))
    for i in range(1, N_Z):
        pl.when(i > z)(functools.partial(greet, at_z(i)))
    for i in range(1, N_DP):
        pl.when(i > rank)(functools.partial(greet, {"dp": DP_ORDER[i]}))
    pl.when((x == 0) & (z > 0))(functools.partial(greet, {"seq": seat - 1}))

    block, select = masks()
    for fetch in fetches[:2] + fetches[3:]:
        fetch.wait()
    live = [(kind[0, i] > 0).astype(I32) for i in range(3)]
    n = live[0] + live[1] + live[2]
    kinds = [
        jnp.where(n == 3, kind[0, 2], jnp.where(n == 2, kind[0, 1], kind[0, 0])),
        jnp.where(n == 2, kind[0, 0], kind[0, 1]),
        jnp.where(n == 3, kind[0, 0], kind[0, 2]),
    ]
    joined = [jnp.full((8, C), kinds[t], I32) == 2 for t in range(3)]
    mine[...] = jnp.full((1, 128), n, I32)
    xcounts[pl.ds(x, 1)] = jnp.full((1, 1, 128), n, I32)
    shard[0:64, :] = ew[...]
    bias_row = jnp.broadcast_to(eb[...].reshape(1, 144).astype(F32), (16, 144))
    shard[64:80, :] = jnp.where(iota((16, 144), 0) == 0, bias_row, 0.0).astype(BF16)
    shards[pl.ds(row, 1)] = shard[...].reshape(1, 80, 144)
    lanes[0:1, 0:16] = lb[...]
    lat_bias = lanes[...]
    for step in (16, 32, 64):
        lat_bias = lat_bias + pltpu.roll(lat_bias, step, 1)
    lat_bias = lat_bias[0:1]
    tap_columns(lw, lw3)

    number = jnp.full((16, C), n, I32)
    for i in range(16):
        first, middle, last = [feat[256 * k + 16 * i : 256 * k + 16 * i + 16, :] for k in range(3)]
        part = slice(16 * i, 16 * i + 16)
        slots[0, part, :] = jnp.where(number == 3, last, jnp.where(number == 2, middle, first))
        slots[1, part, :] = jnp.where(number == 2, first, middle)
        slots[2, part, :] = jnp.where(number == 3, first, last)

    def loader(t):
        def load(r):
            return slots[t, 8 * r : 8 * r + 8, :].astype(F32), slots[t, 128 + 8 * r : 136 + 8 * r, :].astype(F32)

        return load

    def inner_loader(t):
        def load(r):
            v = inner[t, 16 * r : 16 * r + 16, :].astype(F32)
            return v[:8], v[8:]

        return load

    def first_norm(t):
        norm_first(loader(t), block, joined[t], bg[...], bs[...], pad.at[t])

    def convolve(t):
        conv(pad.at[t], w, res.at[t])

    def finish(t):
        residual(loader(t), res.at[t], jnp.broadcast_to(bb[...], (8, C)), inner.at[t])
        norm_second(inner_loader(t), block, joined[t], fg[...], fs[...], act.at[t])
        sent[t] = latent_patches(act.at[t], lw3[...], lat_bias, joined[t], select)

    def copy_to(source, target, send_sem, recv_sem, device):
        return pltpu.make_async_remote_copy(
            src_ref=source, dst_ref=target, send_sem=send_sem, recv_sem=recv_sem,
            device_id=device, device_id_type=MESH,
        )

    x_copies = [copy_to(mine, xcounts.at[x], x_send.at[i], x_recv.at[x], at_x(i)) for i in range(N_X)]
    x_arrivals = [copy_to(mine, xcounts.at[i], x_send.at[i], x_recv.at[i], at_x(i)) for i in range(N_X)]
    z_copies = [copy_to(rowsum, zsums.at[z], z_send.at[i], z_recv.at[z], at_z(i)) for i in range(N_Z)]
    z_arrivals = [copy_to(rowsum, zsums.at[i], z_send.at[i], z_recv.at[i], at_z(i)) for i in range(N_Z)]
    d_peers = [{"dp": DP_ORDER[i]} for i in range(N_DP)]
    d_copies = [copy_to(shard, shards.at[row], d_send.at[i], d_recv.at[rank], d_peers[i]) for i in range(N_DP)]
    d_arrivals = [
        copy_to(shard, shards.at[DP_ORDER[i]], d_send.at[i], d_recv.at[i], d_peers[i]) for i in range(N_DP)
    ]
    p_copies = [
        copy_to(sent.at[t], got.at[t], p_send.at[t], p_recv.at[t], {"seq": lax.rem(seat + 1, N_Z * N_X)})
        for t in range(2)
    ]

    def send_patch(t):
        pl.when(seat < N_Z * N_X - 1)(p_copies[t].start)

    first_norm(0)
    earlier = x + z + rank + ((x == N_X - 1) & (z < N_Z - 1)).astype(I32)

    @pl.when(earlier > 0)
    def _():
        pl.semaphore_wait(barrier, earlier)


    def ready(sem, target):
        pl.semaphore_signal(sem, inc=1, device_id=target, device_id_type=MESH)

    for i in range(N_X - 1):
        pl.when(i < x)(functools.partial(ready, x_ready.at[x], at_x(i)))
    for i in range(N_Z - 1):
        pl.when(i < z)(functools.partial(ready, z_ready.at[z], at_z(i)))
    for i in range(N_DP - 1):
        pl.when(i < rank)(functools.partial(ready, d_ready.at[rank], d_peers[i]))
    exchange([(i < x, x_copies[i], None) for i in range(N_X - 1)], True)
    exchange([(i < rank, d_copies[i], None) for i in range(N_DP - 1)], True)

    first_norm(1)
    fetches[2].wait()
    convolve(0)
    first_norm(2)
    exchange([(i > x, x_copies[i], x_ready.at[i]) for i in range(1, N_X)], False)
    exchange([(i > rank, d_copies[i], d_ready.at[i]) for i in range(1, N_DP)], False)

    convolve(1)
    finish(0)
    send_patch(0)

    for i in range(N_X):
        pl.when(i != x)(x_arrivals[i].wait_recv)
    rowsum[...] = jnp.sum(xcounts[...], axis=0)
    exchange([((i > z) & (i < z + 4), z_copies[i], z_ready.at[i]) for i in range(1, N_Z)], False)

    convolve(2)
    finish(1)
    send_patch(1)

    exchange([(i >= z + 4, z_copies[i], z_ready.at[i]) for i in range(4, N_Z)], False)
    for i in range(N_DP):
        pl.when(i != rank)(d_arrivals[i].wait_recv)
    for i in range(N_DP):
        embed_out[:, 144 * i : 144 * i + 144] = shards[i]

    finish(2)
    for i in range(N_Z - 1):
        pl.when(i < z)(z_arrivals[i].wait_recv)
    before = jnp.where(iota((N_X, 1, 128), 0) < x, xcounts[...], 0)
    carry_in = jnp.sum(zsums[...], axis=0) + jnp.sum(before, axis=0) - 2 * seat
    for i in range(N_X):
        pl.when(i != x)(x_arrivals[i].wait_send)
    for i in range(N_DP):
        pl.when(i != rank)(d_arrivals[i].wait_send)
    for i in range(1, N_Z):
        pl.when(i > z)(z_arrivals[i].wait_send)
    for t in range(2):
        pl.when(seat < N_Z * N_X - 1)(p_copies[t].wait_send)
    for t in range(2):
        pl.when(seat > 0)(p_copies[t].wait_recv)

    carry_in = jnp.broadcast_to(carry_in, (64, 128))
    number = jnp.full((64, 128), n, I32)
    own = [sent[t].astype(F32) for t in range(3)]
    came = [got[t].astype(F32) for t in range(2)]
    newest = jnp.where(number == 3, own[2], jnp.where(number == 2, own[1], own[0]))
    second = jnp.where(number == 3, own[1], own[0])
    out0 = jnp.where(carry_in == 0, newest, jnp.where(carry_in == 1, came[0], came[1]))
    out1 = jnp.where(carry_in == 0, second, jnp.where(carry_in == 1, newest, came[0]))
    patches = jnp.concatenate([out0, out1], axis=0)
    patches = jnp.where(iota((128, 128), 1) == 64, 1.0, patches).astype(BF16)
    patch_out[...] = patches[:, :80]


def local(feat, kind, bg, bs, w, bb, fg, fs, lw, lb, ew, eb):
    hbm = pl.BlockSpec(memory_space=pl.ANY)
    vmem = pl.BlockSpec(memory_space=pltpu.VMEM)
    dma, regular, V = pltpu.SemaphoreType.DMA, pltpu.SemaphoreType.REGULAR, pltpu.VMEM
    vec = V((1, C), F32)
    patches, embed = pl.pallas_call(
        kernel,
        out_shape=(jax.ShapeDtypeStruct((128, 80), BF16), jax.ShapeDtypeStruct((80, HID), BF16)),
        in_specs=[hbm] * 12,
        out_specs=(vmem, vmem),
        scratch_shapes=[
            pltpu.SMEM((1, 3), I32), V((768, C), BF16), vec, vec, V((9 * C, C), BF16), vec, vec, vec,
            V((144, C), BF16), V((1, 16), F32), V((64, 144), BF16), V((144,), BF16),
            V((3, 256, C), BF16), V((3, 3, 288, C), BF16), V((3, 256, C), F32), V((3, 256, C), BF16),
            V((3, 256, C), BF16), V((C, 384), BF16), V((8, 128), F32), V((1, 128), I32), V((1, 128), I32),
            V((N_X, 1, 128), I32), V((N_Z, 1, 128), I32), V((80, 144), BF16), V((N_DP, 80, 144), BF16),
            V((3, 64, 128), BF16), V((2, 64, 128), BF16),
            dma((12,)), dma((N_X,)), dma((N_X,)), dma((N_Z,)), dma((N_Z,)), dma((N_DP,)), dma((N_DP,)),
            dma((2,)), dma((2,)), regular((N_X,)), regular((N_Z,)), regular((N_DP,)),
        ],
        compiler_params=pltpu.CompilerParams(
            collective_id=0, has_side_effects=True, vmem_limit_bytes=60 << 20
        ),
    )(
        kind, feat, bg.reshape(1, C), bs.reshape(1, C), w, bb.reshape(1, C), fg.reshape(1, C),
        fs.reshape(1, C), lw.T, lb.reshape(1, 16), ew, eb,
    )
    return jnp.dot(patches, embed, preferred_element_type=F32).astype(BF16)[None]


def solution(mesh):
    shared = P()
    return jax.shard_map(
        local,
        mesh=mesh,
        in_specs=(P("dp", "seq", None), P("dp", "seq")) + (shared,) * 8 + (P(None, "dp"), P("dp")),
        out_specs=P("dp", "seq", None),
        check_vma=False,
    )
```

```python
import functools
import jax
import jax.numpy as jnp
from jax import lax
from jax.experimental import pallas as pl
from jax.experimental.pallas import tpu as pltpu
from jax.sharding import PartitionSpec as P

F32, BF16, I32 = jnp.float32, jnp.bfloat16, jnp.int32
MESH = pl.DeviceIdType.MESH
LATENT_SHIFT = 0.0609
LATENT_SCALE = 1.5305
EPS = 1e-06
C = 512
HID = 1152
TAPS = [(a, b) for a in (-1, 0, 1) for b in (-1, 0, 1)]
N_DP, N_Z, N_X = 8, 8, 4


def iota(shape, dim):
    return lax.broadcasted_iota(I32, shape, dim)


def drain(*streams):
    live = [[stream, steps, 0] for stream, steps in streams]
    while live:
        entry = min(live, key=lambda e: (e[2] + 1) / e[1])
        entry[2] += 1
        try:
            next(entry[0])
        except StopIteration:
            live.remove(entry)


def group_sums(parts, block):
    rows = jnp.concatenate([p[:, 256 * i : 256 * i + 256] for p in parts for i in range(2)], axis=0)
    hi = rows.astype(BF16)
    rest = rows - hi.astype(F32)
    mid = rest.astype(BF16)
    low = (rest - mid.astype(F32)).astype(BF16)
    sums = jnp.dot(jnp.concatenate([hi, mid, low], axis=0), block, preferred_element_type=F32)
    total = sums[:32] + sums[32:64] + sums[64:]
    out = []
    for i in range(len(parts)):
        tiles = [total[16 * i + 8 * j : 16 * i + 8 * j + 8] for j in range(2)]
        tiles = [jnp.broadcast_to(jnp.sum(t, axis=0, keepdims=True), (8, 256)) for t in tiles]
        out.append(jnp.concatenate(tiles, axis=1))
    return out


def norm_factors(sums, load, block, joined, gain, shift):
    m0, m1 = group_sums(sums, block)
    m0, m1 = m0 * (1.0 / 2048), m1 * (1.0 / 2048)
    both = (m0 + m1) * 0.5
    c0, c1 = jnp.where(joined, both, m0), jnp.where(joined, both, m1)
    low, high = jnp.zeros((8, C), F32), jnp.zeros((8, C), F32)
    for r in range(16):
        x0, x1 = load(r)
        x0, x1 = x0 - c0, x1 - c1
        low, high = low + x0 * x0, high + x1 * x1
        yield
    v0, v1 = group_sums([low, high], block)
    v0, v1 = v0 * (1.0 / 2048), v1 * (1.0 / 2048)
    both = (v0 + v1) * 0.5
    v0, v1 = jnp.where(joined, both, v0), jnp.where(joined, both, v1)
    s0 = lax.rsqrt(v0 + EPS) * gain * 0.5
    s1 = lax.rsqrt(v1 + EPS) * gain * 0.5
    return s0, s1, shift * 0.5 - c0 * s0, shift * 0.5 - c1 * s1


def silu_half(half):
    return half + half * jnp.tanh(half)


def pair(top, bottom):
    return jnp.concatenate([top, bottom], axis=0).astype(BF16)


def loader(ref):
    def load(r):
        return ref[16 * r : 16 * r + 8, :], ref[16 * r + 8 : 16 * r + 16, :]

    return load


def order_slot(pick, slot):
    low, high = jnp.zeros((8, C), F32), jnp.zeros((8, C), F32)
    for i in range(8):
        top, bottom = pick(16 * i).astype(F32), pick(128 + 16 * i).astype(F32)
        for j in range(2):
            x0, x1 = top[8 * j : 8 * j + 8], bottom[8 * j : 8 * j + 8]
            r = 2 * i + j
            slot[16 * r : 16 * r + 8, :], slot[16 * r + 8 : 16 * r + 16, :] = x0, x1
            low, high = low + x0, high + x1
        yield
    return low, high


def norm_first(pick, slot, block, joined, gain, shift, pad):
    sums = yield from order_slot(pick, slot)
    load = loader(slot)
    s0, s1, t0, t1 = yield from norm_factors(sums, load, block, joined, gain, shift)
    zero = jnp.zeros((8, C), F32)
    col = iota((8, C), 0)
    for r in range(16):
        x0, x1 = load(r)
        sides = []
        for y in (silu_half(x0 * s0 + t0), silu_half(x1 * s1 + t1)):
            left = jnp.where(col >= 1, pltpu.roll(y, 1, 0), 0.0)
            right = jnp.where(col <= 6, pltpu.roll(y, 7, 0), 0.0)
            sides.append((left, y, right))
        for b in range(3):
            pad[b, 16 * (r + 1) : 16 * (r + 2), :] = pair(sides[0][b], sides[1][b])
            if r == 0:
                pad[b, 16 * 17 : 16 * 18, :] = pair(jnp.where(joined, sides[1][b], 0.0), zero)
            if r == 15:
                pad[b, 0:16, :] = pair(zero, jnp.where(joined, sides[0][b], 0.0))
        yield


def conv(pad, w, res):
    lhs = jnp.concatenate(
        [pad[b + 1, 16 * (a + 1) : 16 * (a + 1) + 256, :] for a, b in TAPS], axis=1
    )
    res[...] = jnp.dot(lhs, w[...], preferred_element_type=F32)


def finish(slot, res, bias, block, joined, gain, shift, act, lw3, lat_bias, select, out):
    own, added = loader(slot), loader(res)
    low, high = jnp.zeros((8, C), F32), jnp.zeros((8, C), F32)
    for r in range(16):
        (x0, x1), (d0, d1) = own(r), added(r)
        x0, x1 = x0 + d0 + bias, x1 + d1 + bias
        res[16 * r : 16 * r + 8, :], res[16 * r + 8 : 16 * r + 16, :] = x0, x1
        low, high = low + x0, high + x1
        yield
    s0, s1, t0, t1 = yield from norm_factors([low, high], added, block, joined, gain, shift)
    for r in range(16):
        x0, x1 = added(r)
        act[16 * r : 16 * r + 16, :] = pair(silu_half(x0 * s0 + t0), silu_half(x1 * s1 + t1))
        yield
    yield from latent_patches(act, lw3, lat_bias, joined, select, out)


def latent_patches(act, lw3, lat_bias, joined, select, out):
    terms = jnp.dot(act[...], lw3[...], preferred_element_type=F32)
    yield
    joined = joined[:, :128]
    zero = jnp.zeros((8, 128), F32)

    def part(a, r, h):
        return terms[16 * r + 8 * h : 16 * r + 8 * h + 8, 128 * (a + 1) : 128 * (a + 2)]

    col = iota((8, 128), 0)
    lane = iota((8, 128), 1)
    rows = []
    for r in range(16):
        for h in range(2):
            i = r % 2
            above = part(-1, r - 1, h) if r > 0 else (jnp.where(joined, part(-1, 15, 0), 0.0) if h == 1 else zero)
            below = part(1, r + 1, h) if r < 15 else (jnp.where(joined, part(1, 0, 1), 0.0) if h == 0 else zero)
            v = above + part(0, r, h) + below
            left = jnp.where(col >= 1, pltpu.roll(v, 1, 0), 0.0)
            right = jnp.where(col <= 6, pltpu.roll(v, 7, 0), 0.0)
            if i == 0:
                lat = left + pltpu.roll(v, 96, 1) + pltpu.roll(right, 64, 1)
            else:
                lat = pltpu.roll(left, 32, 1) + v + pltpu.roll(right, 96, 1)
            lat = (lat + lat_bias - LATENT_SHIFT) * LATENT_SCALE
            rows.append(jnp.where((lane // 16) == (2 * i + col % 2), lat, 0.0))
        if r % 2:
            yield
    cells = jnp.concatenate(rows, axis=0).astype(BF16)
    out[...] = jnp.dot(select, cells, preferred_element_type=F32).astype(BF16)


def tap_columns(lwt, lw3):
    zero = jnp.zeros((16, C), BF16)
    for a in range(3):
        taps = [lwt[16 * (3 * a + b) : 16 * (3 * a + b) + 16, :] for b in range(3)]
        rows = jnp.concatenate([taps[0], taps[0], taps[1], taps[1], taps[2], taps[2], zero, zero], axis=0)
        lw3[:, 128 * a : 128 * a + 128] = rows.T


def masks():
    block = jnp.where(iota((256, 256), 0) // 16 == iota((256, 256), 1) // 16, 1.0, 0.0).astype(BF16)
    t, m = iota((64, 256), 0), iota((64, 256), 1)
    same = (m // 32 == (t // 4) % 8) & ((m // 8) % 2 == t // 32) & ((m % 8) // 2 == t % 4)
    return block, jnp.where(same, 1.0, 0.0).astype(BF16)


DP_ORDER = (0, 1, 2, 6, 3, 7, 4, 5)


def exchange(pairs, start_now):
    for condition, copy, ready in pairs:

        @pl.when(condition)
        def _(copy=copy, ready=ready):
            if not start_now:
                pl.semaphore_wait(ready, 1)
            copy.start()


def kernel(
    kind_hbm, feat_hbm, bg_hbm, bs_hbm, w_hbm, bb_hbm, fg_hbm, fs_hbm, lw_hbm, lb_hbm, ew_hbm, eb_hbm,
    patch_out, embed_out,
    kind, feat, bg, bs, w, bb, fg, fs, lw, lb, ew, eb,
    slots, pad, res, act, lw3, lanes, mine, rowsum, xcounts, zsums, shard, shards, sent, got,
    in_sem, x_send, x_recv, z_send, z_recv, d_send, d_recv, p_send, p_recv, x_ready, z_ready, d_ready,
):
    seat, row = lax.axis_index("seq"), lax.axis_index("dp")
    z, x = seat // N_X, lax.rem(seat, N_X)
    rank = sum(jnp.where(row == DP_ORDER[i], i, 0) for i in range(N_DP))

    def at_x(i):
        return {"seq": z * N_X + i}

    def at_z(i):
        return {"seq": i * N_X + x}

    fetches = [
        pltpu.make_async_copy(source, target, in_sem.at[i])
        for i, (source, target) in enumerate(
            [
                (kind_hbm, kind), (feat_hbm.at[0], feat), (w_hbm, w), (lw_hbm, lw), (bg_hbm, bg), (bs_hbm, bs),
                (bb_hbm, bb), (fg_hbm, fg), (fs_hbm, fs), (lb_hbm, lb), (ew_hbm, ew), (eb_hbm, eb),
            ]
        )
    ]
    for fetch in fetches:
        fetch.start()
    zsums[...] = jnp.zeros((N_Z, 1, 128), I32)
    got[...] = jnp.zeros((2, 64, 128), BF16)
    lanes[...] = jnp.zeros((8, 128), F32)

    barrier = pltpu.get_barrier_semaphore()

    def greet(target):
        pl.semaphore_signal(barrier, inc=1, device_id=target, device_id_type=MESH)

    for i in range(1, N_X):
        pl.when(i > x)(functools.partial(greet, at_x(i)))
    for i in range(1, N_Z):
        pl.when(i > z)(functools.partial(greet, at_z(i)))
    for i in range(1, N_DP):
        pl.when(i > rank)(functools.partial(greet, {"dp": DP_ORDER[i]}))
    pl.when((x == 0) & (z > 0))(functools.partial(greet, {"seq": seat - 1}))

    block, select = masks()
    for fetch in fetches[:2] + fetches[3:]:
        fetch.wait()
    live = [(kind[0, i] > 0).astype(I32) for i in range(3)]
    n = live[0] + live[1] + live[2]
    kinds = [
        jnp.where(n == 3, kind[0, 2], jnp.where(n == 2, kind[0, 1], kind[0, 0])),
        jnp.where(n == 2, kind[0, 0], kind[0, 1]),
        jnp.where(n == 3, kind[0, 0], kind[0, 2]),
    ]
    joined = [jnp.full((8, C), kinds[t], I32) == 2 for t in range(3)]
    mine[...] = jnp.full((1, 128), n, I32)
    xcounts[pl.ds(x, 1)] = jnp.full((1, 1, 128), n, I32)
    shard[0:64, :] = ew[...]
    bias_row = jnp.broadcast_to(eb[...].reshape(1, 144).astype(F32), (16, 144))
    shard[64:80, :] = jnp.where(iota((16, 144), 0) == 0, bias_row, 0.0).astype(BF16)
    shards[pl.ds(row, 1)] = shard[...].reshape(1, 80, 144)
    lanes[0:1, 0:16] = lb[...]
    lat_bias = lanes[...]
    for step in (16, 32, 64):
        lat_bias = lat_bias + pltpu.roll(lat_bias, step, 1)
    lat_bias = lat_bias[0:1]

    number = jnp.full((16, C), n, I32)

    def cells(k, i):
        return feat[256 * k + i : 256 * k + i + 16, :]

    def pick(t):
        def rows(i):
            if t == 0:
                return jnp.where(number == 3, cells(2, i), jnp.where(number == 2, cells(1, i), cells(0, i)))
            if t == 1:
                return jnp.where(number == 2, cells(0, i), cells(1, i))
            return jnp.where(number == 3, cells(0, i), cells(2, i))

        return rows

    def spread(vector):
        return jnp.broadcast_to(vector[...], (8, C))

    def first_norm(t):
        return norm_first(pick(t), slots.at[t], block, joined[t], spread(bg), spread(bs), pad.at[t])

    def convolve(t):
        conv(pad.at[t], w, res.at[t])

    def last(t):
        return finish(
            slots.at[t], res.at[t], spread(bb), block, joined[t], spread(fg), spread(fs), act.at[t],
            lw3, lat_bias, select, sent.at[t],
        )

    def copy_to(source, target, send_sem, recv_sem, device):
        return pltpu.make_async_remote_copy(
            src_ref=source, dst_ref=target, send_sem=send_sem, recv_sem=recv_sem,
            device_id=device, device_id_type=MESH,
        )

    x_copies = [copy_to(mine, xcounts.at[x], x_send.at[i], x_recv.at[x], at_x(i)) for i in range(N_X)]
    x_arrivals = [copy_to(mine, xcounts.at[i], x_send.at[i], x_recv.at[i], at_x(i)) for i in range(N_X)]
    z_copies = [copy_to(rowsum, zsums.at[z], z_send.at[i], z_recv.at[z], at_z(i)) for i in range(N_Z)]
    z_arrivals = [copy_to(rowsum, zsums.at[i], z_send.at[i], z_recv.at[i], at_z(i)) for i in range(N_Z)]
    d_peers = [{"dp": DP_ORDER[i]} for i in range(N_DP)]
    d_copies = [copy_to(shard, shards.at[row], d_send.at[i], d_recv.at[rank], d_peers[i]) for i in range(N_DP)]
    d_arrivals = [
        copy_to(shard, shards.at[DP_ORDER[i]], d_send.at[i], d_recv.at[i], d_peers[i]) for i in range(N_DP)
    ]
    p_copies = [
        copy_to(sent.at[t], got.at[t], p_send.at[t], p_recv.at[t], {"seq": lax.rem(seat + 1, N_Z * N_X)})
        for t in range(2)
    ]

    def send_patch(t):
        pl.when(seat < N_Z * N_X - 1)(p_copies[t].start)

    earlier = x + z + rank + ((x == N_X - 1) & (z < N_Z - 1)).astype(I32)

    @pl.when(earlier > 0)
    def _():
        pl.semaphore_wait(barrier, earlier)


    def ready(sem, target):
        pl.semaphore_signal(sem, inc=1, device_id=target, device_id_type=MESH)

    for i in range(N_X - 1):
        pl.when(i < x)(functools.partial(ready, x_ready.at[x], at_x(i)))
    for i in range(N_Z - 1):
        pl.when(i < z)(functools.partial(ready, z_ready.at[z], at_z(i)))
    for i in range(N_DP - 1):
        pl.when(i < rank)(functools.partial(ready, d_ready.at[rank], d_peers[i]))
    exchange([(i < x, x_copies[i], None) for i in range(N_X - 1)], True)
    exchange([(i < rank, d_copies[i], None) for i in range(N_DP - 1)], True)

    tap_columns(lw, lw3)
    drain((first_norm(0), 42), (first_norm(1), 42))
    fetches[2].wait()
    convolve(0)
    drain((last(0), 60), (first_norm(2), 42))
    exchange([(i > x, x_copies[i], x_ready.at[i]) for i in range(1, N_X)], False)
    send_patch(0)

    convolve(1)
    exchange([(i > rank, d_copies[i], d_ready.at[i]) for i in range(1, N_DP)], False)
    for i in range(N_X):
        pl.when(i != x)(x_arrivals[i].wait_recv)
    rowsum[...] = jnp.sum(xcounts[...], axis=0)
    exchange([((i > z) & (i < z + 4), z_copies[i], z_ready.at[i]) for i in range(1, N_Z)], False)
    drain((last(1), 60))
    send_patch(1)

    convolve(2)
    exchange([(i >= z + 4, z_copies[i], z_ready.at[i]) for i in range(4, N_Z)], False)
    for i in range(N_DP):
        pl.when(i != rank)(d_arrivals[i].wait_recv)
    for i in range(N_DP):
        embed_out[:, 144 * i : 144 * i + 144] = shards[i]
    drain((last(2), 60))
    for i in range(N_Z - 1):
        pl.when(i < z)(z_arrivals[i].wait_recv)
    before = jnp.where(iota((N_X, 1, 128), 0) < x, xcounts[...], 0)
    carry_in = jnp.sum(zsums[...], axis=0) + jnp.sum(before, axis=0) - 2 * seat
    for i in range(N_X):
        pl.when(i != x)(x_arrivals[i].wait_send)
    for i in range(N_DP):
        pl.when(i != rank)(d_arrivals[i].wait_send)
    for i in range(1, N_Z):
        pl.when(i > z)(z_arrivals[i].wait_send)
    for t in range(2):
        pl.when(seat < N_Z * N_X - 1)(p_copies[t].wait_send)
    for t in range(2):
        pl.when(seat > 0)(p_copies[t].wait_recv)

    carry_in = jnp.broadcast_to(carry_in, (64, 128))
    number = jnp.full((64, 128), n, I32)
    own = [sent[t].astype(F32) for t in range(3)]
    came = [got[t].astype(F32) for t in range(2)]
    newest = jnp.where(number == 3, own[2], jnp.where(number == 2, own[1], own[0]))
    second = jnp.where(number == 3, own[1], own[0])
    out0 = jnp.where(carry_in == 0, newest, jnp.where(carry_in == 1, came[0], came[1]))
    out1 = jnp.where(carry_in == 0, second, jnp.where(carry_in == 1, newest, came[0]))
    patches = jnp.concatenate([out0, out1], axis=0)
    patches = jnp.where(iota((128, 128), 1) == 64, 1.0, patches).astype(BF16)
    patch_out[...] = patches[:, :80]


def local(feat, kind, bg, bs, w, bb, fg, fs, lw, lb, ew, eb):
    hbm = pl.BlockSpec(memory_space=pl.ANY)
    vmem = pl.BlockSpec(memory_space=pltpu.VMEM)
    dma, regular, V = pltpu.SemaphoreType.DMA, pltpu.SemaphoreType.REGULAR, pltpu.VMEM
    vec = V((1, C), F32)
    patches, embed = pl.pallas_call(
        kernel,
        out_shape=(jax.ShapeDtypeStruct((128, 80), BF16), jax.ShapeDtypeStruct((80, HID), BF16)),
        in_specs=[hbm] * 12,
        out_specs=(vmem, vmem),
        scratch_shapes=[
            pltpu.SMEM((1, 3), I32), V((768, C), BF16), vec, vec, V((9 * C, C), BF16), vec, vec, vec,
            V((144, C), BF16), V((1, 16), F32), V((64, 144), BF16), V((144,), BF16),
            V((3, 256, C), F32), V((3, 3, 288, C), BF16), V((3, 256, C), F32), V((3, 256, C), BF16),
            V((C, 384), BF16), V((8, 128), F32), V((1, 128), I32), V((1, 128), I32),
            V((N_X, 1, 128), I32), V((N_Z, 1, 128), I32), V((80, 144), BF16), V((N_DP, 80, 144), BF16),
            V((3, 64, 128), BF16), V((2, 64, 128), BF16),
            dma((12,)), dma((N_X,)), dma((N_X,)), dma((N_Z,)), dma((N_Z,)), dma((N_DP,)), dma((N_DP,)),
            dma((2,)), dma((2,)), regular((N_X,)), regular((N_Z,)), regular((N_DP,)),
        ],
        compiler_params=pltpu.CompilerParams(
            collective_id=0, has_side_effects=True, vmem_limit_bytes=60 << 20
        ),
    )(
        kind, feat, bg.reshape(1, C), bs.reshape(1, C), w, bb.reshape(1, C), fg.reshape(1, C),
        fs.reshape(1, C), lw.T, lb.reshape(1, 16), ew, eb,
    )
    return jnp.dot(patches, embed, preferred_element_type=F32).astype(BF16)[None]


def solution(mesh):
    shared = P()
    return jax.shard_map(
        local,
        mesh=mesh,
        in_specs=(P("dp", "seq", None), P("dp", "seq")) + (shared,) * 8 + (P(None, "dp"), P("dp")),
        out_specs=P("dp", "seq", None),
        check_vma=False,
    )
```

```python
import functools
import jax
import jax.numpy as jnp
from jax import lax
from jax.experimental import pallas as pl
from jax.experimental.pallas import tpu as pltpu
from jax.sharding import PartitionSpec as P

F32, BF16, I32 = jnp.float32, jnp.bfloat16, jnp.int32
MESH = pl.DeviceIdType.MESH
LATENT_SHIFT = 0.0609
LATENT_SCALE = 1.5305
EPS = 1e-06
C = 512
HID = 1152
TAPS = [(a, b) for a in (-1, 0, 1) for b in (-1, 0, 1)]
N_DP, N_Z, N_X = 8, 8, 4


def iota(shape, dim):
    return lax.broadcasted_iota(I32, shape, dim)


def drain(*streams):
    live = [[stream, steps, 0] for stream, steps in streams]
    while live:
        entry = min(live, key=lambda e: (e[2] + 1) / e[1])
        entry[2] += 1
        try:
            next(entry[0])
        except StopIteration:
            live.remove(entry)


def group_sums(parts, block):
    rows = jnp.concatenate([p[:, 256 * i : 256 * i + 256] for p in parts for i in range(2)], axis=0)
    hi = rows.astype(BF16)
    rest = rows - hi.astype(F32)
    mid = rest.astype(BF16)
    low = (rest - mid.astype(F32)).astype(BF16)
    sums = jnp.dot(jnp.concatenate([hi, mid, low], axis=0), block, preferred_element_type=F32)
    total = sums[:32] + sums[32:64] + sums[64:]
    out = []
    for i in range(len(parts)):
        tiles = [total[16 * i + 8 * j : 16 * i + 8 * j + 8] for j in range(2)]
        tiles = [jnp.broadcast_to(jnp.sum(t, axis=0, keepdims=True), (8, 256)) for t in tiles]
        out.append(jnp.concatenate(tiles, axis=1))
    return out


def norm_factors(sums, load, block, joined, gain, shift):
    m0, m1 = group_sums(sums, block)
    m0, m1 = m0 * (1.0 / 2048), m1 * (1.0 / 2048)
    both = (m0 + m1) * 0.5
    c0, c1 = jnp.where(joined, both, m0), jnp.where(joined, both, m1)
    low, high = jnp.zeros((8, C), F32), jnp.zeros((8, C), F32)
    for r in range(16):
        x0, x1 = load(r)
        x0, x1 = x0 - c0, x1 - c1
        low, high = low + x0 * x0, high + x1 * x1
        yield
    v0, v1 = group_sums([low, high], block)
    v0, v1 = v0 * (1.0 / 2048), v1 * (1.0 / 2048)
    both = (v0 + v1) * 0.5
    v0, v1 = jnp.where(joined, both, v0), jnp.where(joined, both, v1)
    s0 = lax.rsqrt(v0 + EPS) * gain * 0.5
    s1 = lax.rsqrt(v1 + EPS) * gain * 0.5
    return s0, s1, shift * 0.5 - c0 * s0, shift * 0.5 - c1 * s1


def silu_half(half):
    return half + half * jnp.tanh(half)


def pair(top, bottom):
    return jnp.concatenate([top, bottom], axis=0).astype(BF16)


def loader(ref):
    def load(r):
        return ref[16 * r : 16 * r + 8, :], ref[16 * r + 8 : 16 * r + 16, :]

    return load


def order_slot(pick, slot):
    low, high = jnp.zeros((8, C), F32), jnp.zeros((8, C), F32)
    for i in range(8):
        top, bottom = pick(16 * i).astype(F32), pick(128 + 16 * i).astype(F32)
        for j in range(2):
            x0, x1 = top[8 * j : 8 * j + 8], bottom[8 * j : 8 * j + 8]
            r = 2 * i + j
            slot[16 * r : 16 * r + 8, :], slot[16 * r + 8 : 16 * r + 16, :] = x0, x1
            low, high = low + x0, high + x1
        yield
    return low, high


def norm_first(pick, slot, block, joined, gain, shift, pad):
    sums = yield from order_slot(pick, slot)
    load = loader(slot)
    s0, s1, t0, t1 = yield from norm_factors(sums, load, block, joined, gain, shift)
    zero = jnp.zeros((8, C), F32)
    col = iota((8, C), 0)
    for r in range(16):
        x0, x1 = load(r)
        sides = []
        for y in (silu_half(x0 * s0 + t0), silu_half(x1 * s1 + t1)):
            left = jnp.where(col >= 1, pltpu.roll(y, 1, 0), 0.0)
            right = jnp.where(col <= 6, pltpu.roll(y, 7, 0), 0.0)
            sides.append((left, y, right))
        for b in range(3):
            pad[b, 16 * (r + 1) : 16 * (r + 2), :] = pair(sides[0][b], sides[1][b])
            if r == 0:
                pad[b, 16 * 17 : 16 * 18, :] = pair(jnp.where(joined, sides[1][b], 0.0), zero)
            if r == 15:
                pad[b, 0:16, :] = pair(zero, jnp.where(joined, sides[0][b], 0.0))
        yield


def conv(pad, w, res):
    lhs = jnp.concatenate(
        [pad[b + 1, 16 * (a + 1) : 16 * (a + 1) + 256, :] for a, b in TAPS], axis=1
    )
    res[...] = jnp.dot(lhs, w[...], preferred_element_type=F32)


def finish(slot, res, bias, block, joined, gain, shift, act, lw3, lat_bias, select, out):
    own, added = loader(slot), loader(res)
    low, high = jnp.zeros((8, C), F32), jnp.zeros((8, C), F32)
    for r in range(16):
        (x0, x1), (d0, d1) = own(r), added(r)
        x0, x1 = x0 + d0 + bias, x1 + d1 + bias
        res[16 * r : 16 * r + 8, :], res[16 * r + 8 : 16 * r + 16, :] = x0, x1
        low, high = low + x0, high + x1
        yield
    s0, s1, t0, t1 = yield from norm_factors([low, high], added, block, joined, gain, shift)
    for r in range(16):
        x0, x1 = added(r)
        act[16 * r : 16 * r + 16, :] = pair(silu_half(x0 * s0 + t0), silu_half(x1 * s1 + t1))
        yield
    yield from latent_patches(act, lw3, lat_bias, joined, select, out)


def latent_patches(act, lw3, lat_bias, joined, select, out):
    terms = jnp.dot(act[...], lw3[...], preferred_element_type=F32)
    yield
    joined = joined[:, :128]
    zero = jnp.zeros((8, 128), F32)

    def part(a, r, h):
        return terms[16 * r + 8 * h : 16 * r + 8 * h + 8, 128 * (a + 1) : 128 * (a + 2)]

    col = iota((8, 128), 0)
    lane = iota((8, 128), 1)
    rows = []
    for r in range(16):
        for h in range(2):
            i = r % 2
            above = part(-1, r - 1, h) if r > 0 else (jnp.where(joined, part(-1, 15, 0), 0.0) if h == 1 else zero)
            below = part(1, r + 1, h) if r < 15 else (jnp.where(joined, part(1, 0, 1), 0.0) if h == 0 else zero)
            v = above + part(0, r, h) + below
            left = jnp.where(col >= 1, pltpu.roll(v, 1, 0), 0.0)
            right = jnp.where(col <= 6, pltpu.roll(v, 7, 0), 0.0)
            if i == 0:
                lat = left + pltpu.roll(v, 96, 1) + pltpu.roll(right, 64, 1)
            else:
                lat = pltpu.roll(left, 32, 1) + v + pltpu.roll(right, 96, 1)
            lat = (lat + lat_bias - LATENT_SHIFT) * LATENT_SCALE
            rows.append(jnp.where((lane // 16) == (2 * i + col % 2), lat, 0.0))
        if r % 2:
            yield
    cells = jnp.concatenate(rows, axis=0).astype(BF16)
    out[...] = jnp.dot(select, cells, preferred_element_type=F32).astype(BF16)


def tap_columns(lwt, lw3):
    zero = jnp.zeros((16, C), BF16)
    for a in range(3):
        taps = [lwt[16 * (3 * a + b) : 16 * (3 * a + b) + 16, :] for b in range(3)]
        rows = jnp.concatenate([taps[0], taps[0], taps[1], taps[1], taps[2], taps[2], zero, zero], axis=0)
        lw3[:, 128 * a : 128 * a + 128] = rows.T


def masks():
    block = jnp.where(iota((256, 256), 0) // 16 == iota((256, 256), 1) // 16, 1.0, 0.0).astype(BF16)
    t, m = iota((64, 256), 0), iota((64, 256), 1)
    same = (m // 32 == (t // 4) % 8) & ((m // 8) % 2 == t // 32) & ((m % 8) // 2 == t % 4)
    return block, jnp.where(same, 1.0, 0.0).astype(BF16)


DP_ORDER = (0, 1, 2, 6, 3, 7, 4, 5)


def exchange(pairs, start_now):
    for condition, copy, ready in pairs:

        @pl.when(condition)
        def _(copy=copy, ready=ready):
            if not start_now:
                pl.semaphore_wait(ready, 1)
            copy.start()


def kernel(
    kind_hbm, feat_hbm, bg_hbm, bs_hbm, w_hbm, bb_hbm, fg_hbm, fs_hbm, lw_hbm, lb_hbm, ew_hbm, eb_hbm,
    patch_out, embed_out,
    kind, feat, bg, bs, w, bb, fg, fs, lw, lb, ew, eb,
    slots, pad, res, act, lw3, lanes, mine, rowsum, xcounts, zsums, shard, shards, sent, got,
    in_sem, x_send, x_recv, z_send, z_recv, d_send, d_recv, p_send, p_recv, x_ready, z_ready, d_ready,
):
    seat, row = lax.axis_index("seq"), lax.axis_index("dp")
    z, x = seat // N_X, lax.rem(seat, N_X)
    rank = sum(jnp.where(row == DP_ORDER[i], i, 0) for i in range(N_DP))

    def at_x(i):
        return {"seq": z * N_X + i}

    def at_z(i):
        return {"seq": i * N_X + x}

    fetches = [
        pltpu.make_async_copy(source, target, in_sem.at[i])
        for i, (source, target) in enumerate(
            [
                (kind_hbm, kind), (feat_hbm.at[0], feat), (w_hbm, w), (lw_hbm, lw), (bg_hbm, bg), (bs_hbm, bs),
                (bb_hbm, bb), (fg_hbm, fg), (fs_hbm, fs), (lb_hbm, lb), (ew_hbm, ew), (eb_hbm, eb),
            ]
        )
    ]
    for fetch in fetches:
        fetch.start()
    zsums[...] = jnp.zeros((N_Z, 1, 128), I32)
    got[...] = jnp.zeros((2, 64, 128), BF16)
    lanes[...] = jnp.zeros((8, 128), F32)

    barrier = pltpu.get_barrier_semaphore()

    def greet(target):
        pl.semaphore_signal(barrier, inc=1, device_id=target, device_id_type=MESH)

    for i in range(1, N_X):
        pl.when(i > x)(functools.partial(greet, at_x(i)))
    for i in range(1, N_Z):
        pl.when(i > z)(functools.partial(greet, at_z(i)))
    for i in range(1, N_DP):
        pl.when(i > rank)(functools.partial(greet, {"dp": DP_ORDER[i]}))
    pl.when((x == 0) & (z > 0))(functools.partial(greet, {"seq": seat - 1}))

    block, select = masks()
    for fetch in fetches[:2] + fetches[3:]:
        fetch.wait()
    live = [(kind[0, i] > 0).astype(I32) for i in range(3)]
    n = live[0] + live[1] + live[2]
    kinds = [
        jnp.where(n == 3, kind[0, 2], jnp.where(n == 2, kind[0, 1], kind[0, 0])),
        jnp.where(n == 2, kind[0, 0], kind[0, 1]),
        jnp.where(n == 3, kind[0, 0], kind[0, 2]),
    ]
    joined = [jnp.full((8, C), kinds[t], I32) == 2 for t in range(3)]
    mine[...] = jnp.full((1, 128), n, I32)
    xcounts[pl.ds(x, 1)] = jnp.full((1, 1, 128), n, I32)
    shard[0:64, :] = ew[...]
    bias_row = jnp.broadcast_to(eb[...].reshape(1, 144).astype(F32), (16, 144))
    shard[64:80, :] = jnp.where(iota((16, 144), 0) == 0, bias_row, 0.0).astype(BF16)
    shards[pl.ds(row, 1)] = shard[...].reshape(1, 80, 144)
    lanes[0:1, 0:16] = lb[...]
    lat_bias = lanes[...]
    for step in (16, 32, 64):
        lat_bias = lat_bias + pltpu.roll(lat_bias, step, 1)
    lat_bias = lat_bias[0:1]

    number = jnp.full((16, C), n, I32)

    def cells(k, i):
        return feat[256 * k + i : 256 * k + i + 16, :]

    def pick(t):
        def rows(i):
            if t == 0:
                return jnp.where(number == 3, cells(2, i), jnp.where(number == 2, cells(1, i), cells(0, i)))
            if t == 1:
                return jnp.where(number == 2, cells(0, i), cells(1, i))
            return jnp.where(number == 3, cells(0, i), cells(2, i))

        return rows

    def spread(vector):
        return jnp.broadcast_to(vector[...], (8, C))

    def first_norm(t):
        return norm_first(pick(t), slots.at[t], block, joined[t], spread(bg), spread(bs), pad.at[t])

    def convolve(t):
        conv(pad.at[t], w, res.at[t])

    def last(t):
        return finish(
            slots.at[t], res.at[t], spread(bb), block, joined[t], spread(fg), spread(fs), act.at[t],
            lw3, lat_bias, select, sent.at[t],
        )

    def copy_to(source, target, send_sem, recv_sem, device):
        return pltpu.make_async_remote_copy(
            src_ref=source, dst_ref=target, send_sem=send_sem, recv_sem=recv_sem,
            device_id=device, device_id_type=MESH,
        )

    x_copies = [copy_to(mine, xcounts.at[x], x_send.at[i], x_recv.at[x], at_x(i)) for i in range(N_X)]
    x_arrivals = [copy_to(mine, xcounts.at[i], x_send.at[i], x_recv.at[i], at_x(i)) for i in range(N_X)]
    z_copies = [copy_to(rowsum, zsums.at[z], z_send.at[i], z_recv.at[z], at_z(i)) for i in range(N_Z)]
    z_arrivals = [copy_to(rowsum, zsums.at[i], z_send.at[i], z_recv.at[i], at_z(i)) for i in range(N_Z)]
    d_peers = [{"dp": DP_ORDER[i]} for i in range(N_DP)]
    d_copies = [copy_to(shard, shards.at[row], d_send.at[i], d_recv.at[rank], d_peers[i]) for i in range(N_DP)]
    d_arrivals = [
        copy_to(shard, shards.at[DP_ORDER[i]], d_send.at[i], d_recv.at[i], d_peers[i]) for i in range(N_DP)
    ]
    p_copies = [
        copy_to(sent.at[t], got.at[t], p_send.at[t], p_recv.at[t], {"seq": lax.rem(seat + 1, N_Z * N_X)})
        for t in range(2)
    ]

    def send_patch(t):
        pl.when(seat < N_Z * N_X - 1)(p_copies[t].start)

    earlier = x + z + rank + ((x == N_X - 1) & (z < N_Z - 1)).astype(I32)

    @pl.when(earlier > 0)
    def _():
        pl.semaphore_wait(barrier, earlier)


    def ready(sem, target):
        pl.semaphore_signal(sem, inc=1, device_id=target, device_id_type=MESH)

    for i in range(N_X - 1):
        pl.when(i < x)(functools.partial(ready, x_ready.at[x], at_x(i)))
    for i in range(N_Z - 1):
        pl.when(i < z)(functools.partial(ready, z_ready.at[z], at_z(i)))
    for i in range(N_DP - 1):
        pl.when(i < rank)(functools.partial(ready, d_ready.at[rank], d_peers[i]))
    exchange([(i < x, x_copies[i], None) for i in range(N_X - 1)], True)
    exchange([(i < rank, d_copies[i], None) for i in range(N_DP - 1)], True)

    tap_columns(lw, lw3)
    drain((first_norm(0), 42), (first_norm(1), 42))
    fetches[2].wait()
    convolve(0)
    drain((last(0), 60))
    exchange([(i > x, x_copies[i], x_ready.at[i]) for i in range(1, N_X)], False)
    send_patch(0)

    convolve(1)
    exchange([(i > rank, d_copies[i], d_ready.at[i]) for i in range(1, N_DP)], False)
    for i in range(N_X):
        pl.when(i != x)(x_arrivals[i].wait_recv)
    rowsum[...] = jnp.sum(xcounts[...], axis=0)
    exchange([((i > z) & (i < z + 4), z_copies[i], z_ready.at[i]) for i in range(1, N_Z)], False)
    drain((last(1), 60))
    send_patch(1)
    exchange([(i >= z + 4, z_copies[i], z_ready.at[i]) for i in range(4, N_Z)], False)

    drain((first_norm(2), 42))
    convolve(2)
    drain((last(2), 60))
    for i in range(N_DP):
        pl.when(i != rank)(d_arrivals[i].wait_recv)
    for i in range(N_DP):
        embed_out[:, 144 * i : 144 * i + 144] = shards[i]
    for i in range(N_Z - 1):
        pl.when(i < z)(z_arrivals[i].wait_recv)
    before = jnp.where(iota((N_X, 1, 128), 0) < x, xcounts[...], 0)
    carry_in = jnp.sum(zsums[...], axis=0) + jnp.sum(before, axis=0) - 2 * seat
    for i in range(N_X):
        pl.when(i != x)(x_arrivals[i].wait_send)
    for i in range(N_DP):
        pl.when(i != rank)(d_arrivals[i].wait_send)
    for i in range(1, N_Z):
        pl.when(i > z)(z_arrivals[i].wait_send)
    for t in range(2):
        pl.when(seat < N_Z * N_X - 1)(p_copies[t].wait_send)
    for t in range(2):
        pl.when(seat > 0)(p_copies[t].wait_recv)

    carry_in = jnp.broadcast_to(carry_in, (64, 128))
    number = jnp.full((64, 128), n, I32)
    own = [sent[t].astype(F32) for t in range(3)]
    came = [got[t].astype(F32) for t in range(2)]
    newest = jnp.where(number == 3, own[2], jnp.where(number == 2, own[1], own[0]))
    second = jnp.where(number == 3, own[1], own[0])
    out0 = jnp.where(carry_in == 0, newest, jnp.where(carry_in == 1, came[0], came[1]))
    out1 = jnp.where(carry_in == 0, second, jnp.where(carry_in == 1, newest, came[0]))
    patches = jnp.concatenate([out0, out1], axis=0)
    patches = jnp.where(iota((128, 128), 1) == 64, 1.0, patches).astype(BF16)
    patch_out[...] = patches[:, :80]


def local(feat, kind, bg, bs, w, bb, fg, fs, lw, lb, ew, eb):
    hbm = pl.BlockSpec(memory_space=pl.ANY)
    vmem = pl.BlockSpec(memory_space=pltpu.VMEM)
    dma, regular, V = pltpu.SemaphoreType.DMA, pltpu.SemaphoreType.REGULAR, pltpu.VMEM
    vec = V((1, C), F32)
    patches, embed = pl.pallas_call(
        kernel,
        out_shape=(jax.ShapeDtypeStruct((128, 80), BF16), jax.ShapeDtypeStruct((80, HID), BF16)),
        in_specs=[hbm] * 12,
        out_specs=(vmem, vmem),
        scratch_shapes=[
            pltpu.SMEM((1, 3), I32), V((768, C), BF16), vec, vec, V((9 * C, C), BF16), vec, vec, vec,
            V((144, C), BF16), V((1, 16), F32), V((64, 144), BF16), V((144,), BF16),
            V((3, 256, C), F32), V((3, 3, 288, C), BF16), V((3, 256, C), F32), V((3, 256, C), BF16),
            V((C, 384), BF16), V((8, 128), F32), V((1, 128), I32), V((1, 128), I32),
            V((N_X, 1, 128), I32), V((N_Z, 1, 128), I32), V((80, 144), BF16), V((N_DP, 80, 144), BF16),
            V((3, 64, 128), BF16), V((2, 64, 128), BF16),
            dma((12,)), dma((N_X,)), dma((N_X,)), dma((N_Z,)), dma((N_Z,)), dma((N_DP,)), dma((N_DP,)),
            dma((2,)), dma((2,)), regular((N_X,)), regular((N_Z,)), regular((N_DP,)),
        ],
        compiler_params=pltpu.CompilerParams(
            collective_id=0, has_side_effects=True, vmem_limit_bytes=60 << 20
        ),
    )(
        kind, feat, bg.reshape(1, C), bs.reshape(1, C), w, bb.reshape(1, C), fg.reshape(1, C),
        fs.reshape(1, C), lw.T, lb.reshape(1, 16), ew, eb,
    )
    return jnp.dot(patches, embed, preferred_element_type=F32).astype(BF16)[None]


def solution(mesh):
    shared = P()
    return jax.shard_map(
        local,
        mesh=mesh,
        in_specs=(P("dp", "seq", None), P("dp", "seq")) + (shared,) * 8 + (P(None, "dp"), P("dp")),
        out_specs=P("dp", "seq", None),
        check_vma=False,
    )
```

```python
import functools
import jax
import jax.numpy as jnp
from jax import lax
from jax.experimental import pallas as pl
from jax.experimental.pallas import tpu as pltpu
from jax.sharding import PartitionSpec as P

F32, BF16, I32 = jnp.float32, jnp.bfloat16, jnp.int32
MESH = pl.DeviceIdType.MESH
LATENT_SHIFT = 0.0609
LATENT_SCALE = 1.5305
EPS = 1e-06
C = 512
HID = 1152
TAPS = [(a, b) for a in (-1, 0, 1) for b in (-1, 0, 1)]
N_DP, N_Z, N_X = 8, 8, 4


def iota(shape, dim):
    return lax.broadcasted_iota(I32, shape, dim)


def drain(*streams):
    live = [[stream, steps, 0] for stream, steps in streams]
    while live:
        entry = min(live, key=lambda e: (e[2] + 1) / e[1])
        entry[2] += 1
        try:
            next(entry[0])
        except StopIteration:
            live.remove(entry)


def group_sums(parts, block):
    rows = jnp.concatenate([p[:, 256 * i : 256 * i + 256] for p in parts for i in range(2)], axis=0)
    hi = rows.astype(BF16)
    rest = rows - hi.astype(F32)
    mid = rest.astype(BF16)
    low = (rest - mid.astype(F32)).astype(BF16)
    sums = jnp.dot(jnp.concatenate([hi, mid, low], axis=0), block, preferred_element_type=F32)
    total = sums[:32] + sums[32:64] + sums[64:]
    out = []
    for i in range(len(parts)):
        tiles = [total[16 * i + 8 * j : 16 * i + 8 * j + 8] for j in range(2)]
        tiles = [jnp.broadcast_to(jnp.sum(t, axis=0, keepdims=True), (8, 256)) for t in tiles]
        out.append(jnp.concatenate(tiles, axis=1))
    return out


def norm_factors(sums, load, block, joined, gain, shift):
    m0, m1 = group_sums(sums, block)
    m0, m1 = m0 * (1.0 / 2048), m1 * (1.0 / 2048)
    both = (m0 + m1) * 0.5
    c0, c1 = jnp.where(joined, both, m0), jnp.where(joined, both, m1)
    low, high = jnp.zeros((8, C), F32), jnp.zeros((8, C), F32)
    for r in range(16):
        x0, x1 = load(r)
        x0, x1 = x0 - c0, x1 - c1
        low, high = low + x0 * x0, high + x1 * x1
        yield
    v0, v1 = group_sums([low, high], block)
    v0, v1 = v0 * (1.0 / 2048), v1 * (1.0 / 2048)
    both = (v0 + v1) * 0.5
    v0, v1 = jnp.where(joined, both, v0), jnp.where(joined, both, v1)
    s0 = lax.rsqrt(v0 + EPS) * gain * 0.5
    s1 = lax.rsqrt(v1 + EPS) * gain * 0.5
    return s0, s1, shift * 0.5 - c0 * s0, shift * 0.5 - c1 * s1


def silu_half(half):
    return half + half * jnp.tanh(half)


def pair(top, bottom):
    return jnp.concatenate([top, bottom], axis=0).astype(BF16)


def loader(ref):
    def load(r):
        return ref[16 * r : 16 * r + 8, :], ref[16 * r + 8 : 16 * r + 16, :]

    return load


def order_slot(pick, slot):
    low, high = jnp.zeros((8, C), F32), jnp.zeros((8, C), F32)
    for i in range(8):
        top, bottom = pick(16 * i).astype(F32), pick(128 + 16 * i).astype(F32)
        for j in range(2):
            x0, x1 = top[8 * j : 8 * j + 8], bottom[8 * j : 8 * j + 8]
            r = 2 * i + j
            slot[16 * r : 16 * r + 8, :], slot[16 * r + 8 : 16 * r + 16, :] = x0, x1
            low, high = low + x0, high + x1
        yield
    return low, high


def norm_first(pick, slot, block, joined, gain, shift, pad):
    sums = yield from order_slot(pick, slot)
    load = loader(slot)
    s0, s1, t0, t1 = yield from norm_factors(sums, load, block, joined, gain, shift)
    zero = jnp.zeros((8, C), F32)
    col = iota((8, C), 0)
    for r in range(16):
        x0, x1 = load(r)
        sides = []
        for y in (silu_half(x0 * s0 + t0), silu_half(x1 * s1 + t1)):
            left = jnp.where(col >= 1, pltpu.roll(y, 1, 0), 0.0)
            right = jnp.where(col <= 6, pltpu.roll(y, 7, 0), 0.0)
            sides.append((left, y, right))
        for b in range(3):
            pad[b, 16 * (r + 1) : 16 * (r + 2), :] = pair(sides[0][b], sides[1][b])
            if r == 0:
                pad[b, 16 * 17 : 16 * 18, :] = pair(jnp.where(joined, sides[1][b], 0.0), zero)
            if r == 15:
                pad[b, 0:16, :] = pair(zero, jnp.where(joined, sides[0][b], 0.0))
        yield


def conv(pad, w, res):
    lhs = jnp.concatenate(
        [pad[b + 1, 16 * (a + 1) : 16 * (a + 1) + 256, :] for a, b in TAPS], axis=1
    )
    res[...] = jnp.dot(lhs, w[...], preferred_element_type=F32)


def finish(slot, res, bias, block, joined, gain, shift, act, lw3, lat_bias, select, out):
    own, added = loader(slot), loader(res)
    low, high = jnp.zeros((8, C), F32), jnp.zeros((8, C), F32)
    for r in range(16):
        (x0, x1), (d0, d1) = own(r), added(r)
        x0, x1 = x0 + d0 + bias, x1 + d1 + bias
        res[16 * r : 16 * r + 8, :], res[16 * r + 8 : 16 * r + 16, :] = x0, x1
        low, high = low + x0, high + x1
        yield
    s0, s1, t0, t1 = yield from norm_factors([low, high], added, block, joined, gain, shift)
    for r in range(16):
        x0, x1 = added(r)
        act[16 * r : 16 * r + 16, :] = pair(silu_half(x0 * s0 + t0), silu_half(x1 * s1 + t1))
        yield
    yield from latent_patches(act, lw3, lat_bias, joined, select, out)


def latent_patches(act, lw3, lat_bias, joined, select, out):
    terms = jnp.dot(act[...], lw3[...], preferred_element_type=F32)
    yield
    joined = joined[:, :128]
    zero = jnp.zeros((8, 128), F32)

    def part(a, r, h):
        return terms[16 * r + 8 * h : 16 * r + 8 * h + 8, 128 * (a + 1) : 128 * (a + 2)]

    col = iota((8, 128), 0)
    lane = iota((8, 128), 1)
    rows = []
    for r in range(16):
        for h in range(2):
            i = r % 2
            above = part(-1, r - 1, h) if r > 0 else (jnp.where(joined, part(-1, 15, 0), 0.0) if h == 1 else zero)
            below = part(1, r + 1, h) if r < 15 else (jnp.where(joined, part(1, 0, 1), 0.0) if h == 0 else zero)
            v = above + part(0, r, h) + below
            left = jnp.where(col >= 1, pltpu.roll(v, 1, 0), 0.0)
            right = jnp.where(col <= 6, pltpu.roll(v, 7, 0), 0.0)
            if i == 0:
                lat = left + pltpu.roll(v, 96, 1) + pltpu.roll(right, 64, 1)
            else:
                lat = pltpu.roll(left, 32, 1) + v + pltpu.roll(right, 96, 1)
            lat = (lat + lat_bias - LATENT_SHIFT) * LATENT_SCALE
            rows.append(jnp.where((lane // 16) == (2 * i + col % 2), lat, 0.0))
        if r % 2:
            yield
    cells = jnp.concatenate(rows, axis=0).astype(BF16)
    out[...] = jnp.dot(select, cells, preferred_element_type=F32).astype(BF16)


def tap_columns(lwt, lw3):
    zero = jnp.zeros((16, C), BF16)
    for a in range(3):
        taps = [lwt[16 * (3 * a + b) : 16 * (3 * a + b) + 16, :] for b in range(3)]
        rows = jnp.concatenate([taps[0], taps[0], taps[1], taps[1], taps[2], taps[2], zero, zero], axis=0)
        lw3[:, 128 * a : 128 * a + 128] = rows.T


def masks():
    block = jnp.where(iota((256, 256), 0) // 16 == iota((256, 256), 1) // 16, 1.0, 0.0).astype(BF16)
    t, m = iota((64, 256), 0), iota((64, 256), 1)
    same = (m // 32 == (t // 4) % 8) & ((m // 8) % 2 == t // 32) & ((m % 8) // 2 == t % 4)
    return block, jnp.where(same, 1.0, 0.0).astype(BF16)


DP_ORDER = (0, 1, 2, 6, 3, 7, 4, 5)


def exchange(pairs, start_now):
    for condition, copy, ready in pairs:

        @pl.when(condition)
        def _(copy=copy, ready=ready):
            if not start_now:
                pl.semaphore_wait(ready, 1)
            copy.start()


def kernel(
    kind_hbm, feat_hbm, bg_hbm, bs_hbm, w_hbm, bb_hbm, fg_hbm, fs_hbm, lw_hbm, lb_hbm, ew_hbm, eb_hbm,
    patch_out, embed_out,
    kind, feat, bg, bs, w, bb, fg, fs, lw, lb, ew, eb,
    slots, pad, res, act, lw3, lanes, mine, rowsum, xcounts, zsums, shard, shards, sent, got,
    in_sem, x_send, x_recv, z_send, z_recv, d_send, d_recv, p_send, p_recv, x_ready, z_ready, d_ready,
):
    seat, row = lax.axis_index("seq"), lax.axis_index("dp")
    z, x = seat // N_X, lax.rem(seat, N_X)
    rank = sum(jnp.where(row == DP_ORDER[i], i, 0) for i in range(N_DP))

    def at_x(i):
        return {"seq": z * N_X + i}

    def at_z(i):
        return {"seq": i * N_X + x}

    fetches = [
        pltpu.make_async_copy(source, target, in_sem.at[i])
        for i, (source, target) in enumerate(
            [
                (kind_hbm, kind), (feat_hbm.at[0], feat), (w_hbm, w), (lw_hbm, lw), (bg_hbm, bg), (bs_hbm, bs),
                (bb_hbm, bb), (fg_hbm, fg), (fs_hbm, fs), (lb_hbm, lb), (ew_hbm, ew), (eb_hbm, eb),
            ]
        )
    ]
    for fetch in fetches:
        fetch.start()
    zsums[...] = jnp.zeros((N_Z, 1, 128), I32)
    got[...] = jnp.zeros((2, 64, 128), BF16)
    lanes[...] = jnp.zeros((8, 128), F32)

    barrier = pltpu.get_barrier_semaphore()

    def greet(target):
        pl.semaphore_signal(barrier, inc=1, device_id=target, device_id_type=MESH)

    for i in range(1, N_X):
        pl.when(i > x)(functools.partial(greet, at_x(i)))
    for i in range(1, N_Z):
        pl.when(i > z)(functools.partial(greet, at_z(i)))
    for i in range(1, N_DP):
        pl.when(i > rank)(functools.partial(greet, {"dp": DP_ORDER[i]}))
    pl.when((x == 0) & (z > 0))(functools.partial(greet, {"seq": seat - 1}))

    block, select = masks()
    for fetch in fetches[:2] + fetches[3:]:
        fetch.wait()
    live = [(kind[0, i] > 0).astype(I32) for i in range(3)]
    n = live[0] + live[1] + live[2]
    kinds = [
        jnp.where(n == 3, kind[0, 2], jnp.where(n == 2, kind[0, 1], kind[0, 0])),
        jnp.where(n == 2, kind[0, 0], kind[0, 1]),
        jnp.where(n == 3, kind[0, 0], kind[0, 2]),
    ]
    joined = [jnp.full((8, C), kinds[t], I32) == 2 for t in range(3)]
    mine[...] = jnp.full((1, 128), n, I32)
    xcounts[pl.ds(x, 1)] = jnp.full((1, 1, 128), n, I32)
    shard[0:64, :] = ew[...]
    bias_row = jnp.broadcast_to(eb[...].reshape(1, 144).astype(F32), (16, 144))
    shard[64:80, :] = jnp.where(iota((16, 144), 0) == 0, bias_row, 0.0).astype(BF16)
    shards[pl.ds(row, 1)] = shard[...].reshape(1, 80, 144)
    lanes[0:1, 0:16] = lb[...]
    lat_bias = lanes[...]
    for step in (16, 32, 64):
        lat_bias = lat_bias + pltpu.roll(lat_bias, step, 1)
    lat_bias = lat_bias[0:1]

    number = jnp.full((16, C), n, I32)

    def cells(k, i):
        return feat[256 * k + i : 256 * k + i + 16, :]

    def pick(t):
        def rows(i):
            if t == 0:
                return jnp.where(number == 3, cells(2, i), jnp.where(number == 2, cells(1, i), cells(0, i)))
            if t == 1:
                return jnp.where(number == 2, cells(0, i), cells(1, i))
            return jnp.where(number == 3, cells(0, i), cells(2, i))

        return rows

    def spread(vector):
        return jnp.broadcast_to(vector[...], (8, C))

    def first_norm(t):
        return norm_first(pick(t), slots.at[t], block, joined[t], spread(bg), spread(bs), pad.at[t])

    def convolve(t):
        conv(pad.at[t], w, res.at[t])

    def last(t):
        return finish(
            slots.at[t], res.at[t], spread(bb), block, joined[t], spread(fg), spread(fs), act.at[t],
            lw3, lat_bias, select, sent.at[t],
        )

    def copy_to(source, target, send_sem, recv_sem, device):
        return pltpu.make_async_remote_copy(
            src_ref=source, dst_ref=target, send_sem=send_sem, recv_sem=recv_sem,
            device_id=device, device_id_type=MESH,
        )

    x_copies = [copy_to(mine, xcounts.at[x], x_send.at[i], x_recv.at[x], at_x(i)) for i in range(N_X)]
    x_arrivals = [copy_to(mine, xcounts.at[i], x_send.at[i], x_recv.at[i], at_x(i)) for i in range(N_X)]
    z_copies = [copy_to(rowsum, zsums.at[z], z_send.at[i], z_recv.at[z], at_z(i)) for i in range(N_Z)]
    z_arrivals = [copy_to(rowsum, zsums.at[i], z_send.at[i], z_recv.at[i], at_z(i)) for i in range(N_Z)]
    d_peers = [{"dp": DP_ORDER[i]} for i in range(N_DP)]
    d_copies = [copy_to(shard, shards.at[row], d_send.at[i], d_recv.at[rank], d_peers[i]) for i in range(N_DP)]
    d_arrivals = [
        copy_to(shard, shards.at[DP_ORDER[i]], d_send.at[i], d_recv.at[i], d_peers[i]) for i in range(N_DP)
    ]
    p_copies = [
        copy_to(sent.at[t], got.at[t], p_send.at[t], p_recv.at[t], {"seq": lax.rem(seat + 1, N_Z * N_X)})
        for t in range(2)
    ]

    def send_patch(t):
        pl.when(seat < N_Z * N_X - 1)(p_copies[t].start)

    earlier = x + z + rank + ((x == N_X - 1) & (z < N_Z - 1)).astype(I32)

    @pl.when(earlier > 0)
    def _():
        pl.semaphore_wait(barrier, earlier)


    def ready(sem, target):
        pl.semaphore_signal(sem, inc=1, device_id=target, device_id_type=MESH)

    for i in range(N_X - 1):
        pl.when(i < x)(functools.partial(ready, x_ready.at[x], at_x(i)))
    for i in range(N_Z - 1):
        pl.when(i < z)(functools.partial(ready, z_ready.at[z], at_z(i)))
    for i in range(N_DP - 1):
        pl.when(i < rank)(functools.partial(ready, d_ready.at[rank], d_peers[i]))
    exchange([(i < x, x_copies[i], None) for i in range(N_X - 1)], True)
    exchange([(i < rank, d_copies[i], None) for i in range(N_DP - 1)], True)

    tap_columns(lw, lw3)
    drain((first_norm(0), 42), (first_norm(1), 42))
    fetches[2].wait()
    convolve(0)
    drain((last(0), 60))
    exchange([(i > x, x_copies[i], x_ready.at[i]) for i in range(1, N_X)], False)
    send_patch(0)

    convolve(1)
    exchange([(i > rank, d_copies[i], d_ready.at[i]) for i in range(1, N_DP)], False)

    def row_sums():
        for i in range(N_X):
            pl.when(i != x)(x_arrivals[i].wait_recv)
        rowsum[...] = jnp.sum(xcounts[...], axis=0)
        exchange([((i > z) & (i < z + 4), z_copies[i], z_ready.at[i]) for i in range(1, N_Z)], False)

    pl.when(x < 2)(row_sums)
    drain((last(1), 60))
    send_patch(1)
    pl.when(x >= 2)(row_sums)
    exchange([(i >= z + 4, z_copies[i], z_ready.at[i]) for i in range(4, N_Z)], False)

    drain((first_norm(2), 42))
    convolve(2)
    drain((last(2), 60))
    for i in range(N_DP):
        pl.when(i != rank)(d_arrivals[i].wait_recv)
    for i in range(N_DP):
        embed_out[:, 144 * i : 144 * i + 144] = shards[i]
    for i in range(N_Z - 1):
        pl.when(i < z)(z_arrivals[i].wait_recv)
    before = jnp.where(iota((N_X, 1, 128), 0) < x, xcounts[...], 0)
    carry_in = jnp.sum(zsums[...], axis=0) + jnp.sum(before, axis=0) - 2 * seat
    for i in range(N_X):
        pl.when(i != x)(x_arrivals[i].wait_send)
    for i in range(N_DP):
        pl.when(i != rank)(d_arrivals[i].wait_send)
    for i in range(1, N_Z):
        pl.when(i > z)(z_arrivals[i].wait_send)
    for t in range(2):
        pl.when(seat < N_Z * N_X - 1)(p_copies[t].wait_send)
    for t in range(2):
        pl.when(seat > 0)(p_copies[t].wait_recv)

    carry_in = jnp.broadcast_to(carry_in, (64, 128))
    number = jnp.full((64, 128), n, I32)
    own = [sent[t].astype(F32) for t in range(3)]
    came = [got[t].astype(F32) for t in range(2)]
    newest = jnp.where(number == 3, own[2], jnp.where(number == 2, own[1], own[0]))
    second = jnp.where(number == 3, own[1], own[0])
    out0 = jnp.where(carry_in == 0, newest, jnp.where(carry_in == 1, came[0], came[1]))
    out1 = jnp.where(carry_in == 0, second, jnp.where(carry_in == 1, newest, came[0]))
    patches = jnp.concatenate([out0, out1], axis=0)
    patches = jnp.where(iota((128, 128), 1) == 64, 1.0, patches).astype(BF16)
    patch_out[...] = patches[:, :80]


def embed_patches(patches, embed, out):
    out[0] = jnp.dot(patches[...], embed[...], preferred_element_type=F32).astype(BF16)


def local(feat, kind, bg, bs, w, bb, fg, fs, lw, lb, ew, eb):
    hbm = pl.BlockSpec(memory_space=pl.ANY)
    vmem = pl.BlockSpec(memory_space=pltpu.VMEM)
    dma, regular, V = pltpu.SemaphoreType.DMA, pltpu.SemaphoreType.REGULAR, pltpu.VMEM
    vec = V((1, C), F32)
    patches, embed = pl.pallas_call(
        kernel,
        out_shape=(jax.ShapeDtypeStruct((128, 80), BF16), jax.ShapeDtypeStruct((80, HID), BF16)),
        in_specs=[hbm] * 12,
        out_specs=(vmem, vmem),
        scratch_shapes=[
            pltpu.SMEM((1, 3), I32), V((768, C), BF16), vec, vec, V((9 * C, C), BF16), vec, vec, vec,
            V((144, C), BF16), V((1, 16), F32), V((64, 144), BF16), V((144,), BF16),
            V((3, 256, C), F32), V((3, 3, 288, C), BF16), V((3, 256, C), F32), V((3, 256, C), BF16),
            V((C, 384), BF16), V((8, 128), F32), V((1, 128), I32), V((1, 128), I32),
            V((N_X, 1, 128), I32), V((N_Z, 1, 128), I32), V((80, 144), BF16), V((N_DP, 80, 144), BF16),
            V((3, 64, 128), BF16), V((2, 64, 128), BF16),
            dma((12,)), dma((N_X,)), dma((N_X,)), dma((N_Z,)), dma((N_Z,)), dma((N_DP,)), dma((N_DP,)),
            dma((2,)), dma((2,)), regular((N_X,)), regular((N_Z,)), regular((N_DP,)),
        ],
        compiler_params=pltpu.CompilerParams(
            collective_id=0, has_side_effects=True, vmem_limit_bytes=60 << 20
        ),
    )(
        kind, feat, bg.reshape(1, C), bs.reshape(1, C), w, bb.reshape(1, C), fg.reshape(1, C),
        fs.reshape(1, C), lw.T, lb.reshape(1, 16), ew, eb,
    )
    return pl.pallas_call(
        embed_patches,
        out_shape=jax.ShapeDtypeStruct((1, 128, HID), BF16),
        in_specs=[vmem, vmem],
        out_specs=vmem,
    )(patches, embed)


def solution(mesh):
    shared = P()
    return jax.shard_map(
        local,
        mesh=mesh,
        in_specs=(P("dp", "seq", None), P("dp", "seq")) + (shared,) * 8 + (P(None, "dp"), P("dp")),
        out_specs=P("dp", "seq", None),
        check_vma=False,
    )
```

```python
import functools
import jax
import jax.numpy as jnp
from jax import lax
from jax.experimental import pallas as pl
from jax.experimental.pallas import tpu as pltpu
from jax.sharding import PartitionSpec as P

F32, BF16, I32 = jnp.float32, jnp.bfloat16, jnp.int32
MESH = pl.DeviceIdType.MESH
LATENT_SHIFT = 0.0609
LATENT_SCALE = 1.5305
EPS = 1e-06
C = 512
HID = 1152
TAPS = [(a, b) for a in (-1, 0, 1) for b in (-1, 0, 1)]
N_DP, N_Z, N_X = 8, 8, 4


def iota(shape, dim):
    return lax.broadcasted_iota(I32, shape, dim)


def drain(*streams):
    live = [[stream, steps, 0] for stream, steps in streams]
    while live:
        entry = min(live, key=lambda e: (e[2] + 1) / e[1])
        entry[2] += 1
        try:
            next(entry[0])
        except StopIteration:
            live.remove(entry)


def group_sums(parts, block):
    rows = jnp.concatenate([p[:, 256 * i : 256 * i + 256] for p in parts for i in range(2)], axis=0)
    hi = rows.astype(BF16)
    rest = rows - hi.astype(F32)
    mid = rest.astype(BF16)
    low = (rest - mid.astype(F32)).astype(BF16)
    sums = jnp.dot(jnp.concatenate([hi, mid, low], axis=0), block, preferred_element_type=F32)
    total = sums[:32] + sums[32:64] + sums[64:]
    out = []
    for i in range(len(parts)):
        tiles = [total[16 * i + 8 * j : 16 * i + 8 * j + 8] for j in range(2)]
        tiles = [jnp.broadcast_to(jnp.sum(t, axis=0, keepdims=True), (8, 256)) for t in tiles]
        out.append(jnp.concatenate(tiles, axis=1))
    return out


def norm_factors(sums, load, block, joined, gain, shift):
    m0, m1 = group_sums(sums, block)
    m0, m1 = m0 * (1.0 / 2048), m1 * (1.0 / 2048)
    both = (m0 + m1) * 0.5
    c0, c1 = jnp.where(joined, both, m0), jnp.where(joined, both, m1)
    low, high = jnp.zeros((8, C), F32), jnp.zeros((8, C), F32)
    for r in range(16):
        x0, x1 = load(r)
        x0, x1 = x0 - c0, x1 - c1
        low, high = low + x0 * x0, high + x1 * x1
        yield
    v0, v1 = group_sums([low, high], block)
    v0, v1 = v0 * (1.0 / 2048), v1 * (1.0 / 2048)
    both = (v0 + v1) * 0.5
    v0, v1 = jnp.where(joined, both, v0), jnp.where(joined, both, v1)
    s0 = lax.rsqrt(v0 + EPS) * gain * 0.5
    s1 = lax.rsqrt(v1 + EPS) * gain * 0.5
    return s0, s1, shift * 0.5 - c0 * s0, shift * 0.5 - c1 * s1


def silu_half(half):
    return half + half * jnp.tanh(half)


def pair(top, bottom):
    return jnp.concatenate([top, bottom], axis=0).astype(BF16)


def loader(ref):
    def load(r):
        return ref[16 * r : 16 * r + 8, :], ref[16 * r + 8 : 16 * r + 16, :]

    return load


def order_slot(pick, slot):
    low, high = jnp.zeros((8, C), F32), jnp.zeros((8, C), F32)
    for i in range(8):
        top, bottom = pick(16 * i).astype(F32), pick(128 + 16 * i).astype(F32)
        for j in range(2):
            x0, x1 = top[8 * j : 8 * j + 8], bottom[8 * j : 8 * j + 8]
            r = 2 * i + j
            slot[16 * r : 16 * r + 8, :], slot[16 * r + 8 : 16 * r + 16, :] = x0, x1
            low, high = low + x0, high + x1
        yield
    return low, high


def norm_first(pick, slot, block, joined, gain, shift, pad):
    sums = yield from order_slot(pick, slot)
    load = loader(slot)
    s0, s1, t0, t1 = yield from norm_factors(sums, load, block, joined, gain, shift)
    zero = jnp.zeros((8, C), F32)
    col = iota((8, C), 0)
    for r in range(16):
        x0, x1 = load(r)
        sides = []
        for y in (silu_half(x0 * s0 + t0), silu_half(x1 * s1 + t1)):
            left = jnp.where(col >= 1, pltpu.roll(y, 1, 0), 0.0)
            right = jnp.where(col <= 6, pltpu.roll(y, 7, 0), 0.0)
            sides.append((left, y, right))
        for b in range(3):
            pad[b, 16 * (r + 1) : 16 * (r + 2), :] = pair(sides[0][b], sides[1][b])
            if r == 0:
                pad[b, 16 * 17 : 16 * 18, :] = pair(jnp.where(joined, sides[1][b], 0.0), zero)
            if r == 15:
                pad[b, 0:16, :] = pair(zero, jnp.where(joined, sides[0][b], 0.0))
        yield


def conv(pad, w, res):
    lhs = jnp.concatenate(
        [pad[b + 1, 16 * (a + 1) : 16 * (a + 1) + 256, :] for a, b in TAPS], axis=1
    )
    res[...] = jnp.dot(lhs, w[...], preferred_element_type=F32)


def finish(slot, res, bias, block, joined, gain, shift, act, lw3, lat_bias, select, out):
    own, added = loader(slot), loader(res)
    low, high = jnp.zeros((8, C), F32), jnp.zeros((8, C), F32)
    for r in range(16):
        (x0, x1), (d0, d1) = own(r), added(r)
        x0, x1 = x0 + d0 + bias, x1 + d1 + bias
        res[16 * r : 16 * r + 8, :], res[16 * r + 8 : 16 * r + 16, :] = x0, x1
        low, high = low + x0, high + x1
        yield
    s0, s1, t0, t1 = yield from norm_factors([low, high], added, block, joined, gain, shift)
    for r in range(16):
        x0, x1 = added(r)
        act[16 * r : 16 * r + 16, :] = pair(silu_half(x0 * s0 + t0), silu_half(x1 * s1 + t1))
        yield
    yield from latent_patches(act, lw3, lat_bias, joined, select, out)


def latent_patches(act, lw3, lat_bias, joined, select, out):
    terms = jnp.dot(act[...], lw3[...], preferred_element_type=F32)
    yield
    joined = joined[:, :128]
    zero = jnp.zeros((8, 128), F32)

    def part(a, r, h):
        return terms[16 * r + 8 * h : 16 * r + 8 * h + 8, 128 * (a + 1) : 128 * (a + 2)]

    col = iota((8, 128), 0)
    lane = iota((8, 128), 1)
    rows = []
    for r in range(16):
        for h in range(2):
            i = r % 2
            above = part(-1, r - 1, h) if r > 0 else (jnp.where(joined, part(-1, 15, 0), 0.0) if h == 1 else zero)
            below = part(1, r + 1, h) if r < 15 else (jnp.where(joined, part(1, 0, 1), 0.0) if h == 0 else zero)
            v = above + part(0, r, h) + below
            left = jnp.where(col >= 1, pltpu.roll(v, 1, 0), 0.0)
            right = jnp.where(col <= 6, pltpu.roll(v, 7, 0), 0.0)
            if i == 0:
                lat = left + pltpu.roll(v, 96, 1) + pltpu.roll(right, 64, 1)
            else:
                lat = pltpu.roll(left, 32, 1) + v + pltpu.roll(right, 96, 1)
            lat = (lat + lat_bias - LATENT_SHIFT) * LATENT_SCALE
            rows.append(jnp.where((lane // 16) == (2 * i + col % 2), lat, 0.0))
        if r % 2:
            yield
    cells = jnp.concatenate(rows, axis=0).astype(BF16)
    out[...] = jnp.dot(select, cells, preferred_element_type=F32).astype(BF16)


def tap_columns(lwt, lw3):
    zero = jnp.zeros((16, C), BF16)
    for a in range(3):
        taps = [lwt[16 * (3 * a + b) : 16 * (3 * a + b) + 16, :] for b in range(3)]
        rows = jnp.concatenate([taps[0], taps[0], taps[1], taps[1], taps[2], taps[2], zero, zero], axis=0)
        lw3[:, 128 * a : 128 * a + 128] = rows.T


def masks():
    block = jnp.where(iota((256, 256), 0) // 16 == iota((256, 256), 1) // 16, 1.0, 0.0).astype(BF16)
    t, m = iota((64, 256), 0), iota((64, 256), 1)
    same = (m // 32 == (t // 4) % 8) & ((m // 8) % 2 == t // 32) & ((m % 8) // 2 == t % 4)
    return block, jnp.where(same, 1.0, 0.0).astype(BF16)


DP_ORDER = (0, 1, 2, 6, 3, 7, 4, 5)


def exchange(pairs, start_now):
    for condition, copy, ready in pairs:

        @pl.when(condition)
        def _(copy=copy, ready=ready):
            if not start_now:
                pl.semaphore_wait(ready, 1)
            copy.start()


def kernel(
    kind_hbm, feat_hbm, bg_hbm, bs_hbm, w_hbm, bb_hbm, fg_hbm, fs_hbm, lw_hbm, lb_hbm, ew_hbm, eb_hbm,
    patch_out, embed_out,
    kind, feat, bg, bs, w, bb, fg, fs, lw, lb, ew, eb,
    slots, pad, res, act, lw3, lanes, mine, rowsum, xcounts, zsums, shard, shards, sent, got,
    in_sem, x_send, x_recv, z_send, z_recv, d_send, d_recv, p_send, p_recv, x_ready, z_ready, d_ready,
):
    seat, row = lax.axis_index("seq"), lax.axis_index("dp")
    z, x = seat // N_X, lax.rem(seat, N_X)
    rank = sum(jnp.where(row == DP_ORDER[i], i, 0) for i in range(N_DP))

    def at_x(i):
        return {"seq": z * N_X + i}

    def at_z(i):
        return {"seq": i * N_X + x}

    fetches = [
        pltpu.make_async_copy(source, target, in_sem.at[i])
        for i, (source, target) in enumerate(
            [
                (kind_hbm, kind), (feat_hbm.at[0], feat), (w_hbm, w), (lw_hbm, lw), (bg_hbm, bg), (bs_hbm, bs),
                (bb_hbm, bb), (fg_hbm, fg), (fs_hbm, fs), (lb_hbm, lb), (ew_hbm, ew), (eb_hbm, eb),
            ]
        )
    ]
    for fetch in fetches:
        fetch.start()
    zsums[...] = jnp.zeros((N_Z, 1, 128), I32)
    got[...] = jnp.zeros((2, 64, 128), BF16)
    lanes[...] = jnp.zeros((8, 128), F32)

    barrier = pltpu.get_barrier_semaphore()

    def greet(target):
        pl.semaphore_signal(barrier, inc=1, device_id=target, device_id_type=MESH)

    for i in range(1, N_X):
        pl.when(i > x)(functools.partial(greet, at_x(i)))
    for i in range(1, N_Z):
        pl.when(i > z)(functools.partial(greet, at_z(i)))
    for i in range(1, N_DP):
        pl.when(i > rank)(functools.partial(greet, {"dp": DP_ORDER[i]}))
    pl.when((x == 0) & (z > 0))(functools.partial(greet, {"seq": seat - 1}))

    block, select = masks()
    for fetch in fetches[:2] + fetches[3:]:
        fetch.wait()
    live = [(kind[0, i] > 0).astype(I32) for i in range(3)]
    n = live[0] + live[1] + live[2]
    kinds = [
        jnp.where(n == 3, kind[0, 2], jnp.where(n == 2, kind[0, 1], kind[0, 0])),
        jnp.where(n == 2, kind[0, 0], kind[0, 1]),
        jnp.where(n == 3, kind[0, 0], kind[0, 2]),
    ]
    joined = [jnp.full((8, C), kinds[t], I32) == 2 for t in range(3)]
    mine[...] = jnp.full((1, 128), n, I32)
    xcounts[pl.ds(x, 1)] = jnp.full((1, 1, 128), n, I32)
    shard[0:64, :] = ew[...]
    bias_row = jnp.broadcast_to(eb[...].reshape(1, 144).astype(F32), (16, 144))
    shard[64:80, :] = jnp.where(iota((16, 144), 0) == 0, bias_row, 0.0).astype(BF16)
    shards[pl.ds(row, 1)] = shard[...].reshape(1, 80, 144)
    lanes[0:1, 0:16] = lb[...]
    lat_bias = lanes[...]
    for step in (16, 32, 64):
        lat_bias = lat_bias + pltpu.roll(lat_bias, step, 1)
    lat_bias = lat_bias[0:1]

    number = jnp.full((16, C), n, I32)

    def cells(k, i):
        return feat[256 * k + i : 256 * k + i + 16, :]

    def pick(t):
        def rows(i):
            if t == 0:
                return jnp.where(number == 3, cells(2, i), jnp.where(number == 2, cells(1, i), cells(0, i)))
            if t == 1:
                return jnp.where(number == 2, cells(0, i), cells(1, i))
            return jnp.where(number == 3, cells(0, i), cells(2, i))

        return rows

    def spread(vector):
        return jnp.broadcast_to(vector[...], (8, C))

    def first_norm(t):
        return norm_first(pick(t), slots.at[t], block, joined[t], spread(bg), spread(bs), pad.at[t])

    def convolve(t):
        conv(pad.at[t], w, res.at[t])

    def last(t):
        return finish(
            slots.at[t], res.at[t], spread(bb), block, joined[t], spread(fg), spread(fs), act.at[t],
            lw3, lat_bias, select, sent.at[t],
        )

    def copy_to(source, target, send_sem, recv_sem, device):
        return pltpu.make_async_remote_copy(
            src_ref=source, dst_ref=target, send_sem=send_sem, recv_sem=recv_sem,
            device_id=device, device_id_type=MESH,
        )

    x_copies = [copy_to(mine, xcounts.at[x], x_send.at[i], x_recv.at[x], at_x(i)) for i in range(N_X)]
    x_arrivals = [copy_to(mine, xcounts.at[i], x_send.at[i], x_recv.at[i], at_x(i)) for i in range(N_X)]
    z_copies = [copy_to(rowsum, zsums.at[z], z_send.at[i], z_recv.at[z], at_z(i)) for i in range(N_Z)]
    z_arrivals = [copy_to(rowsum, zsums.at[i], z_send.at[i], z_recv.at[i], at_z(i)) for i in range(N_Z)]
    d_peers = [{"dp": DP_ORDER[i]} for i in range(N_DP)]
    d_copies = [copy_to(shard, shards.at[row], d_send.at[i], d_recv.at[rank], d_peers[i]) for i in range(N_DP)]
    d_arrivals = [
        copy_to(shard, shards.at[DP_ORDER[i]], d_send.at[i], d_recv.at[i], d_peers[i]) for i in range(N_DP)
    ]
    p_copies = [
        copy_to(sent.at[t], got.at[t], p_send.at[t], p_recv.at[t], {"seq": lax.rem(seat + 1, N_Z * N_X)})
        for t in range(2)
    ]

    def send_patch(t):
        pl.when(seat < N_Z * N_X - 1)(p_copies[t].start)

    tap_columns(lw, lw3)
    drain((first_norm(0), 42), (first_norm(1), 42))
    earlier = x + z + rank + ((x == N_X - 1) & (z < N_Z - 1)).astype(I32)

    @pl.when(earlier > 0)
    def _():
        pl.semaphore_wait(barrier, earlier)


    def ready(sem, target):
        pl.semaphore_signal(sem, inc=1, device_id=target, device_id_type=MESH)

    for i in range(N_X - 1):
        pl.when(i < x)(functools.partial(ready, x_ready.at[x], at_x(i)))
    for i in range(N_Z - 1):
        pl.when(i < z)(functools.partial(ready, z_ready.at[z], at_z(i)))
    for i in range(N_DP - 1):
        pl.when(i < rank)(functools.partial(ready, d_ready.at[rank], d_peers[i]))
    exchange([(i < x, x_copies[i], None) for i in range(N_X - 1)], True)
    exchange([(i < rank, d_copies[i], None) for i in range(N_DP - 1)], True)

    fetches[2].wait()
    convolve(0)
    convolve(1)
    exchange([(i > x, x_copies[i], x_ready.at[i]) for i in range(1, N_X)], False)
    exchange([(i > rank, d_copies[i], d_ready.at[i]) for i in range(1, N_DP)], False)
    drain((last(0), 60), (last(1), 60))
    for t in range(2):
        send_patch(t)

    drain((first_norm(2), 42))
    convolve(2)
    for i in range(N_X):
        pl.when(i != x)(x_arrivals[i].wait_recv)
    rowsum[...] = jnp.sum(xcounts[...], axis=0)
    exchange([(i > z, z_copies[i], z_ready.at[i]) for i in range(1, N_Z)], False)
    drain((last(2), 60))
    for i in range(N_DP):
        pl.when(i != rank)(d_arrivals[i].wait_recv)
    for i in range(N_DP):
        embed_out[:, 144 * i : 144 * i + 144] = shards[i]
    for i in range(N_Z - 1):
        pl.when(i < z)(z_arrivals[i].wait_recv)
    before = jnp.where(iota((N_X, 1, 128), 0) < x, xcounts[...], 0)
    carry_in = jnp.sum(zsums[...], axis=0) + jnp.sum(before, axis=0) - 2 * seat
    for i in range(N_X):
        pl.when(i != x)(x_arrivals[i].wait_send)
    for i in range(N_DP):
        pl.when(i != rank)(d_arrivals[i].wait_send)
    for i in range(1, N_Z):
        pl.when(i > z)(z_arrivals[i].wait_send)
    for t in range(2):
        pl.when(seat < N_Z * N_X - 1)(p_copies[t].wait_send)
    for t in range(2):
        pl.when(seat > 0)(p_copies[t].wait_recv)

    carry_in = jnp.broadcast_to(carry_in, (64, 128))
    number = jnp.full((64, 128), n, I32)
    own = [sent[t].astype(F32) for t in range(3)]
    came = [got[t].astype(F32) for t in range(2)]
    newest = jnp.where(number == 3, own[2], jnp.where(number == 2, own[1], own[0]))
    second = jnp.where(number == 3, own[1], own[0])
    out0 = jnp.where(carry_in == 0, newest, jnp.where(carry_in == 1, came[0], came[1]))
    out1 = jnp.where(carry_in == 0, second, jnp.where(carry_in == 1, newest, came[0]))
    patches = jnp.concatenate([out0, out1], axis=0)
    patches = jnp.where(iota((128, 128), 1) == 64, 1.0, patches).astype(BF16)
    patch_out[...] = patches[:, :80]


def embed_patches(patches, embed, out):
    out[0] = jnp.dot(patches[...], embed[...], preferred_element_type=F32).astype(BF16)


def local(feat, kind, bg, bs, w, bb, fg, fs, lw, lb, ew, eb):
    hbm = pl.BlockSpec(memory_space=pl.ANY)
    vmem = pl.BlockSpec(memory_space=pltpu.VMEM)
    dma, regular, V = pltpu.SemaphoreType.DMA, pltpu.SemaphoreType.REGULAR, pltpu.VMEM
    vec = V((1, C), F32)
    patches, embed = pl.pallas_call(
        kernel,
        out_shape=(jax.ShapeDtypeStruct((128, 80), BF16), jax.ShapeDtypeStruct((80, HID), BF16)),
        in_specs=[hbm] * 12,
        out_specs=(vmem, vmem),
        scratch_shapes=[
            pltpu.SMEM((1, 3), I32), V((768, C), BF16), vec, vec, V((9 * C, C), BF16), vec, vec, vec,
            V((144, C), BF16), V((1, 16), F32), V((64, 144), BF16), V((144,), BF16),
            V((3, 256, C), F32), V((3, 3, 288, C), BF16), V((3, 256, C), F32), V((3, 256, C), BF16),
            V((C, 384), BF16), V((8, 128), F32), V((1, 128), I32), V((1, 128), I32),
            V((N_X, 1, 128), I32), V((N_Z, 1, 128), I32), V((80, 144), BF16), V((N_DP, 80, 144), BF16),
            V((3, 64, 128), BF16), V((2, 64, 128), BF16),
            dma((12,)), dma((N_X,)), dma((N_X,)), dma((N_Z,)), dma((N_Z,)), dma((N_DP,)), dma((N_DP,)),
            dma((2,)), dma((2,)), regular((N_X,)), regular((N_Z,)), regular((N_DP,)),
        ],
        compiler_params=pltpu.CompilerParams(
            collective_id=0, has_side_effects=True, vmem_limit_bytes=60 << 20
        ),
    )(
        kind, feat, bg.reshape(1, C), bs.reshape(1, C), w, bb.reshape(1, C), fg.reshape(1, C),
        fs.reshape(1, C), lw.T, lb.reshape(1, 16), ew, eb,
    )
    return pl.pallas_call(
        embed_patches,
        out_shape=jax.ShapeDtypeStruct((1, 128, HID), BF16),
        in_specs=[vmem, vmem],
        out_specs=vmem,
    )(patches, embed)


def solution(mesh):
    shared = P()
    return jax.shard_map(
        local,
        mesh=mesh,
        in_specs=(P("dp", "seq", None), P("dp", "seq")) + (shared,) * 8 + (P(None, "dp"), P("dp")),
        out_specs=P("dp", "seq", None),
        check_vma=False,
    )
```

```python
import functools
import jax
import jax.numpy as jnp
from jax import lax
from jax.experimental import pallas as pl
from jax.experimental.pallas import tpu as pltpu
from jax.sharding import PartitionSpec as P

F32, BF16, I32 = jnp.float32, jnp.bfloat16, jnp.int32
MESH = pl.DeviceIdType.MESH
LATENT_SHIFT = 0.0609
LATENT_SCALE = 1.5305
EPS = 1e-06
C = 512
HID = 1152
TAPS = [(a, b) for a in (-1, 0, 1) for b in (-1, 0, 1)]
N_DP, N_Z, N_X = 8, 8, 4


def iota(shape, dim):
    return lax.broadcasted_iota(I32, shape, dim)


def drain(*streams):
    live = [[stream, steps, 0] for stream, steps in streams]
    while live:
        entry = min(live, key=lambda e: (e[2] + 1) / e[1])
        entry[2] += 1
        try:
            next(entry[0])
        except StopIteration:
            live.remove(entry)


def group_sums(parts, block):
    rows = jnp.concatenate([p[:, 256 * i : 256 * i + 256] for p in parts for i in range(2)], axis=0)
    hi = rows.astype(BF16)
    rest = rows - hi.astype(F32)
    mid = rest.astype(BF16)
    low = (rest - mid.astype(F32)).astype(BF16)
    sums = jnp.dot(jnp.concatenate([hi, mid, low], axis=0), block, preferred_element_type=F32)
    total = sums[:32] + sums[32:64] + sums[64:]
    out = []
    for i in range(len(parts)):
        tiles = [total[16 * i + 8 * j : 16 * i + 8 * j + 8] for j in range(2)]
        tiles = [jnp.broadcast_to(jnp.sum(t, axis=0, keepdims=True), (8, 256)) for t in tiles]
        out.append(jnp.concatenate(tiles, axis=1))
    return out


def norm_factors(sums, load, block, joined, gain, shift):
    m0, m1 = group_sums(sums, block)
    m0, m1 = m0 * (1.0 / 2048), m1 * (1.0 / 2048)
    both = (m0 + m1) * 0.5
    c0, c1 = jnp.where(joined, both, m0), jnp.where(joined, both, m1)
    low, high = jnp.zeros((8, C), F32), jnp.zeros((8, C), F32)
    for r in range(16):
        x0, x1 = load(r)
        x0, x1 = x0 - c0, x1 - c1
        low, high = low + x0 * x0, high + x1 * x1
        yield
    v0, v1 = group_sums([low, high], block)
    v0, v1 = v0 * (1.0 / 2048), v1 * (1.0 / 2048)
    both = (v0 + v1) * 0.5
    v0, v1 = jnp.where(joined, both, v0), jnp.where(joined, both, v1)
    s0 = lax.rsqrt(v0 + EPS) * gain * 0.5
    s1 = lax.rsqrt(v1 + EPS) * gain * 0.5
    return s0, s1, shift * 0.5 - c0 * s0, shift * 0.5 - c1 * s1


def silu_half(half):
    return half + half * jnp.tanh(half)


def pair(top, bottom):
    return jnp.concatenate([top, bottom], axis=0).astype(BF16)


def loader(ref):
    def load(r):
        return ref[16 * r : 16 * r + 8, :], ref[16 * r + 8 : 16 * r + 16, :]

    return load


def order_slot(pick, slot):
    low, high = jnp.zeros((8, C), F32), jnp.zeros((8, C), F32)
    for i in range(8):
        top, bottom = pick(16 * i).astype(F32), pick(128 + 16 * i).astype(F32)
        for j in range(2):
            x0, x1 = top[8 * j : 8 * j + 8], bottom[8 * j : 8 * j + 8]
            r = 2 * i + j
            slot[16 * r : 16 * r + 8, :], slot[16 * r + 8 : 16 * r + 16, :] = x0, x1
            low, high = low + x0, high + x1
        yield
    return low, high


def norm_first(pick, slot, block, joined, gain, shift, pad):
    sums = yield from order_slot(pick, slot)
    load = loader(slot)
    s0, s1, t0, t1 = yield from norm_factors(sums, load, block, joined, gain, shift)
    zero = jnp.zeros((8, C), F32)
    col = iota((8, C), 0)
    for r in range(16):
        x0, x1 = load(r)
        sides = []
        for y in (silu_half(x0 * s0 + t0), silu_half(x1 * s1 + t1)):
            left = jnp.where(col >= 1, pltpu.roll(y, 1, 0), 0.0)
            right = jnp.where(col <= 6, pltpu.roll(y, 7, 0), 0.0)
            sides.append((left, y, right))
        for b in range(3):
            pad[b, 16 * (r + 1) : 16 * (r + 2), :] = pair(sides[0][b], sides[1][b])
            if r == 0:
                pad[b, 16 * 17 : 16 * 18, :] = pair(jnp.where(joined, sides[1][b], 0.0), zero)
            if r == 15:
                pad[b, 0:16, :] = pair(zero, jnp.where(joined, sides[0][b], 0.0))
        yield


def conv(pad, w, res):
    lhs = jnp.concatenate(
        [pad[b + 1, 16 * (a + 1) : 16 * (a + 1) + 256, :] for a, b in TAPS], axis=1
    )
    res[...] = jnp.dot(lhs, w[...], preferred_element_type=F32)


def finish(slot, res, bias, block, joined, gain, shift, act, lw3, lat_bias, select, out):
    own, added = loader(slot), loader(res)
    low, high = jnp.zeros((8, C), F32), jnp.zeros((8, C), F32)
    for r in range(16):
        (x0, x1), (d0, d1) = own(r), added(r)
        x0, x1 = x0 + d0 + bias, x1 + d1 + bias
        res[16 * r : 16 * r + 8, :], res[16 * r + 8 : 16 * r + 16, :] = x0, x1
        low, high = low + x0, high + x1
        yield
    s0, s1, t0, t1 = yield from norm_factors([low, high], added, block, joined, gain, shift)
    for r in range(16):
        x0, x1 = added(r)
        act[16 * r : 16 * r + 16, :] = pair(silu_half(x0 * s0 + t0), silu_half(x1 * s1 + t1))
        yield
    yield from latent_patches(act, lw3, lat_bias, joined, select, out)


def latent_patches(act, lw3, lat_bias, joined, select, out):
    terms = jnp.dot(act[...], lw3[...], preferred_element_type=F32)
    yield
    joined = joined[:, :128]
    zero = jnp.zeros((8, 128), F32)

    def part(a, r, h):
        return terms[16 * r + 8 * h : 16 * r + 8 * h + 8, 128 * (a + 1) : 128 * (a + 2)]

    col = iota((8, 128), 0)
    lane = iota((8, 128), 1)
    rows = []
    for r in range(16):
        for h in range(2):
            i = r % 2
            above = part(-1, r - 1, h) if r > 0 else (jnp.where(joined, part(-1, 15, 0), 0.0) if h == 1 else zero)
            below = part(1, r + 1, h) if r < 15 else (jnp.where(joined, part(1, 0, 1), 0.0) if h == 0 else zero)
            v = above + part(0, r, h) + below
            left = jnp.where(col >= 1, pltpu.roll(v, 1, 0), 0.0)
            right = jnp.where(col <= 6, pltpu.roll(v, 7, 0), 0.0)
            if i == 0:
                lat = left + pltpu.roll(v, 96, 1) + pltpu.roll(right, 64, 1)
            else:
                lat = pltpu.roll(left, 32, 1) + v + pltpu.roll(right, 96, 1)
            lat = (lat + lat_bias - LATENT_SHIFT) * LATENT_SCALE
            rows.append(jnp.where((lane // 16) == (2 * i + col % 2), lat, 0.0))
        if r % 2:
            yield
    cells = jnp.concatenate(rows, axis=0).astype(BF16)
    out[...] = jnp.dot(select, cells, preferred_element_type=F32).astype(BF16)


def tap_columns(lwt, lw3):
    zero = jnp.zeros((16, C), BF16)
    for a in range(3):
        taps = [lwt[16 * (3 * a + b) : 16 * (3 * a + b) + 16, :] for b in range(3)]
        rows = jnp.concatenate([taps[0], taps[0], taps[1], taps[1], taps[2], taps[2], zero, zero], axis=0)
        lw3[:, 128 * a : 128 * a + 128] = rows.T


def masks():
    block = jnp.where(iota((256, 256), 0) // 16 == iota((256, 256), 1) // 16, 1.0, 0.0).astype(BF16)
    t, m = iota((64, 256), 0), iota((64, 256), 1)
    same = (m // 32 == (t // 4) % 8) & ((m // 8) % 2 == t // 32) & ((m % 8) // 2 == t % 4)
    return block, jnp.where(same, 1.0, 0.0).astype(BF16)


DP_ORDER = (0, 1, 2, 6, 3, 7, 4, 5)


def exchange(pairs, start_now):
    for condition, copy, ready in pairs:

        @pl.when(condition)
        def _(copy=copy, ready=ready):
            if not start_now:
                pl.semaphore_wait(ready, 1)
            copy.start()


def kernel(
    kind_hbm, feat_hbm, bg_hbm, bs_hbm, w_hbm, bb_hbm, fg_hbm, fs_hbm, lw_hbm, lb_hbm, ew_hbm, eb_hbm,
    patch_out, embed_out,
    kind, feat, bg, bs, w, bb, fg, fs, lw, lb, ew, eb,
    slots, pad, res, act, lw3, lanes, mine, rowsum, xcounts, zsums, shard, shards, sent, got,
    in_sem, x_send, x_recv, z_send, z_recv, d_send, d_recv, p_send, p_recv, x_ready, z_ready, d_ready,
):
    seat, row = lax.axis_index("seq"), lax.axis_index("dp")
    z, x = seat // N_X, lax.rem(seat, N_X)
    rank = sum(jnp.where(row == DP_ORDER[i], i, 0) for i in range(N_DP))

    def at_x(i):
        return {"seq": z * N_X + i}

    def at_z(i):
        return {"seq": i * N_X + x}

    fetches = [
        pltpu.make_async_copy(source, target, in_sem.at[i])
        for i, (source, target) in enumerate(
            [
                (kind_hbm, kind), (lw_hbm, lw), (bg_hbm, bg), (bs_hbm, bs), (bb_hbm, bb), (fg_hbm, fg),
                (fs_hbm, fs), (lb_hbm, lb), (ew_hbm, ew), (eb_hbm, eb), (feat_hbm.at[0], feat), (w_hbm, w),
            ]
        )
    ]
    for fetch in fetches:
        fetch.start()
    zsums[...] = jnp.zeros((N_Z, 1, 128), I32)
    got[...] = jnp.zeros((2, 64, 128), BF16)
    lanes[...] = jnp.zeros((8, 128), F32)

    barrier = pltpu.get_barrier_semaphore()

    def greet(target):
        pl.semaphore_signal(barrier, inc=1, device_id=target, device_id_type=MESH)

    for i in range(1, N_DP):
        pl.when(i > rank)(functools.partial(greet, {"dp": DP_ORDER[i]}))
    for i in range(1, N_X):
        pl.when(i > x)(functools.partial(greet, at_x(i)))
    pl.when((x == 0) & (z > 0))(functools.partial(greet, {"seq": seat - 1}))
    for i in range(1, N_Z):
        pl.when(i > z)(functools.partial(greet, at_z(i)))

    block, select = masks()
    for fetch in fetches[:10]:
        fetch.wait()
    live = [(kind[0, i] > 0).astype(I32) for i in range(3)]
    n = live[0] + live[1] + live[2]
    kinds = [
        jnp.where(n == 3, kind[0, 2], jnp.where(n == 2, kind[0, 1], kind[0, 0])),
        jnp.where(n == 2, kind[0, 0], kind[0, 1]),
        jnp.where(n == 3, kind[0, 0], kind[0, 2]),
    ]
    joined = [jnp.full((8, C), kinds[t], I32) == 2 for t in range(3)]
    mine[...] = jnp.full((1, 128), n, I32)
    xcounts[pl.ds(x, 1)] = jnp.full((1, 1, 128), n, I32)
    shard[0:64, :] = ew[...]
    bias_row = jnp.broadcast_to(eb[...].reshape(1, 144).astype(F32), (16, 144))
    shard[64:80, :] = jnp.where(iota((16, 144), 0) == 0, bias_row, 0.0).astype(BF16)
    shards[pl.ds(row, 1)] = shard[...].reshape(1, 80, 144)
    lanes[0:1, 0:16] = lb[...]
    lat_bias = lanes[...]
    for step in (16, 32, 64):
        lat_bias = lat_bias + pltpu.roll(lat_bias, step, 1)
    lat_bias = lat_bias[0:1]

    number = jnp.full((16, C), n, I32)

    def cells(k, i):
        return feat[256 * k + i : 256 * k + i + 16, :]

    def pick(t):
        def rows(i):
            if t == 0:
                return jnp.where(number == 3, cells(2, i), jnp.where(number == 2, cells(1, i), cells(0, i)))
            if t == 1:
                return jnp.where(number == 2, cells(0, i), cells(1, i))
            return jnp.where(number == 3, cells(0, i), cells(2, i))

        return rows

    def spread(vector):
        return jnp.broadcast_to(vector[...], (8, C))

    def first_norm(t):
        return norm_first(pick(t), slots.at[t], block, joined[t], spread(bg), spread(bs), pad.at[t])

    def convolve(t):
        conv(pad.at[t], w, res.at[t])

    def last(t):
        return finish(
            slots.at[t], res.at[t], spread(bb), block, joined[t], spread(fg), spread(fs), act.at[t],
            lw3, lat_bias, select, sent.at[t],
        )

    def copy_to(source, target, send_sem, recv_sem, device):
        return pltpu.make_async_remote_copy(
            src_ref=source, dst_ref=target, send_sem=send_sem, recv_sem=recv_sem,
            device_id=device, device_id_type=MESH,
        )

    x_copies = [copy_to(mine, xcounts.at[x], x_send.at[i], x_recv.at[x], at_x(i)) for i in range(N_X)]
    x_arrivals = [copy_to(mine, xcounts.at[i], x_send.at[i], x_recv.at[i], at_x(i)) for i in range(N_X)]
    z_copies = [copy_to(rowsum, zsums.at[z], z_send.at[i], z_recv.at[z], at_z(i)) for i in range(N_Z)]
    z_arrivals = [copy_to(rowsum, zsums.at[i], z_send.at[i], z_recv.at[i], at_z(i)) for i in range(N_Z)]
    d_peers = [{"dp": DP_ORDER[i]} for i in range(N_DP)]
    d_copies = [copy_to(shard, shards.at[row], d_send.at[i], d_recv.at[rank], d_peers[i]) for i in range(N_DP)]
    d_arrivals = [
        copy_to(shard, shards.at[DP_ORDER[i]], d_send.at[i], d_recv.at[i], d_peers[i]) for i in range(N_DP)
    ]
    p_copies = [
        copy_to(sent.at[t], got.at[t], p_send.at[t], p_recv.at[t], {"seq": lax.rem(seat + 1, N_Z * N_X)})
        for t in range(2)
    ]

    def send_patch(t):
        pl.when(seat < N_Z * N_X - 1)(p_copies[t].start)

    tap_columns(lw, lw3)
    fetches[10].wait()
    drain((first_norm(0), 42), (first_norm(1), 42))
    earlier = x + z + rank + ((x == N_X - 1) & (z < N_Z - 1)).astype(I32)

    @pl.when(earlier > 0)
    def _():
        pl.semaphore_wait(barrier, earlier)


    def ready(sem, target):
        pl.semaphore_signal(sem, inc=1, device_id=target, device_id_type=MESH)

    for i in range(N_X - 1):
        pl.when(i < x)(functools.partial(ready, x_ready.at[x], at_x(i)))
    for i in range(N_Z - 1):
        pl.when(i < z)(functools.partial(ready, z_ready.at[z], at_z(i)))
    for i in range(N_DP - 1):
        pl.when(i < rank)(functools.partial(ready, d_ready.at[rank], d_peers[i]))
    exchange([(i < x, x_copies[i], None) for i in range(N_X - 1)], True)
    exchange([(i < rank, d_copies[i], None) for i in range(N_DP - 1)], True)

    fetches[11].wait()
    convolve(0)
    convolve(1)
    exchange([(i > x, x_copies[i], x_ready.at[i]) for i in range(1, N_X)], False)
    exchange([(i > rank, d_copies[i], d_ready.at[i]) for i in range(1, N_DP)], False)
    drain((last(0), 60), (last(1), 60))
    for t in range(2):
        send_patch(t)

    drain((first_norm(2), 42))
    for i in range(N_X):
        pl.when(i != x)(x_arrivals[i].wait_recv)
    rowsum[...] = jnp.sum(xcounts[...], axis=0)
    exchange([(i > z, z_copies[i], z_ready.at[i]) for i in range(1, N_Z)], False)
    convolve(2)
    drain((last(2), 60))
    for i in range(N_DP):
        pl.when(i != rank)(d_arrivals[i].wait_recv)
    for i in range(N_DP):
        embed_out[:, 144 * i : 144 * i + 144] = shards[i]
    for i in range(N_Z - 1):
        pl.when(i < z)(z_arrivals[i].wait_recv)
    before = jnp.where(iota((N_X, 1, 128), 0) < x, xcounts[...], 0)
    carry_in = jnp.sum(zsums[...], axis=0) + jnp.sum(before, axis=0) - 2 * seat
    for i in range(N_X):
        pl.when(i != x)(x_arrivals[i].wait_send)
    for i in range(N_DP):
        pl.when(i != rank)(d_arrivals[i].wait_send)
    for i in range(1, N_Z):
        pl.when(i > z)(z_arrivals[i].wait_send)
    for t in range(2):
        pl.when(seat < N_Z * N_X - 1)(p_copies[t].wait_send)
    for t in range(2):
        pl.when(seat > 0)(p_copies[t].wait_recv)

    carry_in = jnp.broadcast_to(carry_in, (64, 128))
    number = jnp.full((64, 128), n, I32)
    own = [sent[t].astype(F32) for t in range(3)]
    came = [got[t].astype(F32) for t in range(2)]
    newest = jnp.where(number == 3, own[2], jnp.where(number == 2, own[1], own[0]))
    second = jnp.where(number == 3, own[1], own[0])
    out0 = jnp.where(carry_in == 0, newest, jnp.where(carry_in == 1, came[0], came[1]))
    out1 = jnp.where(carry_in == 0, second, jnp.where(carry_in == 1, newest, came[0]))
    patches = jnp.concatenate([out0, out1], axis=0)
    patches = jnp.where(iota((128, 128), 1) == 64, 1.0, patches).astype(BF16)
    patch_out[...] = patches[:, :80]


def embed_patches(patches, embed, out):
    out[0] = jnp.dot(patches[...], embed[...], preferred_element_type=F32).astype(BF16)


def local(feat, kind, bg, bs, w, bb, fg, fs, lw, lb, ew, eb):
    hbm = pl.BlockSpec(memory_space=pl.ANY)
    vmem = pl.BlockSpec(memory_space=pltpu.VMEM)
    dma, regular, V = pltpu.SemaphoreType.DMA, pltpu.SemaphoreType.REGULAR, pltpu.VMEM
    vec = V((1, C), F32)
    patches, embed = pl.pallas_call(
        kernel,
        out_shape=(jax.ShapeDtypeStruct((128, 80), BF16), jax.ShapeDtypeStruct((80, HID), BF16)),
        in_specs=[hbm] * 12,
        out_specs=(vmem, vmem),
        scratch_shapes=[
            pltpu.SMEM((1, 3), I32), V((768, C), BF16), vec, vec, V((9 * C, C), BF16), vec, vec, vec,
            V((144, C), BF16), V((1, 16), F32), V((64, 144), BF16), V((144,), BF16),
            V((3, 256, C), F32), V((3, 3, 288, C), BF16), V((3, 256, C), F32), V((3, 256, C), BF16),
            V((C, 384), BF16), V((8, 128), F32), V((1, 128), I32), V((1, 128), I32),
            V((N_X, 1, 128), I32), V((N_Z, 1, 128), I32), V((80, 144), BF16), V((N_DP, 80, 144), BF16),
            V((3, 64, 128), BF16), V((2, 64, 128), BF16),
            dma((12,)), dma((N_X,)), dma((N_X,)), dma((N_Z,)), dma((N_Z,)), dma((N_DP,)), dma((N_DP,)),
            dma((2,)), dma((2,)), regular((N_X,)), regular((N_Z,)), regular((N_DP,)),
        ],
        compiler_params=pltpu.CompilerParams(
            collective_id=0, has_side_effects=True, vmem_limit_bytes=60 << 20
        ),
    )(
        kind, feat, bg.reshape(1, C), bs.reshape(1, C), w, bb.reshape(1, C), fg.reshape(1, C),
        fs.reshape(1, C), lw.T, lb.reshape(1, 16), ew, eb,
    )
    return pl.pallas_call(
        embed_patches,
        out_shape=jax.ShapeDtypeStruct((1, 128, HID), BF16),
        in_specs=[vmem, vmem],
        out_specs=vmem,
    )(patches, embed)


def solution(mesh):
    shared = P()
    return jax.shard_map(
        local,
        mesh=mesh,
        in_specs=(P("dp", "seq", None), P("dp", "seq")) + (shared,) * 8 + (P(None, "dp"), P("dp")),
        out_specs=P("dp", "seq", None),
        check_vma=False,
    )
```

```python
import functools
import jax
import jax.numpy as jnp
from jax import lax
from jax.experimental import pallas as pl
from jax.experimental.pallas import tpu as pltpu
from jax.sharding import PartitionSpec as P

F32, BF16, I32 = jnp.float32, jnp.bfloat16, jnp.int32
MESH = pl.DeviceIdType.MESH
LATENT_SHIFT = 0.0609
LATENT_SCALE = 1.5305
EPS = 1e-06
C = 512
HID = 1152
TAPS = [(a, b) for a in (-1, 0, 1) for b in (-1, 0, 1)]
N_DP, N_Z, N_X = 8, 8, 4


def iota(shape, dim):
    return lax.broadcasted_iota(I32, shape, dim)


def drain(*streams):
    live = [[stream, steps, 0] for stream, steps in streams]
    while live:
        entry = min(live, key=lambda e: (e[2] + 1) / e[1])
        entry[2] += 1
        try:
            next(entry[0])
        except StopIteration:
            live.remove(entry)


def group_sums(parts, block):
    rows = jnp.concatenate([p[:, 256 * i : 256 * i + 256] for p in parts for i in range(2)], axis=0)
    hi = rows.astype(BF16)
    rest = rows - hi.astype(F32)
    mid = rest.astype(BF16)
    low = (rest - mid.astype(F32)).astype(BF16)
    sums = jnp.dot(jnp.concatenate([hi, mid, low], axis=0), block, preferred_element_type=F32)
    total = sums[:32] + sums[32:64] + sums[64:]
    out = []
    for i in range(len(parts)):
        tiles = [total[16 * i + 8 * j : 16 * i + 8 * j + 8] for j in range(2)]
        tiles = [jnp.broadcast_to(jnp.sum(t, axis=0, keepdims=True), (8, 256)) for t in tiles]
        out.append(jnp.concatenate(tiles, axis=1))
    return out


def norm_factors(sums, load, block, joined, gain, shift):
    m0, m1 = group_sums(sums, block)
    m0, m1 = m0 * (1.0 / 2048), m1 * (1.0 / 2048)
    both = (m0 + m1) * 0.5
    c0, c1 = jnp.where(joined, both, m0), jnp.where(joined, both, m1)
    low, high = jnp.zeros((8, C), F32), jnp.zeros((8, C), F32)
    for r in range(16):
        x0, x1 = load(r)
        x0, x1 = x0 - c0, x1 - c1
        low, high = low + x0 * x0, high + x1 * x1
        yield
    v0, v1 = group_sums([low, high], block)
    v0, v1 = v0 * (1.0 / 2048), v1 * (1.0 / 2048)
    both = (v0 + v1) * 0.5
    v0, v1 = jnp.where(joined, both, v0), jnp.where(joined, both, v1)
    s0 = lax.rsqrt(v0 + EPS) * gain * 0.5
    s1 = lax.rsqrt(v1 + EPS) * gain * 0.5
    return s0, s1, shift * 0.5 - c0 * s0, shift * 0.5 - c1 * s1


def silu_half(half):
    return half + half * jnp.tanh(half)


def pair(top, bottom):
    return jnp.concatenate([top, bottom], axis=0).astype(BF16)


def loader(ref):
    def load(r):
        return ref[16 * r : 16 * r + 8, :], ref[16 * r + 8 : 16 * r + 16, :]

    return load


def order_slot(pick, slot):
    low, high = jnp.zeros((8, C), F32), jnp.zeros((8, C), F32)
    for i in range(8):
        top, bottom = pick(16 * i).astype(F32), pick(128 + 16 * i).astype(F32)
        for j in range(2):
            x0, x1 = top[8 * j : 8 * j + 8], bottom[8 * j : 8 * j + 8]
            r = 2 * i + j
            slot[16 * r : 16 * r + 8, :], slot[16 * r + 8 : 16 * r + 16, :] = x0, x1
            low, high = low + x0, high + x1
        yield
    return low, high


def norm_first(pick, slot, block, joined, gain, shift, pad):
    sums = yield from order_slot(pick, slot)
    load = loader(slot)
    s0, s1, t0, t1 = yield from norm_factors(sums, load, block, joined, gain, shift)
    zero = jnp.zeros((8, C), F32)
    col = iota((8, C), 0)
    for r in range(16):
        x0, x1 = load(r)
        sides = []
        for y in (silu_half(x0 * s0 + t0), silu_half(x1 * s1 + t1)):
            left = jnp.where(col >= 1, pltpu.roll(y, 1, 0), 0.0)
            right = jnp.where(col <= 6, pltpu.roll(y, 7, 0), 0.0)
            sides.append((left, y, right))
        for b in range(3):
            pad[b, 16 * (r + 1) : 16 * (r + 2), :] = pair(sides[0][b], sides[1][b])
            if r == 0:
                pad[b, 16 * 17 : 16 * 18, :] = pair(jnp.where(joined, sides[1][b], 0.0), zero)
            if r == 15:
                pad[b, 0:16, :] = pair(zero, jnp.where(joined, sides[0][b], 0.0))
        yield


def conv(pad, w, res):
    lhs = jnp.concatenate(
        [pad[b + 1, 16 * (a + 1) : 16 * (a + 1) + 256, :] for a, b in TAPS], axis=1
    )
    res[...] = jnp.dot(lhs, w[...], preferred_element_type=F32)


def finish(slot, res, bias, block, joined, gain, shift, act, lw3, lat_bias, select, out):
    own, added = loader(slot), loader(res)
    low, high = jnp.zeros((8, C), F32), jnp.zeros((8, C), F32)
    for r in range(16):
        (x0, x1), (d0, d1) = own(r), added(r)
        x0, x1 = x0 + d0 + bias, x1 + d1 + bias
        res[16 * r : 16 * r + 8, :], res[16 * r + 8 : 16 * r + 16, :] = x0, x1
        low, high = low + x0, high + x1
        yield
    s0, s1, t0, t1 = yield from norm_factors([low, high], added, block, joined, gain, shift)
    for r in range(16):
        x0, x1 = added(r)
        act[16 * r : 16 * r + 16, :] = pair(silu_half(x0 * s0 + t0), silu_half(x1 * s1 + t1))
        yield
    yield from latent_patches(act, lw3, lat_bias, joined, select, out)


def latent_patches(act, lw3, lat_bias, joined, select, out):
    terms = jnp.dot(act[...], lw3[...], preferred_element_type=F32)
    yield
    joined = joined[:, :128]
    zero = jnp.zeros((8, 128), F32)

    def part(a, r, h):
        return terms[16 * r + 8 * h : 16 * r + 8 * h + 8, 128 * (a + 1) : 128 * (a + 2)]

    col = iota((8, 128), 0)
    lane = iota((8, 128), 1)
    offset = (lat_bias - LATENT_SHIFT) * LATENT_SCALE
    rows = []
    for r in range(16):
        for h in range(2):
            i = r % 2
            above = part(-1, r - 1, h) if r > 0 else (jnp.where(joined, part(-1, 15, 0), 0.0) if h == 1 else zero)
            below = part(1, r + 1, h) if r < 15 else (jnp.where(joined, part(1, 0, 1), 0.0) if h == 0 else zero)
            v = above + part(0, r, h) + below
            left = jnp.where(col >= 1, pltpu.roll(v, 1, 0), 0.0)
            right = jnp.where(col <= 6, pltpu.roll(v, 7, 0), 0.0)
            if i == 0:
                lat = left + pltpu.roll(v, 96, 1) + pltpu.roll(right, 64, 1)
            else:
                lat = pltpu.roll(left, 32, 1) + v + pltpu.roll(right, 96, 1)
            lat = lat * LATENT_SCALE + offset
            rows.append(jnp.where((lane // 16) == (2 * i + col % 2), lat, 0.0))
        if r % 2:
            yield
    cells = jnp.concatenate(rows, axis=0).astype(BF16)
    out[...] = jnp.dot(select, cells, preferred_element_type=F32).astype(BF16)


def tap_columns(lwt, lw3):
    zero = jnp.zeros((16, C), BF16)
    for a in range(3):
        taps = [lwt[16 * (3 * a + b) : 16 * (3 * a + b) + 16, :] for b in range(3)]
        rows = jnp.concatenate([taps[0], taps[0], taps[1], taps[1], taps[2], taps[2], zero, zero], axis=0)
        lw3[:, 128 * a : 128 * a + 128] = rows.T


def masks():
    block = jnp.where(iota((256, 256), 0) // 16 == iota((256, 256), 1) // 16, 1.0, 0.0).astype(BF16)
    t, m = iota((64, 256), 0), iota((64, 256), 1)
    same = (m // 32 == (t // 4) % 8) & ((m // 8) % 2 == t // 32) & ((m % 8) // 2 == t % 4)
    return block, jnp.where(same, 1.0, 0.0).astype(BF16)


DP_ORDER = (0, 1, 2, 6, 3, 7, 4, 5)


def exchange(pairs, start_now):
    for condition, copy, ready in pairs:

        @pl.when(condition)
        def _(copy=copy, ready=ready):
            if not start_now:
                pl.semaphore_wait(ready, 1)
            copy.start()


def kernel(
    kind_hbm, feat_hbm, bg_hbm, bs_hbm, w_hbm, bb_hbm, fg_hbm, fs_hbm, lw_hbm, lb_hbm, ew_hbm, eb_hbm,
    patch_out, embed_out,
    kind, feat, bg, bs, w, bb, fg, fs, lw, lb, ew, eb,
    slots, pad, res, act, lw3, lanes, mine, rowsum, xcounts, zsums, shard, shards, sent, got,
    in_sem, x_send, x_recv, z_send, z_recv, d_send, d_recv, p_send, p_recv, x_ready, z_ready, d_ready,
):
    seat, row = lax.axis_index("seq"), lax.axis_index("dp")
    z, x = seat // N_X, lax.rem(seat, N_X)
    rank = sum(jnp.where(row == DP_ORDER[i], i, 0) for i in range(N_DP))

    def at_x(i):
        return {"seq": z * N_X + i}

    def at_z(i):
        return {"seq": i * N_X + x}

    fetches = [
        pltpu.make_async_copy(source, target, in_sem.at[i])
        for i, (source, target) in enumerate(
            [
                (kind_hbm, kind), (lw_hbm, lw), (bg_hbm, bg), (bs_hbm, bs), (bb_hbm, bb), (fg_hbm, fg),
                (fs_hbm, fs), (lb_hbm, lb), (ew_hbm, ew), (eb_hbm, eb), (feat_hbm.at[0], feat), (w_hbm, w),
            ]
        )
    ]
    for fetch in fetches:
        fetch.start()
    zsums[...] = jnp.zeros((N_Z, 1, 128), I32)
    got[...] = jnp.zeros((2, 64, 128), BF16)
    lanes[...] = jnp.zeros((8, 128), F32)

    barrier = pltpu.get_barrier_semaphore()

    def greet(target):
        pl.semaphore_signal(barrier, inc=1, device_id=target, device_id_type=MESH)

    for i in range(1, N_DP):
        pl.when(i > rank)(functools.partial(greet, {"dp": DP_ORDER[i]}))
    for i in range(1, N_X):
        pl.when(i > x)(functools.partial(greet, at_x(i)))
    pl.when((x == 0) & (z > 0))(functools.partial(greet, {"seq": seat - 1}))
    for i in range(1, N_Z):
        pl.when(i > z)(functools.partial(greet, at_z(i)))

    block, select = masks()
    for fetch in fetches[:10]:
        fetch.wait()
    live = [(kind[0, i] > 0).astype(I32) for i in range(3)]
    n = live[0] + live[1] + live[2]
    kinds = [
        jnp.where(n == 3, kind[0, 2], jnp.where(n == 2, kind[0, 1], kind[0, 0])),
        jnp.where(n == 2, kind[0, 0], kind[0, 1]),
        jnp.where(n == 3, kind[0, 0], kind[0, 2]),
    ]
    joined = [jnp.full((8, C), kinds[t], I32) == 2 for t in range(3)]
    mine[...] = jnp.full((1, 128), n, I32)
    xcounts[pl.ds(x, 1)] = jnp.full((1, 1, 128), n, I32)
    shard[0:64, :] = ew[...]
    bias_row = jnp.broadcast_to(eb[...].reshape(1, 144).astype(F32), (16, 144))
    shard[64:80, :] = jnp.where(iota((16, 144), 0) == 0, bias_row, 0.0).astype(BF16)
    shards[pl.ds(row, 1)] = shard[...].reshape(1, 80, 144)
    lanes[0:1, 0:16] = lb[...]
    lat_bias = lanes[...]
    for step in (16, 32, 64):
        lat_bias = lat_bias + pltpu.roll(lat_bias, step, 1)
    lat_bias = lat_bias[0:1]

    number = jnp.full((16, C), n, I32)

    def cells(k, i):
        return feat[256 * k + i : 256 * k + i + 16, :]

    def pick(t):
        def rows(i):
            if t == 0:
                return jnp.where(number == 3, cells(2, i), jnp.where(number == 2, cells(1, i), cells(0, i)))
            if t == 1:
                return jnp.where(number == 2, cells(0, i), cells(1, i))
            return jnp.where(number == 3, cells(0, i), cells(2, i))

        return rows

    def spread(vector):
        return jnp.broadcast_to(vector[...], (8, C))

    def first_norm(t):
        return norm_first(pick(t), slots.at[t], block, joined[t], spread(bg), spread(bs), pad.at[t])

    def convolve(t):
        conv(pad.at[t], w, res.at[t])

    def last(t):
        return finish(
            slots.at[t], res.at[t], spread(bb), block, joined[t], spread(fg), spread(fs), act.at[t],
            lw3, lat_bias, select, sent.at[t],
        )

    def copy_to(source, target, send_sem, recv_sem, device):
        return pltpu.make_async_remote_copy(
            src_ref=source, dst_ref=target, send_sem=send_sem, recv_sem=recv_sem,
            device_id=device, device_id_type=MESH,
        )

    x_copies = [copy_to(mine, xcounts.at[x], x_send.at[i], x_recv.at[x], at_x(i)) for i in range(N_X)]
    x_arrivals = [copy_to(mine, xcounts.at[i], x_send.at[i], x_recv.at[i], at_x(i)) for i in range(N_X)]
    z_copies = [copy_to(rowsum, zsums.at[z], z_send.at[i], z_recv.at[z], at_z(i)) for i in range(N_Z)]
    z_arrivals = [copy_to(rowsum, zsums.at[i], z_send.at[i], z_recv.at[i], at_z(i)) for i in range(N_Z)]
    d_peers = [{"dp": DP_ORDER[i]} for i in range(N_DP)]
    d_copies = [copy_to(shard, shards.at[row], d_send.at[i], d_recv.at[rank], d_peers[i]) for i in range(N_DP)]
    d_arrivals = [
        copy_to(shard, shards.at[DP_ORDER[i]], d_send.at[i], d_recv.at[i], d_peers[i]) for i in range(N_DP)
    ]
    p_copies = [
        copy_to(sent.at[t], got.at[t], p_send.at[t], p_recv.at[t], {"seq": lax.rem(seat + 1, N_Z * N_X)})
        for t in range(2)
    ]

    def send_patch(t):
        pl.when(seat < N_Z * N_X - 1)(p_copies[t].start)

    tap_columns(lw, lw3)
    fetches[10].wait()
    drain((first_norm(0), 42), (first_norm(1), 42))
    earlier = x + z + rank + ((x == N_X - 1) & (z < N_Z - 1)).astype(I32)

    @pl.when(earlier > 0)
    def _():
        pl.semaphore_wait(barrier, earlier)


    def ready(sem, target):
        pl.semaphore_signal(sem, inc=1, device_id=target, device_id_type=MESH)

    for i in range(N_X - 1):
        pl.when(i < x)(functools.partial(ready, x_ready.at[x], at_x(i)))
    for i in range(N_Z - 1):
        pl.when(i < z)(functools.partial(ready, z_ready.at[z], at_z(i)))
    for i in range(N_DP - 1):
        pl.when(i < rank)(functools.partial(ready, d_ready.at[rank], d_peers[i]))
    exchange([(i < x, x_copies[i], None) for i in range(N_X - 1)], True)
    exchange([(i < rank, d_copies[i], None) for i in range(N_DP - 1)], True)

    fetches[11].wait()
    convolve(0)
    convolve(1)
    exchange([(i > x, x_copies[i], x_ready.at[i]) for i in range(1, N_X)], False)
    exchange([(i > rank, d_copies[i], d_ready.at[i]) for i in range(1, N_DP)], False)
    drain((last(0), 60), (last(1), 60))
    for t in range(2):
        send_patch(t)

    drain((first_norm(2), 42))
    for i in range(N_X):
        pl.when(i != x)(x_arrivals[i].wait_recv)
    rowsum[...] = jnp.sum(xcounts[...], axis=0)
    exchange([((i > z) & (i < 4 + N_Z * jnp.minimum(z, 1)), z_copies[i], z_ready.at[i]) for i in range(1, N_Z)], False)
    convolve(2)
    exchange([(z == 0, z_copies[i], z_ready.at[i]) for i in range(4, N_Z)], False)
    drain((last(2), 60))
    for i in range(N_DP):
        pl.when(i != rank)(d_arrivals[i].wait_recv)
    for i in range(N_DP):
        embed_out[:, 144 * i : 144 * i + 144] = shards[i]
    for i in range(N_Z - 1):
        pl.when(i < z)(z_arrivals[i].wait_recv)
    before = jnp.where(iota((N_X, 1, 128), 0) < x, xcounts[...], 0)
    carry_in = jnp.sum(zsums[...], axis=0) + jnp.sum(before, axis=0) - 2 * seat
    for i in range(N_X):
        pl.when(i != x)(x_arrivals[i].wait_send)
    for i in range(N_DP):
        pl.when(i != rank)(d_arrivals[i].wait_send)
    for i in range(1, N_Z):
        pl.when(i > z)(z_arrivals[i].wait_send)
    for t in range(2):
        pl.when(seat < N_Z * N_X - 1)(p_copies[t].wait_send)
    for t in range(2):
        pl.when(seat > 0)(p_copies[t].wait_recv)

    carry_in = jnp.broadcast_to(carry_in, (64, 128))
    number = jnp.full((64, 128), n, I32)
    own = [sent[t].astype(F32) for t in range(3)]
    came = [got[t].astype(F32) for t in range(2)]
    newest = jnp.where(number == 3, own[2], jnp.where(number == 2, own[1], own[0]))
    second = jnp.where(number == 3, own[1], own[0])
    out0 = jnp.where(carry_in == 0, newest, jnp.where(carry_in == 1, came[0], came[1]))
    out1 = jnp.where(carry_in == 0, second, jnp.where(carry_in == 1, newest, came[0]))
    patches = jnp.concatenate([out0, out1], axis=0)
    patches = jnp.where(iota((128, 128), 1) == 64, 1.0, patches).astype(BF16)
    patch_out[...] = patches[:, :80]


def embed_patches(patches, embed, out):
    out[0] = jnp.dot(patches[...], embed[...], preferred_element_type=F32).astype(BF16)


def local(feat, kind, bg, bs, w, bb, fg, fs, lw, lb, ew, eb):
    hbm = pl.BlockSpec(memory_space=pl.ANY)
    vmem = pl.BlockSpec(memory_space=pltpu.VMEM)
    dma, regular, V = pltpu.SemaphoreType.DMA, pltpu.SemaphoreType.REGULAR, pltpu.VMEM
    vec = V((1, C), F32)
    patches, embed = pl.pallas_call(
        kernel,
        out_shape=(jax.ShapeDtypeStruct((128, 80), BF16), jax.ShapeDtypeStruct((80, HID), BF16)),
        in_specs=[hbm] * 12,
        out_specs=(vmem, vmem),
        scratch_shapes=[
            pltpu.SMEM((1, 3), I32), V((768, C), BF16), vec, vec, V((9 * C, C), BF16), vec, vec, vec,
            V((144, C), BF16), V((1, 16), F32), V((64, 144), BF16), V((144,), BF16),
            V((3, 256, C), F32), V((3, 3, 288, C), BF16), V((3, 256, C), F32), V((3, 256, C), BF16),
            V((C, 384), BF16), V((8, 128), F32), V((1, 128), I32), V((1, 128), I32),
            V((N_X, 1, 128), I32), V((N_Z, 1, 128), I32), V((80, 144), BF16), V((N_DP, 80, 144), BF16),
            V((3, 64, 128), BF16), V((2, 64, 128), BF16),
            dma((12,)), dma((N_X,)), dma((N_X,)), dma((N_Z,)), dma((N_Z,)), dma((N_DP,)), dma((N_DP,)),
            dma((2,)), dma((2,)), regular((N_X,)), regular((N_Z,)), regular((N_DP,)),
        ],
        compiler_params=pltpu.CompilerParams(
            collective_id=0, has_side_effects=True, vmem_limit_bytes=60 << 20
        ),
    )(
        kind, feat, bg.reshape(1, C), bs.reshape(1, C), w, bb.reshape(1, C), fg.reshape(1, C),
        fs.reshape(1, C), lw.T, lb.reshape(1, 16), ew, eb,
    )
    return pl.pallas_call(
        embed_patches,
        out_shape=jax.ShapeDtypeStruct((1, 128, HID), BF16),
        in_specs=[vmem, vmem],
        out_specs=vmem,
    )(patches, embed)


def solution(mesh):
    shared = P()
    return jax.shard_map(
        local,
        mesh=mesh,
        in_specs=(P("dp", "seq", None), P("dp", "seq")) + (shared,) * 8 + (P(None, "dp"), P("dp")),
        out_specs=P("dp", "seq", None),
        check_vma=False,
    )
```

```python
import functools
import jax
import jax.numpy as jnp
from jax import lax
from jax.experimental import pallas as pl
from jax.experimental.pallas import tpu as pltpu
from jax.sharding import PartitionSpec as P

F32, BF16, I32 = jnp.float32, jnp.bfloat16, jnp.int32
MESH = pl.DeviceIdType.MESH
LATENT_SHIFT = 0.0609
LATENT_SCALE = 1.5305
EPS = 1e-06
C = 512
HID = 1152
TAPS = [(a, b) for a in (-1, 0, 1) for b in (-1, 0, 1)]
N_DP, N_Z, N_X = 8, 8, 4


def iota(shape, dim):
    return lax.broadcasted_iota(I32, shape, dim)


def drain(*streams):
    live = [[stream, steps, 0] for stream, steps in streams]
    while live:
        entry = min(live, key=lambda e: (e[2] + 1) / e[1])
        entry[2] += 1
        try:
            next(entry[0])
        except StopIteration:
            live.remove(entry)


def group_sums(parts, block):
    rows = jnp.concatenate([p[:, 256 * i : 256 * i + 256] for p in parts for i in range(2)], axis=0)
    hi = rows.astype(BF16)
    rest = rows - hi.astype(F32)
    mid = rest.astype(BF16)
    low = (rest - mid.astype(F32)).astype(BF16)
    sums = jnp.dot(jnp.concatenate([hi, mid, low], axis=0), block, preferred_element_type=F32)
    total = sums[:32] + sums[32:64] + sums[64:]
    out = []
    for i in range(len(parts)):
        tiles = [total[16 * i + 8 * j : 16 * i + 8 * j + 8] for j in range(2)]
        tiles = [jnp.broadcast_to(jnp.sum(t, axis=0, keepdims=True), (8, 256)) for t in tiles]
        out.append(jnp.concatenate(tiles, axis=1))
    return out


def norm_factors(sums, load, block, joined, gain, shift):
    m0, m1 = group_sums(sums, block)
    m0, m1 = m0 * (1.0 / 2048), m1 * (1.0 / 2048)
    both = (m0 + m1) * 0.5
    c0, c1 = jnp.where(joined, both, m0), jnp.where(joined, both, m1)
    low, high = jnp.zeros((8, C), F32), jnp.zeros((8, C), F32)
    for r in range(16):
        x0, x1 = load(r)
        x0, x1 = x0 - c0, x1 - c1
        low, high = low + x0 * x0, high + x1 * x1
        yield
    v0, v1 = group_sums([low, high], block)
    v0, v1 = v0 * (1.0 / 2048), v1 * (1.0 / 2048)
    both = (v0 + v1) * 0.5
    v0, v1 = jnp.where(joined, both, v0), jnp.where(joined, both, v1)
    s0 = lax.rsqrt(v0 + EPS) * gain * 0.5
    s1 = lax.rsqrt(v1 + EPS) * gain * 0.5
    return s0, s1, shift * 0.5 - c0 * s0, shift * 0.5 - c1 * s1


def silu_half(half):
    return half + half * jnp.tanh(half)


def pair(top, bottom):
    return jnp.concatenate([top, bottom], axis=0).astype(BF16)


def loader(ref):
    def load(r):
        return ref[16 * r : 16 * r + 8, :], ref[16 * r + 8 : 16 * r + 16, :]

    return load


def order_slot(pick, slot):
    low, high = jnp.zeros((8, C), F32), jnp.zeros((8, C), F32)
    for i in range(8):
        top, bottom = pick(16 * i).astype(F32), pick(128 + 16 * i).astype(F32)
        for j in range(2):
            x0, x1 = top[8 * j : 8 * j + 8], bottom[8 * j : 8 * j + 8]
            r = 2 * i + j
            slot[16 * r : 16 * r + 8, :], slot[16 * r + 8 : 16 * r + 16, :] = x0, x1
            low, high = low + x0, high + x1
        yield
    return low, high


def norm_first(pick, slot, block, joined, gain, shift, pad):
    sums = yield from order_slot(pick, slot)
    load = loader(slot)
    s0, s1, t0, t1 = yield from norm_factors(sums, load, block, joined, gain, shift)
    zero = jnp.zeros((8, C), F32)
    col = iota((8, C), 0)
    for r in range(16):
        x0, x1 = load(r)
        sides = []
        for y in (silu_half(x0 * s0 + t0), silu_half(x1 * s1 + t1)):
            left = jnp.where(col >= 1, pltpu.roll(y, 1, 0), 0.0)
            right = jnp.where(col <= 6, pltpu.roll(y, 7, 0), 0.0)
            sides.append((left, y, right))
        for b in range(3):
            pad[b, 16 * (r + 1) : 16 * (r + 2), :] = pair(sides[0][b], sides[1][b])
            if r == 0:
                pad[b, 16 * 17 : 16 * 18, :] = pair(jnp.where(joined, sides[1][b], 0.0), zero)
            if r == 15:
                pad[b, 0:16, :] = pair(zero, jnp.where(joined, sides[0][b], 0.0))
        yield


def conv(pad, w, res):
    lhs = jnp.concatenate(
        [pad[b + 1, 16 * (a + 1) : 16 * (a + 1) + 256, :] for a, b in TAPS], axis=1
    )
    res[...] = jnp.dot(lhs, w[...], preferred_element_type=F32)


def finish(slot, res, bias, block, joined, gain, shift, act, lw3, lat_bias, select, out):
    own, added = loader(slot), loader(res)
    low, high = jnp.zeros((8, C), F32), jnp.zeros((8, C), F32)
    for r in range(16):
        (x0, x1), (d0, d1) = own(r), added(r)
        x0, x1 = x0 + d0 + bias, x1 + d1 + bias
        res[16 * r : 16 * r + 8, :], res[16 * r + 8 : 16 * r + 16, :] = x0, x1
        low, high = low + x0, high + x1
        yield
    s0, s1, t0, t1 = yield from norm_factors([low, high], added, block, joined, gain, shift)
    for r in range(16):
        x0, x1 = added(r)
        act[16 * r : 16 * r + 16, :] = pair(silu_half(x0 * s0 + t0), silu_half(x1 * s1 + t1))
        yield
    yield from latent_patches(act, lw3, lat_bias, joined, select, out)


def latent_patches(act, lw3, lat_bias, joined, select, out):
    terms = jnp.dot(act[...], lw3[...], preferred_element_type=F32)
    yield
    joined = joined[:, :128]
    zero = jnp.zeros((8, 128), F32)

    def part(a, r, h):
        return terms[16 * r + 8 * h : 16 * r + 8 * h + 8, 128 * (a + 1) : 128 * (a + 2)]

    col = iota((8, 128), 0)
    lane = iota((8, 128), 1)
    offset = (lat_bias - LATENT_SHIFT) * LATENT_SCALE
    rows = []
    for r in range(16):
        for h in range(2):
            i = r % 2
            above = part(-1, r - 1, h) if r > 0 else (jnp.where(joined, part(-1, 15, 0), 0.0) if h == 1 else zero)
            below = part(1, r + 1, h) if r < 15 else (jnp.where(joined, part(1, 0, 1), 0.0) if h == 0 else zero)
            v = above + part(0, r, h) + below
            left = jnp.where(col >= 1, pltpu.roll(v, 1, 0), 0.0)
            right = jnp.where(col <= 6, pltpu.roll(v, 7, 0), 0.0)
            if i == 0:
                lat = left + pltpu.roll(v, 96, 1) + pltpu.roll(right, 64, 1)
            else:
                lat = pltpu.roll(left, 32, 1) + v + pltpu.roll(right, 96, 1)
            lat = lat * LATENT_SCALE + offset
            rows.append(jnp.where((lane // 16) == (2 * i + col % 2), lat, 0.0))
        if r % 2:
            yield
    cells = jnp.concatenate(rows, axis=0).astype(BF16)
    out[...] = jnp.dot(select, cells, preferred_element_type=F32).astype(BF16)


def tap_columns(lwt, lw3):
    zero = jnp.zeros((16, C), BF16)
    for a in range(3):
        taps = [lwt[16 * (3 * a + b) : 16 * (3 * a + b) + 16, :] for b in range(3)]
        rows = jnp.concatenate([taps[0], taps[0], taps[1], taps[1], taps[2], taps[2], zero, zero], axis=0)
        lw3[:, 128 * a : 128 * a + 128] = rows.T


def masks():
    block = jnp.where(iota((256, 256), 0) // 16 == iota((256, 256), 1) // 16, 1.0, 0.0).astype(BF16)
    t, m = iota((64, 256), 0), iota((64, 256), 1)
    same = (m // 32 == (t // 4) % 8) & ((m // 8) % 2 == t // 32) & ((m % 8) // 2 == t % 4)
    return block, jnp.where(same, 1.0, 0.0).astype(BF16)


DP_ORDER = (0, 1, 2, 6, 3, 7, 4, 5)


def exchange(pairs, start_now):
    for condition, copy, ready in pairs:

        @pl.when(condition)
        def _(copy=copy, ready=ready):
            if not start_now:
                pl.semaphore_wait(ready, 1)
            copy.start()


def kernel(
    kind_hbm, feat_hbm, bg_hbm, bs_hbm, w_hbm, bb_hbm, fg_hbm, fs_hbm, lw_hbm, lb_hbm, ew_hbm, eb_hbm,
    patch_out, embed_out,
    kind, feat, bg, bs, w, bb, fg, fs, lw, lb, ew, eb,
    slots, pad, res, act, lw3, lanes, mine, rowsum, xcounts, zsums, shard, shards, full, sent, got,
    in_sem, x_send, x_recv, z_send, z_recv, d_send, d_recv, p_send, p_recv, x_ready, z_ready, d_ready,
):
    seat, row = lax.axis_index("seq"), lax.axis_index("dp")
    z, x = seat // N_X, lax.rem(seat, N_X)
    rank = sum(jnp.where(row == DP_ORDER[i], i, 0) for i in range(N_DP))

    def at_x(i):
        return {"seq": z * N_X + i}

    def at_z(i):
        return {"seq": i * N_X + x}

    fetches = [
        pltpu.make_async_copy(source, target, in_sem.at[i])
        for i, (source, target) in enumerate(
            [
                (kind_hbm, kind), (lw_hbm, lw), (bg_hbm, bg), (bs_hbm, bs), (bb_hbm, bb), (fg_hbm, fg),
                (fs_hbm, fs), (lb_hbm, lb), (ew_hbm, ew), (eb_hbm, eb), (feat_hbm.at[0], feat), (w_hbm, w),
            ]
        )
    ]
    for fetch in fetches:
        fetch.start()
    zsums[...] = jnp.zeros((N_Z, 1, 128), I32)
    got[...] = jnp.zeros((2, 64, 128), BF16)
    lanes[...] = jnp.zeros((8, 128), F32)

    barrier = pltpu.get_barrier_semaphore()

    def greet(target):
        pl.semaphore_signal(barrier, inc=1, device_id=target, device_id_type=MESH)

    for i in range(1, N_DP):
        pl.when(i > rank)(functools.partial(greet, {"dp": DP_ORDER[i]}))
    for i in range(1, N_X):
        pl.when(i > x)(functools.partial(greet, at_x(i)))
    pl.when((x == 0) & (z > 0))(functools.partial(greet, {"seq": seat - 1}))
    for i in range(1, N_Z):
        pl.when(i > z)(functools.partial(greet, at_z(i)))

    block, select = masks()
    for fetch in fetches[:10]:
        fetch.wait()
    live = [(kind[0, i] > 0).astype(I32) for i in range(3)]
    n = live[0] + live[1] + live[2]
    kinds = [
        jnp.where(n == 3, kind[0, 2], jnp.where(n == 2, kind[0, 1], kind[0, 0])),
        jnp.where(n == 2, kind[0, 0], kind[0, 1]),
        jnp.where(n == 3, kind[0, 0], kind[0, 2]),
    ]
    joined = [jnp.full((8, C), kinds[t], I32) == 2 for t in range(3)]
    mine[...] = jnp.full((1, 128), n, I32)
    xcounts[pl.ds(x, 1)] = jnp.full((1, 1, 128), n, I32)
    shard[0:64, :] = ew[...]
    bias_row = jnp.broadcast_to(eb[...].reshape(1, 144).astype(F32), (16, 144))
    shard[64:80, :] = jnp.where(iota((16, 144), 0) == 0, bias_row, 0.0).astype(BF16)
    shards[pl.ds(row, 1)] = shard[...].reshape(1, 80, 144)
    lanes[0:1, 0:16] = lb[...]
    lat_bias = lanes[...]
    for step in (16, 32, 64):
        lat_bias = lat_bias + pltpu.roll(lat_bias, step, 1)
    lat_bias = lat_bias[0:1]

    number = jnp.full((16, C), n, I32)

    def cells(k, i):
        return feat[256 * k + i : 256 * k + i + 16, :]

    def pick(t):
        def rows(i):
            if t == 0:
                return jnp.where(number == 3, cells(2, i), jnp.where(number == 2, cells(1, i), cells(0, i)))
            if t == 1:
                return jnp.where(number == 2, cells(0, i), cells(1, i))
            return jnp.where(number == 3, cells(0, i), cells(2, i))

        return rows

    def spread(vector):
        return jnp.broadcast_to(vector[...], (8, C))

    def first_norm(t):
        return norm_first(pick(t), slots.at[t], block, joined[t], spread(bg), spread(bs), pad.at[t])

    def convolve(t):
        conv(pad.at[t], w, res.at[t])

    def last(t):
        return finish(
            slots.at[t], res.at[t], spread(bb), block, joined[t], spread(fg), spread(fs), act.at[t],
            lw3, lat_bias, select, sent.at[t],
        )

    def copy_to(source, target, send_sem, recv_sem, device):
        return pltpu.make_async_remote_copy(
            src_ref=source, dst_ref=target, send_sem=send_sem, recv_sem=recv_sem,
            device_id=device, device_id_type=MESH,
        )

    x_copies = [copy_to(mine, xcounts.at[x], x_send.at[i], x_recv.at[x], at_x(i)) for i in range(N_X)]
    x_arrivals = [copy_to(mine, xcounts.at[i], x_send.at[i], x_recv.at[i], at_x(i)) for i in range(N_X)]
    z_copies = [copy_to(rowsum, zsums.at[z], z_send.at[i], z_recv.at[z], at_z(i)) for i in range(N_Z)]
    z_arrivals = [copy_to(rowsum, zsums.at[i], z_send.at[i], z_recv.at[i], at_z(i)) for i in range(N_Z)]
    d_peers = [{"dp": DP_ORDER[i]} for i in range(N_DP)]
    d_copies = [copy_to(shard, shards.at[row], d_send.at[i], d_recv.at[rank], d_peers[i]) for i in range(N_DP)]
    d_arrivals = [
        copy_to(shard, shards.at[DP_ORDER[i]], d_send.at[i], d_recv.at[i], d_peers[i]) for i in range(N_DP)
    ]
    p_copies = [
        copy_to(sent.at[t], got.at[t], p_send.at[t], p_recv.at[t], {"seq": lax.rem(seat + 1, N_Z * N_X)})
        for t in range(2)
    ]

    def send_patch(t):
        pl.when(seat < N_Z * N_X - 1)(p_copies[t].start)

    tap_columns(lw, lw3)
    fetches[10].wait()
    drain((first_norm(0), 42), (first_norm(1), 42))
    earlier = x + z + rank + ((x == N_X - 1) & (z < N_Z - 1)).astype(I32)

    @pl.when(earlier > 0)
    def _():
        pl.semaphore_wait(barrier, earlier)


    def ready(sem, target):
        pl.semaphore_signal(sem, inc=1, device_id=target, device_id_type=MESH)

    for i in range(N_X - 1):
        pl.when(i < x)(functools.partial(ready, x_ready.at[x], at_x(i)))
    for i in range(N_Z - 1):
        pl.when(i < z)(functools.partial(ready, z_ready.at[z], at_z(i)))
    for i in range(N_DP - 1):
        pl.when(i < rank)(functools.partial(ready, d_ready.at[rank], d_peers[i]))
    exchange([(i < x, x_copies[i], None) for i in range(N_X - 1)], True)
    exchange([(i < rank, d_copies[i], None) for i in range(N_DP - 1)], True)

    fetches[11].wait()
    convolve(0)
    convolve(1)
    exchange([(i > x, x_copies[i], x_ready.at[i]) for i in range(1, N_X)], False)
    exchange([(i > rank, d_copies[i], d_ready.at[i]) for i in range(1, N_DP)], False)
    drain((last(0), 60), (last(1), 60))
    for t in range(2):
        send_patch(t)

    drain((first_norm(2), 42))
    for i in range(N_X):
        pl.when(i != x)(x_arrivals[i].wait_recv)
    rowsum[...] = jnp.sum(xcounts[...], axis=0)
    exchange([((i > z) & (i < 4 + N_Z * jnp.minimum(z, 1)), z_copies[i], z_ready.at[i]) for i in range(1, N_Z)], False)
    convolve(2)
    exchange([(z == 0, z_copies[i], z_ready.at[i]) for i in range(4, N_Z)], False)
    drain((last(2), 60))
    for i in range(N_DP):
        pl.when(i != rank)(d_arrivals[i].wait_recv)
    for i in range(N_DP):
        full[:, 144 * i : 144 * i + 144] = shards[i]
    embed_copy = pltpu.make_async_copy(full, embed_out, in_sem.at[0])
    embed_copy.start()
    for i in range(N_Z - 1):
        pl.when(i < z)(z_arrivals[i].wait_recv)
    before = jnp.where(iota((N_X, 1, 128), 0) < x, xcounts[...], 0)
    carry_in = jnp.sum(zsums[...], axis=0) + jnp.sum(before, axis=0) - 2 * seat
    for i in range(N_X):
        pl.when(i != x)(x_arrivals[i].wait_send)
    for i in range(N_DP):
        pl.when(i != rank)(d_arrivals[i].wait_send)
    for i in range(1, N_Z):
        pl.when(i > z)(z_arrivals[i].wait_send)
    for t in range(2):
        pl.when(seat < N_Z * N_X - 1)(p_copies[t].wait_send)
    for t in range(2):
        pl.when(seat > 0)(p_copies[t].wait_recv)

    carry_in = jnp.broadcast_to(carry_in, (64, 128))
    number = jnp.full((64, 128), n, I32)
    own = [sent[t].astype(F32) for t in range(3)]
    came = [got[t].astype(F32) for t in range(2)]
    newest = jnp.where(number == 3, own[2], jnp.where(number == 2, own[1], own[0]))
    second = jnp.where(number == 3, own[1], own[0])
    out0 = jnp.where(carry_in == 0, newest, jnp.where(carry_in == 1, came[0], came[1]))
    out1 = jnp.where(carry_in == 0, second, jnp.where(carry_in == 1, newest, came[0]))
    patches = jnp.concatenate([out0, out1], axis=0)
    patches = jnp.where(iota((128, 128), 1) == 64, 1.0, patches).astype(BF16)
    patch_out[...] = patches[:, :80]
    embed_copy.wait()


def embed_patches(patches, embed, out):
    out[0] = jnp.dot(patches[...], embed[...], preferred_element_type=F32).astype(BF16)


def local(feat, kind, bg, bs, w, bb, fg, fs, lw, lb, ew, eb):
    hbm = pl.BlockSpec(memory_space=pl.ANY)
    vmem = pl.BlockSpec(memory_space=pltpu.VMEM)
    dma, regular, V = pltpu.SemaphoreType.DMA, pltpu.SemaphoreType.REGULAR, pltpu.VMEM
    vec = V((1, C), F32)
    patches, embed = pl.pallas_call(
        kernel,
        out_shape=(jax.ShapeDtypeStruct((128, 80), BF16), jax.ShapeDtypeStruct((80, HID), BF16)),
        in_specs=[hbm] * 12,
        out_specs=(vmem, hbm),
        scratch_shapes=[
            pltpu.SMEM((1, 3), I32), V((768, C), BF16), vec, vec, V((9 * C, C), BF16), vec, vec, vec,
            V((144, C), BF16), V((1, 16), F32), V((64, 144), BF16), V((144,), BF16),
            V((3, 256, C), F32), V((3, 3, 288, C), BF16), V((3, 256, C), F32), V((3, 256, C), BF16),
            V((C, 384), BF16), V((8, 128), F32), V((1, 128), I32), V((1, 128), I32),
            V((N_X, 1, 128), I32), V((N_Z, 1, 128), I32), V((80, 144), BF16), V((N_DP, 80, 144), BF16), V((80, HID), BF16),
            V((3, 64, 128), BF16), V((2, 64, 128), BF16),
            dma((12,)), dma((N_X,)), dma((N_X,)), dma((N_Z,)), dma((N_Z,)), dma((N_DP,)), dma((N_DP,)),
            dma((2,)), dma((2,)), regular((N_X,)), regular((N_Z,)), regular((N_DP,)),
        ],
        compiler_params=pltpu.CompilerParams(
            collective_id=0, has_side_effects=True, vmem_limit_bytes=60 << 20,
        ),
    )(
        kind, feat, bg.reshape(1, C), bs.reshape(1, C), w, bb.reshape(1, C), fg.reshape(1, C),
        fs.reshape(1, C), lw.T, lb.reshape(1, 16), ew, eb,
    )
    return pl.pallas_call(
        embed_patches,
        out_shape=jax.ShapeDtypeStruct((1, 128, HID), BF16),
        in_specs=[vmem, vmem],
        out_specs=vmem,
    )(patches, embed)


def solution(mesh):
    shared = P()
    return jax.shard_map(
        local,
        mesh=mesh,
        in_specs=(P("dp", "seq", None), P("dp", "seq")) + (shared,) * 8 + (P(None, "dp"), P("dp")),
        out_specs=P("dp", "seq", None),
        check_vma=False,
    )
```

```python
import functools
import jax
import jax.numpy as jnp
from jax import lax
from jax.experimental import pallas as pl
from jax.experimental.pallas import tpu as pltpu
from jax.sharding import PartitionSpec as P

F32, BF16, I32 = jnp.float32, jnp.bfloat16, jnp.int32
MESH = pl.DeviceIdType.MESH
LATENT_SHIFT = 0.0609
LATENT_SCALE = 1.5305
EPS = 1e-06
C = 512
HID = 1152
TAPS = [(a, b) for a in (-1, 0, 1) for b in (-1, 0, 1)]
N_DP, N_Z, N_X = 8, 8, 4


def iota(shape, dim):
    return lax.broadcasted_iota(I32, shape, dim)


def drain(*streams):
    live = [[stream, steps, 0] for stream, steps in streams]
    while live:
        entry = min(live, key=lambda e: (e[2] + 1) / e[1])
        entry[2] += 1
        try:
            next(entry[0])
        except StopIteration:
            live.remove(entry)


def group_sums(parts, block):
    rows = jnp.concatenate([p[:, 256 * i : 256 * i + 256] for p in parts for i in range(2)], axis=0)
    hi = rows.astype(BF16)
    rest = rows - hi.astype(F32)
    mid = rest.astype(BF16)
    low = (rest - mid.astype(F32)).astype(BF16)
    sums = jnp.dot(jnp.concatenate([hi, mid, low], axis=0), block, preferred_element_type=F32)
    total = sums[:32] + sums[32:64] + sums[64:]
    out = []
    for i in range(len(parts)):
        tiles = [total[16 * i + 8 * j : 16 * i + 8 * j + 8] for j in range(2)]
        tiles = [jnp.broadcast_to(jnp.sum(t, axis=0, keepdims=True), (8, 256)) for t in tiles]
        out.append(jnp.concatenate(tiles, axis=1))
    return out


def norm_factors(sums, load, block, joined, gain, shift):
    m0, m1 = group_sums(sums, block)
    m0, m1 = m0 * (1.0 / 2048), m1 * (1.0 / 2048)
    both = (m0 + m1) * 0.5
    c0, c1 = jnp.where(joined, both, m0), jnp.where(joined, both, m1)
    low, high = jnp.zeros((8, C), F32), jnp.zeros((8, C), F32)
    for r in range(16):
        x0, x1 = load(r)
        x0, x1 = x0 - c0, x1 - c1
        low, high = low + x0 * x0, high + x1 * x1
        yield
    v0, v1 = group_sums([low, high], block)
    v0, v1 = v0 * (1.0 / 2048), v1 * (1.0 / 2048)
    both = (v0 + v1) * 0.5
    v0, v1 = jnp.where(joined, both, v0), jnp.where(joined, both, v1)
    s0 = lax.rsqrt(v0 + EPS) * gain * 0.5
    s1 = lax.rsqrt(v1 + EPS) * gain * 0.5
    return s0, s1, shift * 0.5 - c0 * s0, shift * 0.5 - c1 * s1


def silu_half(half):
    return half + half * jnp.tanh(half)


def pair(top, bottom):
    return jnp.concatenate([top, bottom], axis=0).astype(BF16)


def loader(ref):
    def load(r):
        return ref[16 * r : 16 * r + 8, :], ref[16 * r + 8 : 16 * r + 16, :]

    return load


def order_slot(pick, slot):
    low, high = jnp.zeros((8, C), F32), jnp.zeros((8, C), F32)
    for i in range(8):
        top, bottom = pick(16 * i).astype(F32), pick(128 + 16 * i).astype(F32)
        for j in range(2):
            x0, x1 = top[8 * j : 8 * j + 8], bottom[8 * j : 8 * j + 8]
            r = 2 * i + j
            slot[16 * r : 16 * r + 8, :], slot[16 * r + 8 : 16 * r + 16, :] = x0, x1
            low, high = low + x0, high + x1
        yield
    return low, high


def norm_first(pick, slot, block, joined, gain, shift, pad):
    sums = yield from order_slot(pick, slot)
    load = loader(slot)
    s0, s1, t0, t1 = yield from norm_factors(sums, load, block, joined, gain, shift)
    zero = jnp.zeros((8, C), F32)
    col = iota((8, C), 0)
    for r in range(16):
        x0, x1 = load(r)
        sides = []
        for y in (silu_half(x0 * s0 + t0), silu_half(x1 * s1 + t1)):
            left = jnp.where(col >= 1, pltpu.roll(y, 1, 0), 0.0)
            right = jnp.where(col <= 6, pltpu.roll(y, 7, 0), 0.0)
            sides.append((left, y, right))
        for b in range(3):
            pad[b, 16 * (r + 1) : 16 * (r + 2), :] = pair(sides[0][b], sides[1][b])
            if r == 0:
                pad[b, 16 * 17 : 16 * 18, :] = pair(jnp.where(joined, sides[1][b], 0.0), zero)
            if r == 15:
                pad[b, 0:16, :] = pair(zero, jnp.where(joined, sides[0][b], 0.0))
        yield


def conv(pad, w, res):
    lhs = jnp.concatenate(
        [pad[b + 1, 16 * (a + 1) : 16 * (a + 1) + 256, :] for a, b in TAPS], axis=1
    )
    res[...] = jnp.dot(lhs, w[...], preferred_element_type=F32)


def finish(slot, res, bias, block, joined, gain, shift, act, lw3, lat_bias, select, out):
    own, added = loader(slot), loader(res)
    low, high = jnp.zeros((8, C), F32), jnp.zeros((8, C), F32)
    for r in range(16):
        (x0, x1), (d0, d1) = own(r), added(r)
        x0, x1 = x0 + d0 + bias, x1 + d1 + bias
        res[16 * r : 16 * r + 8, :], res[16 * r + 8 : 16 * r + 16, :] = x0, x1
        low, high = low + x0, high + x1
        yield
    s0, s1, t0, t1 = yield from norm_factors([low, high], added, block, joined, gain, shift)
    for r in range(16):
        x0, x1 = added(r)
        act[16 * r : 16 * r + 16, :] = pair(silu_half(x0 * s0 + t0), silu_half(x1 * s1 + t1))
        yield
    yield from latent_patches(act, lw3, lat_bias, joined, select, out)


def latent_patches(act, lw3, lat_bias, joined, select, out):
    terms = jnp.dot(act[...], lw3[...], preferred_element_type=F32)
    yield
    joined = joined[:, :128]
    zero = jnp.zeros((8, 128), F32)

    def part(a, r, h):
        return terms[16 * r + 8 * h : 16 * r + 8 * h + 8, 128 * (a + 1) : 128 * (a + 2)]

    col = iota((8, 128), 0)
    lane = iota((8, 128), 1)
    offset = (lat_bias - LATENT_SHIFT) * LATENT_SCALE
    rows = []
    for r in range(16):
        for h in range(2):
            i = r % 2
            above = part(-1, r - 1, h) if r > 0 else (jnp.where(joined, part(-1, 15, 0), 0.0) if h == 1 else zero)
            below = part(1, r + 1, h) if r < 15 else (jnp.where(joined, part(1, 0, 1), 0.0) if h == 0 else zero)
            v = above + part(0, r, h) + below
            left = jnp.where(col >= 1, pltpu.roll(v, 1, 0), 0.0)
            right = jnp.where(col <= 6, pltpu.roll(v, 7, 0), 0.0)
            if i == 0:
                lat = left + pltpu.roll(v, 96, 1) + pltpu.roll(right, 64, 1)
            else:
                lat = pltpu.roll(left, 32, 1) + v + pltpu.roll(right, 96, 1)
            lat = lat * LATENT_SCALE + offset
            rows.append(jnp.where((lane // 16) == (2 * i + col % 2), lat, 0.0))
        if r % 2:
            yield
    cells = jnp.concatenate(rows, axis=0).astype(BF16)
    out[...] = jnp.dot(select, cells, preferred_element_type=F32).astype(BF16)


def tap_columns(lwt, lw3):
    zero = jnp.zeros((16, C), BF16)
    for a in range(3):
        taps = [lwt[16 * (3 * a + b) : 16 * (3 * a + b) + 16, :] for b in range(3)]
        rows = jnp.concatenate([taps[0], taps[0], taps[1], taps[1], taps[2], taps[2], zero, zero], axis=0)
        lw3[:, 128 * a : 128 * a + 128] = rows.T


def masks():
    block = jnp.where(iota((256, 256), 0) // 16 == iota((256, 256), 1) // 16, 1.0, 0.0).astype(BF16)
    t, m = iota((64, 256), 0), iota((64, 256), 1)
    same = (m // 32 == (t // 4) % 8) & ((m // 8) % 2 == t // 32) & ((m % 8) // 2 == t % 4)
    return block, jnp.where(same, 1.0, 0.0).astype(BF16)


DP_ORDER = (0, 1, 2, 6, 3, 7, 4, 5)


def exchange(pairs, start_now):
    for condition, copy, ready in pairs:

        @pl.when(condition)
        def _(copy=copy, ready=ready):
            if not start_now:
                pl.semaphore_wait(ready, 1)
            copy.start()


def kernel(
    kind_hbm, feat_hbm, bg_hbm, bs_hbm, w_hbm, bb_hbm, fg_hbm, fs_hbm, lw_hbm, lb_hbm, ew_hbm, eb_hbm,
    patch_out, embed_out,
    kind, feat, bg, bs, w, bb, fg, fs, lw, lb, ew, eb,
    slots, pad, res, act, lw3, lanes, mine, rowsum, xcounts, zsums, shard, shards, sent, got,
    in_sem, x_send, x_recv, z_send, z_recv, d_send, d_recv, p_send, p_recv, x_ready, z_ready, d_ready,
):
    seat, row = lax.axis_index("seq"), lax.axis_index("dp")
    z, x = seat // N_X, lax.rem(seat, N_X)
    rank = sum(jnp.where(row == DP_ORDER[i], i, 0) for i in range(N_DP))

    def at_x(i):
        return {"seq": z * N_X + i}

    def at_z(i):
        return {"seq": i * N_X + x}

    fetches = [
        pltpu.make_async_copy(source, target, in_sem.at[i])
        for i, (source, target) in enumerate(
            [
                (kind_hbm, kind), (lw_hbm, lw), (bg_hbm, bg), (bs_hbm, bs), (bb_hbm, bb), (fg_hbm, fg),
                (fs_hbm, fs), (lb_hbm, lb), (ew_hbm, ew), (eb_hbm, eb), (feat_hbm.at[0], feat), (w_hbm, w),
            ]
        )
    ]
    for fetch in fetches:
        fetch.start()
    zsums[...] = jnp.zeros((N_Z, 1, 128), I32)
    got[...] = jnp.zeros((2, 64, 128), BF16)
    lanes[...] = jnp.zeros((8, 128), F32)

    barrier = pltpu.get_barrier_semaphore()

    def greet(target):
        pl.semaphore_signal(barrier, inc=1, device_id=target, device_id_type=MESH)

    for i in range(1, N_DP):
        pl.when(i > rank)(functools.partial(greet, {"dp": DP_ORDER[i]}))
    for i in range(1, N_X):
        pl.when(i > x)(functools.partial(greet, at_x(i)))
    pl.when((x == 0) & (z > 0))(functools.partial(greet, {"seq": seat - 1}))
    for i in range(1, N_Z):
        pl.when(i > z)(functools.partial(greet, at_z(i)))

    block, select = masks()
    for fetch in fetches[:10]:
        fetch.wait()
    live = [(kind[0, i] > 0).astype(I32) for i in range(3)]
    n = live[0] + live[1] + live[2]
    kinds = [
        jnp.where(n == 3, kind[0, 2], jnp.where(n == 2, kind[0, 1], kind[0, 0])),
        jnp.where(n == 2, kind[0, 0], kind[0, 1]),
        jnp.where(n == 3, kind[0, 0], kind[0, 2]),
    ]
    joined = [jnp.full((8, C), kinds[t], I32) == 2 for t in range(3)]
    mine[...] = jnp.full((1, 128), n, I32)
    xcounts[pl.ds(x, 1)] = jnp.full((1, 1, 128), n, I32)
    shard[0:64, :] = ew[...]
    bias_row = jnp.broadcast_to(eb[...].reshape(1, 144).astype(F32), (16, 144))
    shard[64:80, :] = jnp.where(iota((16, 144), 0) == 0, bias_row, 0.0).astype(BF16)
    shards[pl.ds(row, 1)] = shard[...].reshape(1, 80, 144)
    lanes[0:1, 0:16] = lb[...]
    lat_bias = lanes[...]
    for step in (16, 32, 64):
        lat_bias = lat_bias + pltpu.roll(lat_bias, step, 1)
    lat_bias = lat_bias[0:1]

    number = jnp.full((16, C), n, I32)

    def cells(k, i):
        return feat[256 * k + i : 256 * k + i + 16, :]

    def pick(t):
        def rows(i):
            if t == 0:
                return jnp.where(number == 3, cells(2, i), jnp.where(number == 2, cells(1, i), cells(0, i)))
            if t == 1:
                return jnp.where(number == 2, cells(0, i), cells(1, i))
            return jnp.where(number == 3, cells(0, i), cells(2, i))

        return rows

    def spread(vector):
        return jnp.broadcast_to(vector[...], (8, C))

    def first_norm(t):
        return norm_first(pick(t), slots.at[t], block, joined[t], spread(bg), spread(bs), pad.at[t])

    def convolve(t):
        conv(pad.at[t], w, res.at[t])

    def last(t):
        return finish(
            slots.at[t], res.at[t], spread(bb), block, joined[t], spread(fg), spread(fs), act.at[t],
            lw3, lat_bias, select, sent.at[t],
        )

    def copy_to(source, target, send_sem, recv_sem, device):
        return pltpu.make_async_remote_copy(
            src_ref=source, dst_ref=target, send_sem=send_sem, recv_sem=recv_sem,
            device_id=device, device_id_type=MESH,
        )

    x_copies = [copy_to(mine, xcounts.at[x], x_send.at[i], x_recv.at[x], at_x(i)) for i in range(N_X)]
    x_arrivals = [copy_to(mine, xcounts.at[i], x_send.at[i], x_recv.at[i], at_x(i)) for i in range(N_X)]
    z_copies = [copy_to(rowsum, zsums.at[z], z_send.at[i], z_recv.at[z], at_z(i)) for i in range(N_Z)]
    z_arrivals = [copy_to(rowsum, zsums.at[i], z_send.at[i], z_recv.at[i], at_z(i)) for i in range(N_Z)]
    d_peers = [{"dp": DP_ORDER[i]} for i in range(N_DP)]
    d_copies = [copy_to(shard, shards.at[row], d_send.at[i], d_recv.at[rank], d_peers[i]) for i in range(N_DP)]
    d_arrivals = [
        copy_to(shard, shards.at[DP_ORDER[i]], d_send.at[i], d_recv.at[i], d_peers[i]) for i in range(N_DP)
    ]
    p_copies = [
        copy_to(sent.at[t], got.at[t], p_send.at[t], p_recv.at[t], {"seq": lax.rem(seat + 1, N_Z * N_X)})
        for t in range(2)
    ]

    def send_patch(t):
        pl.when(seat < N_Z * N_X - 1)(p_copies[t].start)

    tap_columns(lw, lw3)
    fetches[10].wait()
    drain((first_norm(0), 42), (first_norm(1), 42))
    earlier = x + z + rank + ((x == N_X - 1) & (z < N_Z - 1)).astype(I32)

    @pl.when(earlier > 0)
    def _():
        pl.semaphore_wait(barrier, earlier)


    def ready(sem, target):
        pl.semaphore_signal(sem, inc=1, device_id=target, device_id_type=MESH)

    for i in range(N_X - 1):
        pl.when(i < x)(functools.partial(ready, x_ready.at[x], at_x(i)))
    for i in range(N_Z - 1):
        pl.when(i < z)(functools.partial(ready, z_ready.at[z], at_z(i)))
    for i in range(N_DP - 1):
        pl.when(i < rank)(functools.partial(ready, d_ready.at[rank], d_peers[i]))
    exchange([(i < x, x_copies[i], None) for i in range(N_X - 1)], True)
    exchange([(i < rank, d_copies[i], None) for i in range(N_DP - 1)], True)

    fetches[11].wait()
    convolve(0)
    convolve(1)
    exchange([(i > x, x_copies[i], x_ready.at[i]) for i in range(1, N_X)], False)
    drain((last(0), 60), (last(1), 60))
    for t in range(2):
        send_patch(t)
    exchange([(i > rank, d_copies[i], d_ready.at[i]) for i in range(1, N_DP)], False)

    drain((first_norm(2), 42))
    for i in range(N_X):
        pl.when(i != x)(x_arrivals[i].wait_recv)
    rowsum[...] = jnp.sum(xcounts[...], axis=0)
    exchange([((i > z) & (i < 4 + N_Z * jnp.minimum(z, 1)), z_copies[i], z_ready.at[i]) for i in range(1, N_Z)], False)
    convolve(2)
    exchange([(z == 0, z_copies[i], z_ready.at[i]) for i in range(4, N_Z)], False)
    drain((last(2), 60))
    for i in range(N_DP):
        pl.when(i != rank)(d_arrivals[i].wait_recv)
    for i in range(N_DP):
        embed_out[:, 144 * i : 144 * i + 144] = shards[i]
    for i in range(N_Z - 1):
        pl.when(i < z)(z_arrivals[i].wait_recv)
    before = jnp.where(iota((N_X, 1, 128), 0) < x, xcounts[...], 0)
    carry_in = jnp.sum(zsums[...], axis=0) + jnp.sum(before, axis=0) - 2 * seat
    for i in range(N_X):
        pl.when(i != x)(x_arrivals[i].wait_send)
    for i in range(N_DP):
        pl.when(i != rank)(d_arrivals[i].wait_send)
    for i in range(1, N_Z):
        pl.when(i > z)(z_arrivals[i].wait_send)
    for t in range(2):
        pl.when(seat < N_Z * N_X - 1)(p_copies[t].wait_send)
    for t in range(2):
        pl.when(seat > 0)(p_copies[t].wait_recv)

    carry_in = jnp.broadcast_to(carry_in, (64, 128))
    number = jnp.full((64, 128), n, I32)
    own = [sent[t].astype(F32) for t in range(3)]
    came = [got[t].astype(F32) for t in range(2)]
    newest = jnp.where(number == 3, own[2], jnp.where(number == 2, own[1], own[0]))
    second = jnp.where(number == 3, own[1], own[0])
    out0 = jnp.where(carry_in == 0, newest, jnp.where(carry_in == 1, came[0], came[1]))
    out1 = jnp.where(carry_in == 0, second, jnp.where(carry_in == 1, newest, came[0]))
    patches = jnp.concatenate([out0, out1], axis=0)
    patches = jnp.where(iota((128, 128), 1) == 64, 1.0, patches).astype(BF16)
    patch_out[...] = patches[:, :80]


def embed_patches(patches, embed, out):
    out[0] = jnp.dot(patches[...], embed[...], preferred_element_type=F32).astype(BF16)


def local(feat, kind, bg, bs, w, bb, fg, fs, lw, lb, ew, eb):
    hbm = pl.BlockSpec(memory_space=pl.ANY)
    vmem = pl.BlockSpec(memory_space=pltpu.VMEM)
    dma, regular, V = pltpu.SemaphoreType.DMA, pltpu.SemaphoreType.REGULAR, pltpu.VMEM
    vec = V((1, C), F32)
    patches, embed = pl.pallas_call(
        kernel,
        out_shape=(jax.ShapeDtypeStruct((128, 80), BF16), jax.ShapeDtypeStruct((80, HID), BF16)),
        in_specs=[hbm] * 12,
        out_specs=(vmem, vmem),
        scratch_shapes=[
            pltpu.SMEM((1, 3), I32), V((768, C), BF16), vec, vec, V((9 * C, C), BF16), vec, vec, vec,
            V((144, C), BF16), V((1, 16), F32), V((64, 144), BF16), V((144,), BF16),
            V((3, 256, C), F32), V((3, 3, 288, C), BF16), V((3, 256, C), F32), V((3, 256, C), BF16),
            V((C, 384), BF16), V((8, 128), F32), V((1, 128), I32), V((1, 128), I32),
            V((N_X, 1, 128), I32), V((N_Z, 1, 128), I32), V((80, 144), BF16), V((N_DP, 80, 144), BF16),
            V((3, 64, 128), BF16), V((2, 64, 128), BF16),
            dma((12,)), dma((N_X,)), dma((N_X,)), dma((N_Z,)), dma((N_Z,)), dma((N_DP,)), dma((N_DP,)),
            dma((2,)), dma((2,)), regular((N_X,)), regular((N_Z,)), regular((N_DP,)),
        ],
        compiler_params=pltpu.CompilerParams(
            collective_id=0, has_side_effects=True, vmem_limit_bytes=60 << 20
        ),
    )(
        kind, feat, bg.reshape(1, C), bs.reshape(1, C), w, bb.reshape(1, C), fg.reshape(1, C),
        fs.reshape(1, C), lw.T, lb.reshape(1, 16), ew, eb,
    )
    return pl.pallas_call(
        embed_patches,
        out_shape=jax.ShapeDtypeStruct((1, 128, HID), BF16),
        in_specs=[vmem, vmem],
        out_specs=vmem,
    )(patches, embed)


def solution(mesh):
    shared = P()
    return jax.shard_map(
        local,
        mesh=mesh,
        in_specs=(P("dp", "seq", None), P("dp", "seq")) + (shared,) * 8 + (P(None, "dp"), P("dp")),
        out_specs=P("dp", "seq", None),
        check_vma=False,
    )
```
